128 devices in a mesh: patch: 8 (over x, core), proto: 16 (over z, y).
Axes of the slice: x: 4, y: 4, z: 4, core: 2. Of those that a mesh axis runs over, the one named last changes fastest.
Arguments:
- student_feats: bfloat16 [32768, 256], P(('patch', 'proto')), may hold values from -50 to 50
- teacher_feats: bfloat16 [32768, 256], P(('patch', 'proto')), may hold values from -50 to 50
- proto_weight: bfloat16 [256, 131072], P(None, 'proto'), may hold values from -4 to 4
- mask_index: int32 [4096], P(('patch', 'proto')), may hold values from 0 to 255, as said below
- row_weight: bfloat16 [4096], P(('patch', 'proto')), may hold values from 0.5 to 4
Outputs:
- grad_student: float32 [4096, 256], P(('patch', 'proto'))
- grad_proto: float32 [256, 131072], P('patch', 'proto')
- loss: float32 [], replicated
The draws below stay inside these ranges and needn't reach their ends.
Inputs may be any that keep to these rules, and one draw needn't show every extreme that they name: `mask_index`: entries k * 32 to (k + 1) * 32 - 1 are distinct patch positions of image k, counted from that image's first patch.
All inputs are finite; a program needn't handle non-finite values.
Results may differ from the reference program's by a relative error of at most 0.0057.
Values may be sent and summed in bfloat16 or wider, within the bound.
No kernel may reach another device: no remote copies, remote signals or barrier semaphores. Data moves between devices by JAX's collectives and lax.ppermute only.
A program may use at most 128 MiB of HBM per device.

```python
import math
import jax
import jax.numpy as jnp
from jax import lax

D = 256
P_SIZE = 131072
PATCH_DEV = 256
MASK_DEV = 32
SK_ITERS = 3
PATCHES = 32768
MASKED = 4096


regions = 16


def base_normal(key):
    return jnp.clip(jax.random.normal(jax.random.fold_in(key, 11), (D, P_SIZE), jnp.float32), -5.0, 5.0)


def anchor_table(key):
    return jnp.clip(jax.random.normal(jax.random.fold_in(key, 13), (D, regions), jnp.float32), -5.0, 5.0)


def proto_region(key):
    first = jax.random.randint(jax.random.fold_in(key, 14), (P_SIZE,), 0, regions)
    second = jax.random.randint(jax.random.fold_in(key, 15), (P_SIZE,), 0, regions)
    return jnp.minimum(first, second).astype(jnp.int32)


def row_region(key):
    return jax.random.randint(jax.random.fold_in(key, 21), (PATCHES,), 0, regions).astype(jnp.int32)


def draw_proto_weight(key, part):
    base = base_normal(key)
    anchors = anchor_table(key)
    pulled = base + jnp.take(anchors, proto_region(key), axis=1)
    spread = 0.7
    scale = jnp.exp(jax.random.uniform(jax.random.fold_in(key, 12), (P_SIZE,), jnp.float32, -spread, spread))
    values = jnp.clip(pulled * scale[None, :] / math.sqrt(D), -4.0, 4.0)
    return values.astype(jnp.bfloat16)


def feature_rows(key, salt, amp_low, amp_high, ramp_low, ramp_high):
    anchors = anchor_table(key)
    centers = jnp.take(anchors, row_region(key), axis=1).T / math.sqrt(D)
    amplitude = jax.random.uniform(jax.random.fold_in(key, salt), (PATCHES, 1), jnp.float32, amp_low, amp_high)
    along = jnp.arange(PATCHES, dtype=jnp.float32)[:, None] / float(PATCHES - 1)
    amplitude = amplitude * (ramp_low + (ramp_high - ramp_low) * along)
    noise = jnp.clip(jax.random.normal(jax.random.fold_in(key, salt + 1), (PATCHES, D), jnp.float32), -5.0, 5.0)
    row_scale = jnp.exp(jax.random.uniform(jax.random.fold_in(key, salt + 2), (PATCHES, 1), jnp.float32, 0.0, math.log(10.0)))
    rows = (amplitude * centers + noise / math.sqrt(D)) * row_scale
    return jnp.clip(rows, -50.0, 50.0)


def draw_student_feats(key, part):
    rows = feature_rows(key, 31, 0.5, 2.0, 1.0, 6.0)
    return rows.astype(jnp.bfloat16)


def draw_teacher_feats(key, part):
    rows = feature_rows(key, 41, 1.0, 3.0, 1.0, 1.0)
    return rows.astype(jnp.bfloat16)


def draw_mask_index(key, part):
    subkeys = jax.random.split(jax.random.fold_in(key, 51), MASKED // MASK_DEV)
    picks = jax.vmap(lambda subkey: jax.random.permutation(subkey, PATCH_DEV)[:MASK_DEV])(subkeys)
    return picks.reshape(-1).astype(jnp.int32)


def block_scale(stream_key, dims, cuts, smallest, high):
    gain = 1.0
    for dim, parts in cuts:
        draws = jax.random.uniform(jax.random.fold_in(jax.random.fold_in(stream_key, 6), dim), (parts,), jnp.float32, smallest / len(cuts), high / len(cuts))
        gain = gain * jnp.repeat(jnp.exp(draws), dims[dim] // parts).reshape((-1,) + (1,) * (len(dims) - 1 - dim))
    return gain


def setup_inputs(seed: int = 0) -> dict:
    key_list = jax.random.split(jax.random.key(seed), 6)
    student_feats = draw_student_feats(jax.random.fold_in(key_list[5], 71), 0)
    teacher_feats = draw_teacher_feats(jax.random.fold_in(key_list[5], 71), 0)
    proto_weight = draw_proto_weight(jax.random.fold_in(key_list[5], 71), 0)
    mask_index = draw_mask_index(jax.random.fold_in(key_list[5], 71), 0)
    row_weight = jnp.clip(jnp.exp(math.log(4.0) - 2.0794415 * jax.random.uniform(key_list[4], (MASKED,), jnp.float32) ** block_scale(key_list[4], (MASKED,), ((0, 128),), -0.2, 0.2)), 0.5, 4.0).astype(jnp.bfloat16)
    return dict(student_feats=student_feats, teacher_feats=teacher_feats, proto_weight=proto_weight, mask_index=mask_index, row_weight=row_weight)


eps = 1e-06
teacher_temp = 0.07
student_temp = 0.1

def unit_rows(values):
    values = values.astype(jnp.float32)
    inverse = lax.rsqrt(lax.optimization_barrier(jnp.sum(values * values, axis=1)) + eps)
    return (values * inverse[:, None], inverse)

def reference(student_feats, teacher_feats, proto_weight, mask_index, row_weight):
    images = jnp.arange(MASKED, dtype=jnp.int32) // MASK_DEV
    position = (mask_index.astype(jnp.int32) + images * PATCH_DEV).astype(jnp.int32)
    unit_student, inverse_student = unit_rows(jnp.take(student_feats, position, axis=0))
    unit_teacher, _ = unit_rows(jnp.take(teacher_feats, position, axis=0))
    student_rows = unit_student.astype(jnp.bfloat16)
    teacher_rows = unit_teacher.astype(jnp.bfloat16)
    weights = row_weight.astype(jnp.float32)
    w_float = proto_weight.astype(jnp.float32)
    col_inverse = lax.rsqrt(lax.optimization_barrier(jnp.sum(w_float * w_float, axis=0)) + eps)
    unit_proto = w_float * col_inverse[None, :]
    proto_unit = unit_proto.astype(jnp.bfloat16)
    block = min(P_SIZE, 4096)
    block_count = P_SIZE // block

    def blocks(array):
        return jnp.transpose(array.reshape(array.shape[0], block_count, block), (1, 0, 2))
    proto_blocks = blocks(proto_unit)
    unit_blocks = blocks(unit_proto)
    inverse_blocks = col_inverse.reshape(block_count, block)
    highest = lax.Precision.HIGHEST

    def teacher_exp(proto_block):
        return jnp.exp(jnp.dot(teacher_rows, proto_block, preferred_element_type=jnp.float32) / teacher_temp)
    scale_rows = jnp.ones((MASKED,), jnp.float32)
    col_blocks = None
    for sweep in range(SK_ITERS):

        def sweep_block(row_partial, proto_block):
            table = teacher_exp(proto_block)
            scale_cols = 1.0 / jnp.dot(scale_rows, table, precision=highest)
            return (row_partial + jnp.dot(table, scale_cols, precision=highest), scale_cols)
        row_total, col_blocks = lax.scan(sweep_block, jnp.zeros((MASKED,), jnp.float32), proto_blocks)
        scale_rows = 1.0 / row_total

    def exp_block(exp_partial, proto_block):
        logits = jnp.dot(student_rows, proto_block, preferred_element_type=jnp.float32) / student_temp
        return (exp_partial + lax.optimization_barrier(jnp.sum(jnp.exp(logits), axis=1)), None)
    exp_total, _ = lax.scan(exp_block, jnp.zeros((MASKED,), jnp.float32), proto_blocks)
    log_total = jnp.log(exp_total)

    def final_block(carry, pieces):
        feature_partial, loss_partial = carry
        proto_block, unit_block, inverse_block, scale_cols = pieces
        codes = teacher_exp(proto_block) * scale_rows[:, None] * scale_cols[None, :]
        logits = jnp.dot(student_rows, proto_block, preferred_element_type=jnp.float32) / student_temp
        student_probs = jnp.exp(logits) / exp_total[:, None]
        grad_logits = (weights[:, None] * (student_probs - codes)).astype(jnp.bfloat16)
        loss_partial = loss_partial + jnp.sum(weights[:, None] * codes * (log_total[:, None] - logits))
        feature_partial = feature_partial + jnp.dot(grad_logits, proto_block.T, preferred_element_type=jnp.float32) / student_temp
        head = jnp.dot(student_rows.T, grad_logits, preferred_element_type=jnp.float32) / student_temp
        inner = lax.optimization_barrier(jnp.sum(unit_block * head, axis=0))
        return ((feature_partial, loss_partial), inverse_block[None, :] * (head - unit_block * inner[None, :]))
    start_carry = (jnp.zeros((MASKED, D), jnp.float32), jnp.zeros((), jnp.float32))
    (feature_grad, loss_sum), grad_blocks = lax.scan(final_block, start_carry, (proto_blocks, unit_blocks, inverse_blocks, col_blocks))
    grad_proto = jnp.transpose(grad_blocks, (1, 0, 2)).reshape(D, P_SIZE)
    grad_student = inverse_student[:, None] * (feature_grad - unit_student * lax.optimization_barrier(jnp.sum(unit_student * feature_grad, axis=1))[:, None])
    loss = loss_sum / jnp.sum(weights)
    return (grad_student, grad_proto, loss)
```

```python
import functools

import jax
import jax.numpy as jnp
from jax import lax
from jax.experimental import pallas as pl
from jax.experimental.pallas import tpu as pltpu
from jax.sharding import PartitionSpec as P

SK_ITERS = 3
EPS = 1e-06
TEACHER_TEMP = 0.07
STUDENT_TEMP = 0.1
F32 = jnp.float32
BF16 = jnp.bfloat16
BLOCK = 2048
VMEM_LIMIT = 48 * 1024 * 1024

NN = (((1,), (0,)), ((), ()))
NT = (((1,), (1,)), ((), ()))


def mm(a, b, dims=NN):
    return lax.dot_general(a, b, dims, preferred_element_type=F32)


def call(body, name, out_shape, flops=0, bytes_accessed=0, **kwargs):
    return pl.pallas_call(
        body,
        name=name,
        out_shape=out_shape,
        compiler_params=pltpu.CompilerParams(vmem_limit_bytes=VMEM_LIMIT),
        cost_estimate=pl.CostEstimate(
            flops=flops, bytes_accessed=bytes_accessed, transcendentals=0
        ),
        **kwargs,
    )


def whole(shape):
    return pl.BlockSpec(shape, lambda j: (0,) * len(shape))


def cols(rows):
    return pl.BlockSpec((rows, BLOCK), lambda j: (0, j))


def shape(dims, dtype):
    return jax.ShapeDtypeStruct(dims, dtype)


def three_terms(row):
    high = row.astype(BF16).astype(F32)
    rest = row - high
    mid = rest.astype(BF16).astype(F32)
    low = rest - mid
    index = lax.broadcasted_iota(jnp.int32, (16, row.shape[1]), 0)
    terms = jnp.where(
        index == 0, high, jnp.where(index == 1, mid, jnp.where(index == 2, low, 0.0))
    )
    return terms.astype(BF16)


def rows_body(place_ref, student_ref, teacher_ref, index_ref, weight_ref, rows_ref, x_ref, w_ref):
    picks = index_ref[...]
    length = student_ref.shape[0]
    count = picks.shape[1]
    one_hot = (lax.broadcasted_iota(jnp.int32, (length, count), 0) == picks).astype(BF16)
    tn = (((0,), (0,)), ((), ()))
    x = mm(one_hot, student_ref[...], tn)
    y = mm(one_hot, teacher_ref[...], tn)
    x_ref[...] = x
    unit_x = x * lax.rsqrt(jnp.sum(x * x, axis=1, keepdims=True) + EPS)
    unit_y = y * lax.rsqrt(jnp.sum(y * y, axis=1, keepdims=True) + EPS)
    both = jnp.concatenate([unit_y.astype(BF16), unit_x.astype(BF16)], axis=0)
    rows_ref[...] = jnp.broadcast_to(both[None], rows_ref.shape)
    lanes = w_ref.shape[1]
    spot = lax.broadcasted_iota(jnp.int32, (count, lanes), 1) - place_ref[0] * count
    spread = (spot == lax.broadcasted_iota(jnp.int32, (count, lanes), 0)).astype(BF16)
    w_ref[...] = jnp.broadcast_to(mm(weight_ref[...], spread), w_ref.shape)


def proto_body(w_ref, unit_ref, inverse_ref):
    w = w_ref[...].astype(F32)
    inverse = lax.rsqrt(jnp.sum(w * w, axis=0, keepdims=True) + EPS)
    inverse_ref[...] = inverse
    unit_ref[...] = (w * inverse).astype(BF16)


def table_body(rows_ref, unit_ref, table_ref, sums_ref):
    half = rows_ref.shape[1] // 2
    teacher = rows_ref[:, :half, :].reshape(-1, rows_ref.shape[2])
    table = jnp.exp(mm(teacher, unit_ref[...]) * (1.0 / TEACHER_TEMP)).astype(BF16)
    table_ref[...] = table
    total = jnp.sum(table.astype(F32), axis=0, keepdims=True)
    sums_ref[...] = jnp.broadcast_to(total, sums_ref.shape)


def row_pass_body(sums_ref, table_ref, extra_ref, out_ref, acc_ref):
    @pl.when(pl.program_id(0) == 0)
    def _():
        acc_ref[...] = jnp.zeros_like(acc_ref)

    scale = 1.0 / jnp.sum(sums_ref[...], axis=0, keepdims=True)
    acc_ref[...] += mm(three_terms(scale), table_ref[...], NT)

    @pl.when(pl.program_id(0) == pl.num_programs(0) - 1)
    def _():
        total = jnp.sum(acc_ref[...], axis=0, keepdims=True)
        n = total.shape[1]
        out_ref[:, :n] = jnp.broadcast_to(total, (out_ref.shape[0], n))
        if out_ref.shape[1] > n:
            out_ref[:, n:] = jnp.broadcast_to(extra_ref[0:1, :], (out_ref.shape[0], n))


def col_pass_body(totals_ref, table_ref, out_ref):
    n = table_ref.shape[0]
    scale = 1.0 / jnp.sum(totals_ref[:, :n], axis=0, keepdims=True)
    total = jnp.sum(mm(three_terms(scale), table_ref[...]), axis=0, keepdims=True)
    out_ref[...] = jnp.broadcast_to(total, out_ref.shape)


def student_body(rows_ref, unit_ref, table_ref, sums_ref, feature_ref, turned_ref, acc_ref):
    half = rows_ref.shape[1] // 2
    student = rows_ref[:, half:, :].reshape(-1, rows_ref.shape[2])
    first = pl.program_id(0) == 0

    @pl.when(first)
    def _():
        acc_ref[...] = jnp.zeros_like(acc_ref)
        feature_ref[...] = jnp.zeros_like(feature_ref)
        d = student.shape[1]
        eye = (
            lax.broadcasted_iota(jnp.int32, (d, d), 0)
            == lax.broadcasted_iota(jnp.int32, (d, d), 1)
        ).astype(BF16)
        turned_ref[...] = mm(eye, student, NT).astype(BF16)

    unit = unit_ref[...]
    table = jnp.exp(mm(student, unit) * (1.0 / STUDENT_TEMP)).astype(BF16)
    table_ref[...] = table
    ones = jnp.ones((16, table.shape[1]), BF16)
    acc_ref[...] += mm(ones, table, NT)
    feature_ref[...] += mm(unit, table, NT)

    @pl.when(pl.program_id(0) == pl.num_programs(0) - 1)
    def _():
        sums_ref[...] = acc_ref[0:8, :]


def codes_feature_body(sums_ref, unit_ref, table_ref, feature_ref):
    @pl.when(pl.program_id(0) == 0)
    def _():
        feature_ref[...] = jnp.zeros_like(feature_ref)

    scale = 1.0 / jnp.sum(sums_ref[...], axis=0, keepdims=True)
    scaled = (unit_ref[...].astype(F32) * scale).astype(BF16)
    feature_ref[...] += mm(scaled, table_ref[...], NT)


def head_body(
    place_ref,
    totals_ref,
    exp_totals_ref,
    sums_ref,
    turned_ref,
    codes_ref,
    probs_ref,
    w_ref,
    inverse_ref,
    keep_ref,
    send_ref,
    grad_ref,
):
    n = codes_ref.shape[0]
    row_scale = 1.0 / jnp.sum(totals_ref[:, :n], axis=0, keepdims=True)
    exp_total = jnp.sum(exp_totals_ref[:, :n], axis=0, keepdims=True)
    weights = jnp.sum(exp_totals_ref[:, n:], axis=0, keepdims=True)
    turned = turned_ref[...].astype(F32)
    left_probs = (turned * (weights / exp_total * (1.0 / STUDENT_TEMP))).astype(BF16)
    left_codes = (turned * (weights * row_scale * (1.0 / STUDENT_TEMP))).astype(BF16)
    scale_cols = 1.0 / jnp.sum(sums_ref[...], axis=0, keepdims=True)
    head = mm(left_probs, probs_ref[...]) - scale_cols * mm(left_codes, codes_ref[...])
    inverse = inverse_ref[...]
    unit = w_ref[...].astype(F32) * inverse
    inner = jnp.sum(unit * head, axis=0, keepdims=True)
    grad = inverse * (head - unit * inner)
    grad_ref[...] = grad.reshape(grad_ref.shape)
    x = place_ref[1]
    core = place_ref[2]
    for k in range(keep_ref.shape[0]):
        keep_ref[k] = grad_ref[x ^ k, core]
        send_ref[k] = grad_ref[x ^ k, 1 - core].astype(BF16)


def feature_body(
    totals_ref, exp_totals_ref, probs_ref, codes_ref, turned_ref, out_ref, loss_ref
):
    n = probs_ref.shape[1]
    total = jnp.sum(totals_ref[:, :n], axis=0, keepdims=True)
    exp_total = jnp.sum(exp_totals_ref[:, :n], axis=0, keepdims=True)
    weights = jnp.sum(exp_totals_ref[:, n:], axis=0, keepdims=True)
    codes = codes_ref[...]
    over = weights / total * (1.0 / STUDENT_TEMP)
    feature = probs_ref[...] * (weights / exp_total * (1.0 / STUDENT_TEMP)) - codes * over
    rows = feature.T.astype(BF16)
    out_ref[...] = rows.reshape(out_ref.shape)
    share = 1.0 / out_ref.shape[0]
    cross = jnp.sum(turned_ref[...].astype(F32) * codes, axis=0, keepdims=True)
    part = jnp.sum(weights * jnp.log(exp_total) * share - over * cross)
    count = jnp.sum(weights) * share
    lane = lax.broadcasted_iota(jnp.int32, loss_ref.shape, 1)
    loss_ref[...] = jnp.where(lane == 0, part, jnp.where(lane == 1, count, 0.0))


def on_device(student_feats, teacher_feats, proto_weight, mask_index, row_weight):
    n_patch, n_proto = lax.axis_size("patch"), lax.axis_size("proto")
    d, protos = proto_weight.shape
    own = mask_index.shape[0]
    rows = own * n_proto
    steps = protos // BLOCK
    chips = n_patch // 2
    share = d // n_patch
    patch, proto = lax.axis_index("patch"), lax.axis_index("proto")
    place = jnp.stack([proto, patch // 2, patch % 2]).astype(jnp.int32)
    smem = pl.BlockSpec(memory_space=pltpu.SMEM)
    product = 2 * rows * d * protos
    table_bytes = rows * protos * 2

    def exchange(array, axis):
        return lax.all_to_all(array, axis, 0, 0, tiled=True)

    own_rows, x_rows, own_weights = call(
        rows_body,
        "own_rows",
        (
            shape((n_proto, 2 * own, d), BF16),
            shape((own, d), F32),
            shape((n_proto, rows), F32),
        ),
        flops=1 << 24,
        bytes_accessed=1 << 21,
        in_specs=[smem] + [pl.BlockSpec(memory_space=pltpu.VMEM)] * 4,
    )(place, student_feats, teacher_feats, mask_index[None, :], row_weight[None, :])

    unit, inverse = call(
        proto_body,
        "proto_unit",
        (shape((d, protos), BF16), shape((1, protos), F32)),
        flops=6 * d * protos,
        bytes_accessed=4 * d * protos,
        grid=(steps,),
        in_specs=[cols(d)],
        out_specs=[cols(d), cols(1)],
    )(proto_weight)

    all_rows = exchange(own_rows, "proto")
    rows_spec = whole((n_proto, 2 * own, d))

    codes, sums = call(
        table_body,
        "teacher_table",
        (shape((rows, protos), BF16), shape((n_patch, protos), F32)),
        flops=product,
        bytes_accessed=table_bytes,
        grid=(steps,),
        in_specs=[rows_spec, cols(d)],
        out_specs=[cols(rows), cols(n_patch)],
    )(all_rows, unit)

    probs, exp_sums, probs_feature, turned = call(
        student_body,
        "student_table",
        (
            shape((rows, protos), BF16),
            shape((8, rows), F32),
            shape((d, rows), F32),
            shape((d, rows), BF16),
        ),
        flops=2 * product,
        bytes_accessed=table_bytes,
        grid=(steps,),
        in_specs=[rows_spec, cols(d)],
        out_specs=[cols(rows), whole((8, rows)), whole((d, rows)), whole((d, rows))],
        scratch_shapes=[pltpu.VMEM((16, rows), F32)],
    )(all_rows, unit)
    exp_part = jnp.concatenate(
        [jnp.broadcast_to(exp_sums[0:1], (n_proto, rows)), own_weights], axis=1
    )
    exp_totals = exchange(exp_part, "proto")

    for sweep in range(SK_ITERS):
        all_sums = exchange(sums, "patch")
        part = call(
            row_pass_body,
            "row_pass",
            shape((n_proto, rows), F32),
            flops=product // 4,
            bytes_accessed=table_bytes,
            grid=(steps,),
            in_specs=[cols(n_patch), cols(rows), whole((8, rows))],
            out_specs=whole((n_proto, rows)),
            scratch_shapes=[pltpu.VMEM((16, rows), F32)],
        )(all_sums, codes, exp_sums)
        totals = exchange(part, "proto")
        if sweep < SK_ITERS - 1:
            sums = call(
                col_pass_body,
                "col_pass",
                shape((n_patch, protos), F32),
                flops=product // 4,
                bytes_accessed=table_bytes,
                grid=(steps,),
                in_specs=[whole((n_proto, rows)), cols(rows)],
                out_specs=cols(n_patch),
            )(totals, codes)

    codes_feature = call(
        codes_feature_body,
        "codes_feature",
        shape((d, rows), F32),
        flops=product,
        bytes_accessed=table_bytes,
        grid=(steps,),
        in_specs=[cols(n_patch), cols(d), cols(rows)],
        out_specs=whole((d, rows)),
    )(all_sums, unit, codes)

    keep, send = call(
        head_body,
        "head",
        (shape((chips, share, protos), F32), shape((chips, share, protos), BF16)),
        flops=2 * product,
        bytes_accessed=3 * table_bytes,
        grid=(steps,),
        in_specs=[
            smem,
            whole((n_proto, rows)),
            whole((n_proto, 2 * rows)),
            cols(n_patch),
            whole((d, rows)),
            cols(rows),
            cols(rows),
            cols(d),
            cols(1),
        ],
        out_specs=[
            pl.BlockSpec((chips, share, BLOCK), lambda j: (0, 0, j)),
            pl.BlockSpec((chips, share, BLOCK), lambda j: (0, 0, j)),
        ],
        scratch_shapes=[pltpu.VMEM((chips, 2, share, BLOCK), F32)],
    )(place, totals, exp_totals, all_sums, turned, codes, probs, proto_weight, inverse)

    def hop(array, bits):
        return lax.ppermute(array, "patch", [(i, i ^ bits) for i in range(n_patch)])

    near = hop(send, 1)
    grad_proto = keep[0] + near[0].astype(F32)
    for k in range(1, chips):
        pair = (keep[k] + near[k].astype(F32)).astype(BF16)
        grad_proto = grad_proto + hop(pair, 2 * k).astype(F32)

    feature_part, loss_part = call(
        feature_body,
        "feature",
        (shape((n_proto, own, d), BF16), shape((n_patch * n_proto, 128), F32)),
        flops=1 << 24,
        bytes_accessed=1 << 21,
    )(totals, exp_totals, probs_feature, codes_feature, turned)
    feature = jnp.sum(exchange(feature_part, "proto").astype(F32), axis=0)
    losses = jnp.sum(exchange(loss_part, ("patch", "proto")), axis=0)
    loss = losses[0] / losses[1]

    inverse_student = lax.rsqrt(jnp.sum(x_rows * x_rows, axis=1, keepdims=True) + EPS)
    unit_student = x_rows * inverse_student
    grad_student = inverse_student * (
        feature - unit_student * jnp.sum(unit_student * feature, axis=1, keepdims=True)
    )
    return (grad_student, grad_proto, loss)


def solution(mesh):
    both = ("patch", "proto")
    in_specs = (P(both, None), P(both, None), P(None, "proto"), P(both), P(both))
    out_specs = (P(both, None), P("patch", "proto"), P())
    return jax.shard_map(
        on_device, mesh=mesh, in_specs=in_specs, out_specs=out_specs, check_vma=False
    )
```

```python
import functools

import jax
import jax.numpy as jnp
from jax import lax
from jax.experimental import pallas as pl
from jax.experimental.pallas import tpu as pltpu
from jax.sharding import PartitionSpec as P

SK_ITERS = 3
EPS = 1e-06
TEACHER_TEMP = 0.07
STUDENT_TEMP = 0.1
F32 = jnp.float32
BF16 = jnp.bfloat16
LANES = 128
VMEM_LIMIT = 20 * 1024 * 1024

NN = (((1,), (0,)), ((), ()))
NT = (((1,), (1,)), ((), ()))
TN = (((0,), (0,)), ((), ()))
SMEM = pl.BlockSpec(memory_space=pltpu.SMEM)
VMEM = pl.BlockSpec(memory_space=pltpu.VMEM)
ANY = pl.BlockSpec(memory_space=pl.ANY)
HBM = pl.BlockSpec(memory_space=pltpu.HBM)


def mm(a, b, dims=NN):
    return lax.dot_general(a, b, dims, preferred_element_type=F32)


def shape(dims, dtype):
    return jax.ShapeDtypeStruct(dims, dtype)


def call(body, name, out_shape, args, flops, specs=None, outs=None, after=(), scratch=()):
    specs = specs or [VMEM] * len(args)
    skip = len(after)

    def ordered(*refs):
        body(*refs[skip:])

    many = isinstance(out_shape, tuple)
    return pl.pallas_call(
        ordered,
        name=name,
        out_shape=out_shape,
        in_specs=[ANY] * skip + specs,
        out_specs=outs or (tuple(VMEM for _ in out_shape) if many else VMEM),
        scratch_shapes=list(scratch),
        compiler_params=pltpu.CompilerParams(vmem_limit_bytes=VMEM_LIMIT),
        cost_estimate=pl.CostEstimate(flops=flops, bytes_accessed=1 << 16, transcendentals=0),
    )(*after, *args)


def three_terms(row):
    high = row.astype(BF16).astype(F32)
    rest = row - high
    mid = rest.astype(BF16).astype(F32)
    low = rest - mid
    index = lax.broadcasted_iota(jnp.int32, (16, row.shape[1]), 0)
    terms = jnp.where(
        index == 0, high, jnp.where(index == 1, mid, jnp.where(index == 2, low, 0.0))
    )
    return terms.astype(BF16)


def column_sum(refs):
    total = refs[0][...]
    for ref in refs[1:]:
        total = total + ref[...]
    return total


def chunks(table_ref, count=8):
    width = table_ref.shape[1] // count
    return [(j, pl.ds(j * width, width)) for j in range(count)]


def fetch(hbm_ref, start, held_ref, sems, count):
    width = held_ref.shape[1] // count
    copies = [
        pltpu.make_async_copy(
            hbm_ref.at[:, pl.ds(start + j * width, width)],
            held_ref.at[:, pl.ds(j * width, width)],
            sems.at[j],
        )
        for j in range(count)
    ]
    for copy in copies:
        copy.start()
    return copies


def read_rows(message_ref, start, n):
    total = jnp.sum(message_ref[...], axis=0)
    pieces = [total[start + k : start + k + 1, :] for k in range(n // LANES)]
    return jnp.concatenate(pieces, axis=1)


def write_rows(message_ref, start, row):
    count = message_ref.shape[0]
    for k in range(row.shape[1] // LANES):
        piece = row[:, k * LANES : (k + 1) * LANES]
        message_ref[:, start + k, :] = jnp.broadcast_to(piece, (count, LANES))


def rows_body(
    place_ref,
    student_hbm,
    teacher_hbm,
    index_hbm,
    weight_hbm,
    rows_ref,
    x_ref,
    w_ref,
    student_ref,
    teacher_ref,
    index_ref,
    weight_ref,
    sems,
):
    copies = [
        pltpu.make_async_copy(index_hbm, index_ref, sems.at[0]),
        pltpu.make_async_copy(teacher_hbm, teacher_ref, sems.at[1]),
        pltpu.make_async_copy(student_hbm, student_ref, sems.at[2]),
        pltpu.make_async_copy(weight_hbm, weight_ref, sems.at[3]),
    ]
    for copy in copies:
        copy.start()
    for copy in copies:
        copy.wait()
    picks = index_ref[...]
    length = student_ref.shape[0]
    count = picks.shape[1]
    one_hot = (lax.broadcasted_iota(jnp.int32, (length, count), 0) == picks).astype(BF16)
    x = mm(one_hot, student_ref[...], TN)
    y = mm(one_hot, teacher_ref[...], TN)
    x_ref[...] = x
    unit_x = x * lax.rsqrt(jnp.sum(x * x, axis=1, keepdims=True) + EPS)
    unit_y = y * lax.rsqrt(jnp.sum(y * y, axis=1, keepdims=True) + EPS)
    both = jnp.concatenate([unit_y.astype(BF16), unit_x.astype(BF16)], axis=0)
    rows_ref[...] = jnp.broadcast_to(both[None], rows_ref.shape)
    lanes = w_ref.shape[1]
    spot = lax.broadcasted_iota(jnp.int32, (count, lanes), 1) - place_ref[0] * count
    spread = (spot == lax.broadcasted_iota(jnp.int32, (count, lanes), 0)).astype(BF16)
    w_ref[...] = jnp.broadcast_to(mm(weight_ref[...], spread), w_ref.shape)


def proto_body(w_hbm, unit_hbm, inverse_ref, w_ref, unit_ref, in_sems, out_sems):
    copies = fetch(w_hbm, 0, w_ref, in_sems, 8)
    stores = []
    for j, cols in chunks(w_ref):
        copies[j].wait()
        w = w_ref[:, cols].astype(F32)
        inverse = lax.rsqrt(jnp.sum(w * w, axis=0, keepdims=True) + EPS)
        inverse_ref[pl.ds(j, 1), :] = inverse
        unit_ref[:, cols] = (w * inverse).astype(BF16)
        store = pltpu.make_async_copy(unit_ref.at[:, cols], unit_hbm.at[:, cols], out_sems.at[j])
        store.start()
        stores.append(store)
    for store in stores:
        store.wait()


def table_body(rows_ref, unit_hbm, table_ref, sums_ref, unit_ref, sems):
    copies = fetch(unit_hbm, 0, unit_ref, sems, 8)
    half = rows_ref.shape[1] // 2
    teacher = rows_ref[:, :half, :].reshape(-1, rows_ref.shape[2])
    for j, cols in chunks(table_ref):
        copies[j].wait()
        table = jnp.exp(mm(teacher, unit_ref[:, cols]) * (1.0 / TEACHER_TEMP)).astype(BF16)
        table_ref[:, cols] = table
        sums_ref[pl.ds(j, 1), :] = jnp.sum(table.astype(F32), axis=0, keepdims=True)


def row_pass_body(parts, *refs):
    sums_refs, table_ref, extra_refs, out_ref = refs[:parts], refs[parts], refs[parts + 1 : -1], refs[-1]
    scale = 1.0 / column_sum(sums_refs)
    n = table_ref.shape[0]
    total = jnp.zeros((16, n), F32)
    for j, cols in chunks(table_ref):
        total += mm(three_terms(scale[j : j + 1, :]), table_ref[:, cols], NT)
    write_rows(out_ref, 0, jnp.sum(total, axis=0, keepdims=True))
    write_rows(out_ref, n // LANES, column_sum(extra_refs)[0:1, :])


def col_pass_body(message_ref, table_ref, out_ref):
    terms = three_terms(1.0 / read_rows(message_ref, 0, table_ref.shape[0]))
    for j, cols in chunks(table_ref):
        out_ref[pl.ds(j, 1), :] = jnp.sum(mm(terms, table_ref[:, cols]), axis=0, keepdims=True)


def student_body(start, rows_ref, unit_hbm, table_ref, sums_ref, feature_ref, turned_ref, unit_ref, sems):
    copies = fetch(unit_hbm, start, unit_ref, sems, 4)
    half = rows_ref.shape[1] // 2
    student = rows_ref[:, half:, :].reshape(-1, rows_ref.shape[2])
    d = student.shape[1]
    if start == 0:
        eye = (
            lax.broadcasted_iota(jnp.int32, (d, d), 0)
            == lax.broadcasted_iota(jnp.int32, (d, d), 1)
        ).astype(BF16)
        turned_ref[...] = mm(eye, student, NT).astype(BF16)
    total = jnp.zeros((16, student.shape[0]), F32)
    for j, cols in chunks(table_ref, 4):
        copies[j].wait()
        unit = unit_ref[:, cols]
        table = jnp.exp(mm(student, unit) * (1.0 / STUDENT_TEMP)).astype(BF16)
        table_ref[:, cols] = table
        total += mm(jnp.ones((16, table.shape[1]), BF16), table, NT)
        part = mm(unit, table, NT)
        if j == 0:
            feature_ref[...] = part
        else:
            feature_ref[...] += part
    sums_ref[...] = total[0:8]


def codes_feature_body(*refs):
    *sums_refs, unit_hbm, table_ref, feature_ref, unit_ref, sems = refs
    copies = fetch(unit_hbm, 0, unit_ref, sems, 8)
    scale = 1.0 / column_sum(sums_refs)
    for j, cols in chunks(table_ref):
        copies[j].wait()
        scaled = (unit_ref[:, cols].astype(F32) * scale[j : j + 1, :]).astype(BF16)
        part = mm(scaled, table_ref[:, cols], NT)
        if j == 0:
            feature_ref[...] = part
        else:
            feature_ref[...] += part


def row_factors(first_ref, second_ref, third_ref, n):
    tile = n // LANES
    return (
        read_rows(first_ref, tile, n),
        read_rows(second_ref, tile, n),
        read_rows(third_ref, 0, n),
    )


def head_body(half, *refs):
    (place_ref, first_ref, second_ref, third_ref, *sums_refs) = refs[:-11]
    (turned_ref, codes_ref, probs_ref, w_hbm, inverse_ref) = refs[-11:-6]
    (keep_ref, near_ref, grad_ref, w_ref, sems, _) = refs[-6:]
    count = 4
    span = probs_ref.shape[1]
    copies = fetch(w_hbm, half * span, w_ref, sems, count)
    n = codes_ref.shape[0]
    weights, exp_total, total = row_factors(first_ref, second_ref, third_ref, n)
    turned = turned_ref[...].astype(F32)
    left_probs = (turned * (weights / exp_total * (1.0 / STUDENT_TEMP))).astype(BF16)
    left_codes = (turned * (weights / total * (1.0 / STUDENT_TEMP))).astype(BF16)
    scale = 1.0 / column_sum(sums_refs)
    x = place_ref[1]
    core = place_ref[2]
    for j, cols in chunks(probs_ref, count):
        row = half * count + j
        here = pl.ds(half * span + j * (span // count), span // count)
        head = mm(left_probs, probs_ref[:, cols]) - scale[row : row + 1, :] * mm(
            left_codes, codes_ref[:, here]
        )
        copies[j].wait()
        inverse = inverse_ref[pl.ds(row, 1), :]
        unit = w_ref[:, cols].astype(F32) * inverse
        inner = jnp.sum(unit * head, axis=0, keepdims=True)
        grad = inverse * (head - unit * inner)
        grad_ref[...] = grad.reshape(grad_ref.shape)
        for k in range(keep_ref.shape[0]):
            keep_ref[k, :, cols] = grad_ref[x ^ k, core]
            near_ref[k, :, cols] = grad_ref[x ^ k, 1 - core].astype(BF16)


def feature_body(
    first_ref, second_ref, third_ref, left_ref, right_ref, codes_ref, turned_ref, out_ref
):
    n = codes_ref.shape[1]
    weights, exp_total, total = row_factors(first_ref, second_ref, third_ref, n)
    codes = codes_ref[...]
    probs = left_ref[...] + right_ref[...]
    over = weights / total * (1.0 / STUDENT_TEMP)
    feature = probs * (weights / exp_total * (1.0 / STUDENT_TEMP)) - codes * over
    own = n // out_ref.shape[0]
    out_ref[:, :own, :] = feature.T.reshape(out_ref.shape[0], own, out_ref.shape[2])
    share = 1.0 / out_ref.shape[0]
    cross = jnp.sum(turned_ref[...].astype(F32) * codes, axis=0, keepdims=True)
    part = jnp.sum(weights * jnp.log(exp_total) * share - over * cross)
    count = jnp.sum(weights) * share
    tail = (out_ref.shape[0], out_ref.shape[1] - own, out_ref.shape[2])
    lane = lax.broadcasted_iota(jnp.int32, tail, 2)
    out_ref[:, own:, :] = jnp.where(lane == 0, part, jnp.where(lane == 1, count, 0.0))


def on_device(student_feats, teacher_feats, proto_weight, mask_index, row_weight):
    n_patch, n_proto = lax.axis_size("patch"), lax.axis_size("proto")
    d, protos = proto_weight.shape
    length = student_feats.shape[0]
    own = mask_index.shape[0]
    rows = own * n_proto
    chips = n_patch // 2
    share = d // n_patch
    width = protos // 8
    patch, proto = lax.axis_index("patch"), lax.axis_index("proto")
    place = jnp.stack([proto, patch // 2, patch % 2]).astype(jnp.int32)
    product = 2 * rows * d * protos

    def exchange(array, axis):
        return lax.all_to_all(array, axis, 0, 0)

    def hop(array, bits):
        return lax.ppermute(array, "patch", [(i, i ^ bits) for i in range(n_patch)])

    own_rows, x_rows, own_weights = call(
        rows_body,
        "own_rows",
        (
            shape((n_proto, 2 * own, d), BF16),
            shape((own, d), F32),
            shape((8, rows), F32),
        ),
        (place, student_feats, teacher_feats, mask_index[None, :], row_weight[None, :]),
        1 << 28,
        specs=[SMEM, HBM, HBM, HBM, HBM],
        scratch=[
            pltpu.VMEM((length, d), BF16),
            pltpu.VMEM((length, d), BF16),
            pltpu.VMEM((1, own), jnp.int32),
            pltpu.VMEM((1, own), BF16),
            pltpu.SemaphoreType.DMA((4,)),
        ],
    )
    all_rows = exchange(own_rows, "proto")
    unit, inverse = call(
        proto_body,
        "proto_unit",
        (shape((d, protos), BF16), shape((8, width), F32)),
        (proto_weight,),
        product,
        specs=[HBM],
        outs=(HBM, VMEM),
        scratch=[
            pltpu.VMEM((d, protos), BF16),
            pltpu.VMEM((d, protos), BF16),
            pltpu.SemaphoreType.DMA((8,)),
            pltpu.SemaphoreType.DMA((8,)),
        ],
    )
    unit_scratch = [pltpu.VMEM((d, protos), BF16), pltpu.SemaphoreType.DMA((8,))]
    codes, sums = call(
        table_body,
        "teacher_table",
        (shape((rows, protos), BF16), shape((8, width), F32)),
        (all_rows, unit),
        2 * product,
        specs=[VMEM, HBM],
        scratch=unit_scratch,
    )

    extras = (own_weights,)
    messages = []
    halves = []
    for sweep in range(SK_ITERS):
        sums = sums + hop(sums, 1)
        parts = [sums] + [hop(sums, 2 * k) for k in range(1, chips)]
        if sweep < 2:
            halves.append(
                call(
                    functools.partial(student_body, sweep * (protos // 2)),
                    "student_table",
                    (
                        shape((rows, protos // 2), BF16),
                        shape((8, rows), F32),
                        shape((d, rows), F32),
                        shape((d, rows), BF16),
                    ),
                    (all_rows, unit),
                    3 * product // 2,
                    specs=[VMEM, HBM],
                    after=(sums,),
                    scratch=[pltpu.VMEM((d, protos // 2), BF16), pltpu.SemaphoreType.DMA((4,))],
                )
            )
        if sweep == 1:
            extras = (halves[0][1], halves[1][1])
        part = call(
            functools.partial(row_pass_body, chips),
            "row_pass",
            shape((n_proto, 8, LANES), F32),
            (*parts, codes, *extras),
            product,
            after=(halves[sweep][1],) if sweep == 0 else (),
        )
        messages.append(exchange(part, "proto"))
        if sweep < SK_ITERS - 1:
            sums = call(
                col_pass_body,
                "col_pass",
                shape((8, width), F32),
                (messages[-1], codes),
                product // 2,
            )

    turned = halves[0][3]
    keeps, nears = [], []
    for half in range(2):
        keep, near = call(
            functools.partial(head_body, half),
            "head",
            (
                shape((chips, share, protos // 2), F32),
                shape((chips, share, protos // 2), BF16),
            ),
            (place, *messages, *parts, turned, codes, halves[half][0], proto_weight, inverse),
            2 * product,
            specs=[SMEM] + [VMEM] * (len(messages) + len(parts) + 3) + [HBM, VMEM],
            after=tuple(nears[-1:]),
            scratch=[
                pltpu.VMEM((chips, 2, share, width), F32),
                pltpu.VMEM((d, protos // 2), BF16),
                pltpu.SemaphoreType.DMA((4,)),
                pltpu.VMEM((8, LANES), F32),
            ],
        )
        keeps.append(keep)
        nears.append(near)
    codes_feature = call(
        codes_feature_body,
        "codes_feature",
        shape((d, rows), F32),
        (*parts, unit, codes),
        product,
        specs=[VMEM] * len(parts) + [HBM, VMEM],
        after=(nears[-1],),
        scratch=unit_scratch,
    )
    grads = []
    for keep, near in zip(keeps, nears):
        near = hop(near, 1)
        pairs = [(keep[k] + near[k].astype(F32)).astype(BF16) for k in range(1, chips)]
        far = [hop(pair, 2 * (k + 1)) for k, pair in enumerate(pairs)]
        grad = keep[0] + near[0].astype(F32)
        for array in far:
            grad = grad + array.astype(F32)
        grads.append(grad)
    grad_proto = jnp.concatenate(grads, axis=1)

    feature_part = call(
        feature_body,
        "feature",
        shape((n_proto, own + 8, d), F32),
        (*messages, halves[0][2], halves[1][2], codes_feature, turned),
        product // 4,
        after=(pairs[-1],),
    )
    sent = jnp.sum(exchange(feature_part, "proto"), axis=0)
    feature, tail = sent[:own], sent[own:, :LANES]
    losses = jnp.sum(exchange(jnp.broadcast_to(tail[None], (n_patch, 8, LANES)), "patch"), axis=0)
    loss = losses[0, 0] / losses[0, 1]

    inverse_student = lax.rsqrt(jnp.sum(x_rows * x_rows, axis=1, keepdims=True) + EPS)
    unit_student = x_rows * inverse_student
    grad_student = inverse_student * (
        feature - unit_student * jnp.sum(unit_student * feature, axis=1, keepdims=True)
    )
    return (grad_student, grad_proto, loss)


def solution(mesh):
    both = ("patch", "proto")
    in_specs = (P(both, None), P(both, None), P(None, "proto"), P(both), P(both))
    out_specs = (P(both, None), P("patch", "proto"), P())
    return jax.shard_map(
        on_device, mesh=mesh, in_specs=in_specs, out_specs=out_specs, check_vma=False
    )
```

```python
import functools

import jax
import jax.numpy as jnp
from jax import lax
from jax.experimental import pallas as pl
from jax.experimental.pallas import tpu as pltpu
from jax.sharding import PartitionSpec as P

SK_ITERS = 3
EPS = 1e-06
TEACHER_TEMP = 0.07
STUDENT_TEMP = 0.1
F32 = jnp.float32
BF16 = jnp.bfloat16
LANES = 128
VMEM_LIMIT = 20 * 1024 * 1024

NN = (((1,), (0,)), ((), ()))
NT = (((1,), (1,)), ((), ()))
TN = (((0,), (0,)), ((), ()))
SMEM = pl.BlockSpec(memory_space=pltpu.SMEM)
VMEM = pl.BlockSpec(memory_space=pltpu.VMEM)
ANY = pl.BlockSpec(memory_space=pl.ANY)
HBM = pl.BlockSpec(memory_space=pltpu.HBM)


def mm(a, b, dims=NN):
    return lax.dot_general(a, b, dims, preferred_element_type=F32)


def shape(dims, dtype):
    return jax.ShapeDtypeStruct(dims, dtype)


def call(body, name, out_shape, args, flops, specs=None, after=(), scratch=(), limit=VMEM_LIMIT):
    specs = specs or [VMEM] * len(args)
    skip = len(after)
    args = [
        pltpu.with_memory_space_constraint(arg, pltpu.HBM) if spec is HBM else arg
        for arg, spec in zip(args, specs)
    ]

    def ordered(*refs):
        body(*refs[skip:])

    def out_spec(out):
        return VMEM if isinstance(out, jax.ShapeDtypeStruct) else HBM

    many = isinstance(out_shape, tuple)
    return pl.pallas_call(
        ordered,
        name=name,
        out_shape=out_shape,
        in_specs=[ANY] * skip + specs,
        out_specs=tuple(map(out_spec, out_shape)) if many else out_spec(out_shape),
        scratch_shapes=list(scratch),
        compiler_params=pltpu.CompilerParams(vmem_limit_bytes=limit),
        cost_estimate=pl.CostEstimate(flops=flops, bytes_accessed=1 << 16, transcendentals=0),
    )(*after, *args)


def three_terms(row):
    high = row.astype(BF16).astype(F32)
    rest = row - high
    mid = rest.astype(BF16).astype(F32)
    low = rest - mid
    index = lax.broadcasted_iota(jnp.int32, (16, row.shape[1]), 0)
    terms = jnp.where(
        index == 0, high, jnp.where(index == 1, mid, jnp.where(index == 2, low, 0.0))
    )
    return terms.astype(BF16)


def column_sum(refs):
    total = refs[0][...]
    for ref in refs[1:]:
        total = total + ref[...]
    return total


def chunks(table_ref, count=8):
    width = table_ref.shape[1] // count
    return [(j, pl.ds(j * width, width)) for j in range(count)]


def move(source, start, target, sems, count):
    width = target.shape[1] // count
    copies = [
        pltpu.make_async_copy(
            source.at[:, pl.ds(start + j * width, width)],
            target.at[:, pl.ds(j * width, width)],
            sems.at[j],
        )
        for j in range(count)
    ]
    for copy in copies:
        copy.start()
    return copies


def store(source, target, cols, sem):
    copy = pltpu.make_async_copy(source.at[:, cols], target.at[:, cols], sem)
    copy.start()
    return copy


def read_rows(message_ref, start, n):
    total = jnp.sum(message_ref[...], axis=0)
    pieces = [total[start + k : start + k + 1, :] for k in range(n // LANES)]
    return jnp.concatenate(pieces, axis=1)


def write_rows(message_ref, start, row):
    count = message_ref.shape[0]
    for k in range(row.shape[1] // LANES):
        piece = row[:, k * LANES : (k + 1) * LANES]
        message_ref[:, start + k, :] = jnp.broadcast_to(piece, (count, LANES))


def rows_body(
    place_ref,
    student_hbm,
    teacher_hbm,
    index_hbm,
    weight_hbm,
    rows_ref,
    x_ref,
    w_ref,
    student_ref,
    teacher_ref,
    index_ref,
    weight_ref,
    sems,
):
    copies = [
        pltpu.make_async_copy(index_hbm, index_ref, sems.at[0]),
        pltpu.make_async_copy(teacher_hbm, teacher_ref, sems.at[1]),
        pltpu.make_async_copy(student_hbm, student_ref, sems.at[2]),
        pltpu.make_async_copy(weight_hbm, weight_ref, sems.at[3]),
    ]
    for copy in copies:
        copy.start()
    for copy in copies:
        copy.wait()
    picks = index_ref[...]
    length = student_ref.shape[0]
    count = picks.shape[1]
    one_hot = (lax.broadcasted_iota(jnp.int32, (length, count), 0) == picks).astype(BF16)
    x = mm(one_hot, student_ref[...], TN)
    y = mm(one_hot, teacher_ref[...], TN)
    x_ref[...] = x
    unit_x = x * lax.rsqrt(jnp.sum(x * x, axis=1, keepdims=True) + EPS)
    unit_y = y * lax.rsqrt(jnp.sum(y * y, axis=1, keepdims=True) + EPS)
    both = jnp.concatenate([unit_y.astype(BF16), unit_x.astype(BF16)], axis=0)
    rows_ref[...] = jnp.broadcast_to(both[None], rows_ref.shape)
    lanes = w_ref.shape[1]
    spot = lax.broadcasted_iota(jnp.int32, (count, lanes), 1) - place_ref[0] * count
    spread = (spot == lax.broadcasted_iota(jnp.int32, (count, lanes), 0)).astype(BF16)
    w_ref[...] = jnp.broadcast_to(mm(weight_ref[...], spread), w_ref.shape)


def proto_body(w_hbm, unit_hbm, inverse_ref, w_ref, unit_ref, in_sems, out_sems):
    copies = move(w_hbm, 0, w_ref, in_sems, 8)
    stores = []
    for j, cols in chunks(w_ref):
        copies[j].wait()
        w = w_ref[:, cols].astype(F32)
        inverse = lax.rsqrt(jnp.sum(w * w, axis=0, keepdims=True) + EPS)
        inverse_ref[pl.ds(j, 1), :] = inverse
        unit_ref[:, cols] = (w * inverse).astype(BF16)
        stores.append(store(unit_ref, unit_hbm, cols, out_sems.at[j]))
    for copy in stores:
        copy.wait()


def table_body(rows_ref, unit_hbm, table_ref, table_hbm, sums_ref, unit_ref, sems, out_sems):
    copies = move(unit_hbm, 0, unit_ref, sems, 8)
    stores = []
    half = rows_ref.shape[1] // 2
    teacher = rows_ref[:, :half, :].reshape(-1, rows_ref.shape[2])
    for j, cols in chunks(table_ref):
        copies[j].wait()
        table = jnp.exp(mm(teacher, unit_ref[:, cols]) * (1.0 / TEACHER_TEMP)).astype(BF16)
        table_ref[:, cols] = table
        sums_ref[pl.ds(j, 1), :] = jnp.sum(table.astype(F32), axis=0, keepdims=True)
        stores.append(store(table_ref, table_hbm, cols, out_sems.at[j]))
    for copy in stores:
        copy.wait()


def row_pass_body(parts, *refs):
    sums_refs, table_ref, extra_refs, out_ref = refs[:parts], refs[parts], refs[parts + 1 : -1], refs[-1]
    scale = 1.0 / column_sum(sums_refs)
    n = table_ref.shape[0]
    total = jnp.zeros((16, n), F32)
    for j, cols in chunks(table_ref):
        total += mm(three_terms(scale[j : j + 1, :]), table_ref[:, cols], NT)
    write_rows(out_ref, 0, jnp.sum(total, axis=0, keepdims=True))
    write_rows(out_ref, n // LANES, column_sum(extra_refs)[0:1, :])


def col_pass_body(message_ref, table_ref, out_ref):
    terms = three_terms(1.0 / read_rows(message_ref, 0, table_ref.shape[0]))
    for j, cols in chunks(table_ref):
        out_ref[pl.ds(j, 1), :] = jnp.sum(mm(terms, table_ref[:, cols]), axis=0, keepdims=True)


def student_body(start, rows_ref, unit_hbm, table_hbm, sums_ref, turned_ref, *scratch):
    unit_ref, table_ref, sems, out_sems = scratch
    copies = move(unit_hbm, start, unit_ref, sems, 4)
    stores = []
    half = rows_ref.shape[1] // 2
    student = rows_ref[:, half:, :].reshape(-1, rows_ref.shape[2])
    d = student.shape[1]
    total = jnp.zeros((16, student.shape[0]), F32)
    for j, cols in chunks(table_ref, 4):
        copies[j].wait()
        table = jnp.exp(mm(student, unit_ref[:, cols]) * (1.0 / STUDENT_TEMP)).astype(BF16)
        table_ref[:, cols] = table
        total += mm(jnp.ones((16, table.shape[1]), BF16), table, NT)
        stores.append(store(table_ref, table_hbm, cols, out_sems.at[j]))
    sums_ref[...] = total[0:8]
    if start == 0:
        turned_ref[...] = jnp.zeros_like(turned_ref)
    else:
        eye = (
            lax.broadcasted_iota(jnp.int32, (d, d), 0)
            == lax.broadcasted_iota(jnp.int32, (d, d), 1)
        ).astype(BF16)
        turned_ref[...] = mm(eye, student, NT).astype(BF16)
    for copy in stores:
        copy.wait()


def products_body(parts, *refs):
    sums_refs = refs[:parts]
    unit_hbm, codes_hbm, left_hbm, right_hbm = refs[parts : parts + 4]
    probs_out, codes_out, unit_ref, codes_ref, probs_ref, unit_sems, codes_sems, probs_sems = refs[
        parts + 4 :
    ]
    count = 8
    width = unit_ref.shape[1] // count
    copies = []
    for j in range(count):
        cols = pl.ds(j * width, width)
        side = left_hbm if j < count // 2 else right_hbm
        side_cols = pl.ds((j % (count // 2)) * width, width)
        copies.append(
            [
                pltpu.make_async_copy(unit_hbm.at[:, cols], unit_ref.at[:, cols], unit_sems.at[j]),
                pltpu.make_async_copy(
                    codes_hbm.at[:, cols], codes_ref.at[:, cols], codes_sems.at[j]
                ),
                pltpu.make_async_copy(
                    side.at[:, side_cols], probs_ref.at[:, cols], probs_sems.at[j]
                ),
            ]
        )
        for copy in copies[-1]:
            copy.start()
    scale = 1.0 / column_sum(sums_refs)
    for j, cols in chunks(unit_ref, count):
        for copy in copies[j]:
            copy.wait()
        unit = unit_ref[:, cols]
        scaled = (unit.astype(F32) * scale[j : j + 1, :]).astype(BF16)
        probs = mm(unit, probs_ref[:, cols], NT)
        codes = mm(scaled, codes_ref[:, cols], NT)
        if j == 0:
            probs_out[...] = probs
            codes_out[...] = codes
        else:
            probs_out[...] += probs
            codes_out[...] += codes


def row_factors(first_ref, second_ref, third_ref, n):
    tile = n // LANES
    return (
        read_rows(first_ref, tile, n),
        read_rows(second_ref, tile, n),
        read_rows(third_ref, 0, n),
    )


def head_body(half, *refs):
    (place_ref, first_ref, second_ref, third_ref, *sums_refs) = refs[:-15]
    (turned_ref, inverse_ref, codes_hbm, probs_hbm, w_hbm) = refs[-15:-10]
    (keep_ref, near_ref, grad_ref, codes_ref, probs_ref, w_ref) = refs[-10:-4]
    (codes_sems, probs_sems, w_sems, _) = refs[-4:]
    count = 4
    span = probs_ref.shape[1]
    width = span // count
    copies = []
    for j in range(count):
        cols = pl.ds(j * width, width)
        here = pl.ds(half * span + j * width, width)
        copies.append(
            [
                pltpu.make_async_copy(
                    probs_hbm.at[:, cols], probs_ref.at[:, cols], probs_sems.at[j]
                ),
                pltpu.make_async_copy(
                    codes_hbm.at[:, here], codes_ref.at[:, cols], codes_sems.at[j]
                ),
                pltpu.make_async_copy(w_hbm.at[:, here], w_ref.at[:, cols], w_sems.at[j]),
            ]
        )
        for copy in copies[-1]:
            copy.start()
    n = codes_ref.shape[0]
    weights, exp_total, total = row_factors(first_ref, second_ref, third_ref, n)
    turned = turned_ref[...].astype(F32)
    left_probs = (turned * (weights / exp_total * (1.0 / STUDENT_TEMP))).astype(BF16)
    left_codes = (turned * (weights / total * (1.0 / STUDENT_TEMP))).astype(BF16)
    scale = 1.0 / column_sum(sums_refs)
    x = place_ref[1]
    core = place_ref[2]
    for j, cols in chunks(probs_ref, count):
        for copy in copies[j]:
            copy.wait()
        row = half * count + j
        head = mm(left_probs, probs_ref[:, cols]) - scale[row : row + 1, :] * mm(
            left_codes, codes_ref[:, cols]
        )
        inverse = inverse_ref[pl.ds(row, 1), :]
        unit = w_ref[:, cols].astype(F32) * inverse
        inner = jnp.sum(unit * head, axis=0, keepdims=True)
        grad = inverse * (head - unit * inner)
        grad_ref[...] = grad.reshape(grad_ref.shape)
        for k in range(keep_ref.shape[0]):
            keep_ref[k, :, cols] = grad_ref[x ^ k, core]
            near_ref[k, :, cols] = grad_ref[x ^ k, 1 - core].astype(BF16)


def pair_body(keep_ref, near_ref, own_ref, *pair_refs):
    own_ref[...] = keep_ref[0] + near_ref[0].astype(F32)
    for k, pair_ref in enumerate(pair_refs, 1):
        pair_ref[...] = (keep_ref[k] + near_ref[k].astype(F32)).astype(BF16)


def final_body(*refs):
    out_ref = refs[-1]
    count = len(refs) - 1
    each = count // 2
    span = out_ref.shape[1] // 2
    for half in range(2):
        own_ref, *far_refs = refs[half * each : (half + 1) * each]
        total = own_ref[...]
        for far_ref in far_refs:
            total = total + far_ref[...].astype(F32)
        out_ref[:, half * span : (half + 1) * span] = total


def feature_body(
    first_ref, second_ref, third_ref, probs_ref, codes_ref, turned_ref, out_ref
):
    n = codes_ref.shape[1]
    weights, exp_total, total = row_factors(first_ref, second_ref, third_ref, n)
    codes = codes_ref[...]
    probs = probs_ref[...]
    over = weights / total * (1.0 / STUDENT_TEMP)
    feature = probs * (weights / exp_total * (1.0 / STUDENT_TEMP)) - codes * over
    own = n // out_ref.shape[0]
    out_ref[:, :own, :] = feature.T.reshape(out_ref.shape[0], own, out_ref.shape[2])
    share = 1.0 / out_ref.shape[0]
    cross = jnp.sum(turned_ref[...].astype(F32) * codes, axis=0, keepdims=True)
    part = jnp.sum(weights * jnp.log(exp_total) * share - over * cross)
    count = jnp.sum(weights) * share
    tail = (out_ref.shape[0], out_ref.shape[1] - own, out_ref.shape[2])
    lane = lax.broadcasted_iota(jnp.int32, tail, 2)
    out_ref[:, own:, :] = jnp.where(lane == 0, part, jnp.where(lane == 1, count, 0.0))


def on_device(student_feats, teacher_feats, proto_weight, mask_index, row_weight):
    n_patch, n_proto = lax.axis_size("patch"), lax.axis_size("proto")
    d, protos = proto_weight.shape
    length = student_feats.shape[0]
    own = mask_index.shape[0]
    rows = own * n_proto
    chips = n_patch // 2
    share = d // n_patch
    width = protos // 8
    patch, proto = lax.axis_index("patch"), lax.axis_index("proto")
    place = jnp.stack([proto, patch // 2, patch % 2]).astype(jnp.int32)
    product = 2 * rows * d * protos

    def exchange(array, axis):
        return lax.all_to_all(array, axis, 0, 0)

    def hop(array, bits):
        return lax.ppermute(array, "patch", [(i, i ^ bits) for i in range(n_patch)])

    own_rows, x_rows, own_weights = call(
        rows_body,
        "own_rows",
        (
            shape((n_proto, 2 * own, d), BF16),
            shape((own, d), F32),
            shape((8, rows), F32),
        ),
        (place, student_feats, teacher_feats, mask_index[None, :], row_weight[None, :]),
        1 << 28,
        specs=[SMEM, HBM, HBM, HBM, HBM],
        scratch=[
            pltpu.VMEM((length, d), BF16),
            pltpu.VMEM((length, d), BF16),
            pltpu.VMEM((1, own), jnp.int32),
            pltpu.VMEM((1, own), BF16),
            pltpu.SemaphoreType.DMA((4,)),
        ],
    )
    all_rows = exchange(own_rows, "proto")
    unit, inverse = call(
        proto_body,
        "proto_unit",
        (pltpu.HBM((d, protos), BF16), shape((8, width), F32)),
        (proto_weight,),
        product,
        specs=[HBM],
        scratch=[
            pltpu.VMEM((d, protos), BF16),
            pltpu.VMEM((d, protos), BF16),
            pltpu.SemaphoreType.DMA((8,)),
            pltpu.SemaphoreType.DMA((8,)),
        ],
    )
    codes, codes_hbm, sums = call(
        table_body,
        "teacher_table",
        (shape((rows, protos), BF16), pltpu.HBM((rows, protos), BF16), shape((8, width), F32)),
        (all_rows, unit),
        2 * product,
        specs=[VMEM, HBM],
        scratch=[
            pltpu.VMEM((d, protos), BF16),
            pltpu.SemaphoreType.DMA((8,)),
            pltpu.SemaphoreType.DMA((8,)),
        ],
    )

    extras = (own_weights,)
    messages = []
    halves = []
    for sweep in range(SK_ITERS):
        sums = sums + hop(sums, 1)
        parts = [sums] + [hop(sums, 2 * k) for k in range(1, chips)]
        if sweep < 2:
            halves.append(
                call(
                    functools.partial(student_body, sweep * (protos // 2)),
                    "student_table",
                    (
                        pltpu.HBM((rows, protos // 2), BF16),
                        shape((8, rows), F32),
                        shape((d, rows), BF16),
                    ),
                    (all_rows, unit),
                    product,
                    specs=[VMEM, HBM],
                    after=(sums,),
                    scratch=[
                        pltpu.VMEM((d, protos // 2), BF16),
                        pltpu.VMEM((rows, protos // 2), BF16),
                        pltpu.SemaphoreType.DMA((4,)),
                        pltpu.SemaphoreType.DMA((4,)),
                    ],
                )
            )
        if sweep == 1:
            extras = (halves[0][1], halves[1][1])
        part = call(
            functools.partial(row_pass_body, chips),
            "row_pass",
            shape((n_proto, 8, LANES), F32),
            (*parts, codes, *extras),
            product,
            after=(halves[sweep][1],) if sweep == 0 else (),
        )
        messages.append(exchange(part, "proto"))
        if sweep < SK_ITERS - 1:
            sums = call(
                col_pass_body,
                "col_pass",
                shape((8, width), F32),
                (messages[-1], codes),
                product // 2,
            )

    turned = halves[1][2]
    probs_feature, codes_feature = call(
        functools.partial(products_body, chips),
        "features",
        (shape((d, rows), F32), shape((d, rows), F32)),
        (*parts, unit, codes_hbm, halves[0][0], halves[1][0]),
        3 * product,
        specs=[VMEM] * chips + [HBM] * 4,
        after=(part,),
        scratch=[
            pltpu.VMEM((d, protos), BF16),
            pltpu.VMEM((rows, protos), BF16),
            pltpu.VMEM((rows, protos), BF16),
            pltpu.SemaphoreType.DMA((8,)),
            pltpu.SemaphoreType.DMA((8,)),
            pltpu.SemaphoreType.DMA((8,)),
        ],
        limit=2 * VMEM_LIMIT,
    )
    heads = []
    for half in range(2):
        heads.append(
            call(
                functools.partial(head_body, half),
                "head",
                (
                    shape((chips, share, protos // 2), F32),
                    shape((chips, share, protos // 2), BF16),
                ),
                (
                    place,
                    *messages,
                    *parts,
                    turned,
                    inverse,
                    codes_hbm,
                    halves[half][0],
                    proto_weight,
                ),
                2 * product,
                specs=[SMEM] + [VMEM] * (len(messages) + chips + 2) + [HBM] * 3,
                after=(heads[-1][1] if heads else codes_feature,),
                scratch=[
                    pltpu.VMEM((chips, 2, share, width), F32),
                    pltpu.VMEM((rows, protos // 2), BF16),
                    pltpu.VMEM((rows, protos // 2), BF16),
                    pltpu.VMEM((d, protos // 2), BF16),
                    pltpu.SemaphoreType.DMA((4,)),
                    pltpu.SemaphoreType.DMA((4,)),
                    pltpu.SemaphoreType.DMA((4,)),
                    pltpu.VMEM((8, LANES), F32),
                ],
            )
        )
    blocks = []
    feature_part = None
    for keep, near in heads:
        own_block, *pairs = call(
            pair_body,
            "pair_sums",
            (shape((share, protos // 2), F32),)
            + tuple(shape((share, protos // 2), BF16) for _ in range(chips - 1)),
            (keep, hop(near, 1)),
            0,
            after=() if feature_part is None else (feature_part,),
        )
        blocks += [own_block] + [hop(pair, 2 * (k + 1)) for k, pair in enumerate(pairs)]
        if feature_part is None:
            feature_part = call(
                feature_body,
                "feature",
                shape((n_proto, own + 8, d), F32),
                (*messages, probs_feature, codes_feature, turned),
                0,
                after=(own_block,),
            )
    sent = jnp.sum(exchange(feature_part, "proto"), axis=0)
    feature, tail = sent[:own], sent[own:, :LANES]
    tails = jnp.broadcast_to(tail[None], (n_patch, 8, LANES))
    grad_proto = call(
        final_body,
        "assemble",
        shape((share, protos), F32),
        tuple(blocks),
        0,
        after=(tails,),
    )
    losses = jnp.sum(exchange(tails, "patch"), axis=0)
    loss = losses[0, 0] / losses[0, 1]

    inverse_student = lax.rsqrt(jnp.sum(x_rows * x_rows, axis=1, keepdims=True) + EPS)
    unit_student = x_rows * inverse_student
    grad_student = inverse_student * (
        feature - unit_student * jnp.sum(unit_student * feature, axis=1, keepdims=True)
    )
    return (grad_student, grad_proto, loss)


def solution(mesh):
    both = ("patch", "proto")
    in_specs = (P(both, None), P(both, None), P(None, "proto"), P(both), P(both))
    out_specs = (P(both, None), P("patch", "proto"), P())
    return jax.shard_map(
        on_device, mesh=mesh, in_specs=in_specs, out_specs=out_specs, check_vma=False
    )
```

```python
import functools

import jax
import jax.numpy as jnp
from jax import lax
from jax.experimental import pallas as pl
from jax.experimental.pallas import tpu as pltpu
from jax.sharding import PartitionSpec as P

SK_ITERS = 3
EPS = 1e-06
TEACHER_TEMP = 0.07
STUDENT_TEMP = 0.1
F32 = jnp.float32
BF16 = jnp.bfloat16
LANES = 128
PIECES = (3, 3, 2)
VMEM_LIMIT = 20 * 1024 * 1024

NN = (((1,), (0,)), ((), ()))
NT = (((1,), (1,)), ((), ()))
TN = (((0,), (0,)), ((), ()))
SMEM = pl.BlockSpec(memory_space=pltpu.SMEM)
VMEM = pl.BlockSpec(memory_space=pltpu.VMEM)
ANY = pl.BlockSpec(memory_space=pl.ANY)
HBM = pl.BlockSpec(memory_space=pltpu.HBM)


def mm(a, b, dims=NN):
    return lax.dot_general(a, b, dims, preferred_element_type=F32)


def shape(dims, dtype):
    return jax.ShapeDtypeStruct(dims, dtype)


def call(body, name, out_shape, args, flops, specs=None, after=(), scratch=(), limit=VMEM_LIMIT):
    specs = specs or [VMEM] * len(args)
    skip = len(after)
    args = [
        pltpu.with_memory_space_constraint(arg, pltpu.HBM) if spec is HBM else arg
        for arg, spec in zip(args, specs)
    ]

    def ordered(*refs):
        body(*refs[skip:])

    def out_spec(out):
        return VMEM if isinstance(out, jax.ShapeDtypeStruct) else HBM

    many = isinstance(out_shape, tuple)
    return pl.pallas_call(
        ordered,
        name=name,
        out_shape=out_shape,
        in_specs=[ANY] * skip + specs,
        out_specs=tuple(map(out_spec, out_shape)) if many else out_spec(out_shape),
        scratch_shapes=list(scratch),
        compiler_params=pltpu.CompilerParams(vmem_limit_bytes=limit),
        cost_estimate=pl.CostEstimate(flops=flops, bytes_accessed=1 << 16, transcendentals=0),
    )(*after, *args)


def three_terms(row):
    high = row.astype(BF16).astype(F32)
    rest = row - high
    mid = rest.astype(BF16).astype(F32)
    low = rest - mid
    index = lax.broadcasted_iota(jnp.int32, (16, row.shape[1]), 0)
    terms = jnp.where(
        index == 0, high, jnp.where(index == 1, mid, jnp.where(index == 2, low, 0.0))
    )
    return terms.astype(BF16)


def column_sum(refs):
    total = refs[0][...]
    for ref in refs[1:]:
        total = total + ref[...]
    return total


def chunks(table_ref, count=8):
    width = table_ref.shape[1] // count
    return [(j, pl.ds(j * width, width)) for j in range(count)]


def move(source, start, target, sems, count):
    width = target.shape[1] // count
    copies = [
        pltpu.make_async_copy(
            source.at[:, pl.ds(start + j * width, width)],
            target.at[:, pl.ds(j * width, width)],
            sems.at[j],
        )
        for j in range(count)
    ]
    for copy in copies:
        copy.start()
    return copies


def store(source, target, cols, sem):
    copy = pltpu.make_async_copy(source.at[:, cols], target.at[:, cols], sem)
    copy.start()
    return copy


def read_rows(message_ref, start, n):
    total = jnp.sum(message_ref[...], axis=0)
    pieces = [total[start + k : start + k + 1, :] for k in range(n // LANES)]
    return jnp.concatenate(pieces, axis=1)


def write_rows(message_ref, start, row):
    count = message_ref.shape[0]
    for k in range(row.shape[1] // LANES):
        piece = row[:, k * LANES : (k + 1) * LANES]
        message_ref[:, start + k, :] = jnp.broadcast_to(piece, (count, LANES))


def rows_body(
    place_ref,
    student_hbm,
    teacher_hbm,
    index_hbm,
    weight_hbm,
    rows_ref,
    x_ref,
    w_ref,
    student_ref,
    teacher_ref,
    index_ref,
    weight_ref,
    sems,
):
    copies = [
        pltpu.make_async_copy(index_hbm, index_ref, sems.at[0]),
        pltpu.make_async_copy(teacher_hbm, teacher_ref, sems.at[1]),
        pltpu.make_async_copy(student_hbm, student_ref, sems.at[2]),
        pltpu.make_async_copy(weight_hbm, weight_ref, sems.at[3]),
    ]
    for copy in copies:
        copy.start()
    for copy in copies:
        copy.wait()
    picks = index_ref[...]
    length = student_ref.shape[0]
    count = picks.shape[1]
    one_hot = (lax.broadcasted_iota(jnp.int32, (length, count), 0) == picks).astype(BF16)
    x = mm(one_hot, student_ref[...], TN)
    y = mm(one_hot, teacher_ref[...], TN)
    x_ref[...] = x
    unit_x = x * lax.rsqrt(jnp.sum(x * x, axis=1, keepdims=True) + EPS)
    unit_y = y * lax.rsqrt(jnp.sum(y * y, axis=1, keepdims=True) + EPS)
    both = jnp.concatenate([unit_y.astype(BF16), unit_x.astype(BF16)], axis=0)
    rows_ref[...] = jnp.broadcast_to(both[None], rows_ref.shape)
    lanes = w_ref.shape[1]
    spot = lax.broadcasted_iota(jnp.int32, (count, lanes), 1) - place_ref[0] * count
    spread = (spot == lax.broadcasted_iota(jnp.int32, (count, lanes), 0)).astype(BF16)
    w_ref[...] = jnp.broadcast_to(mm(weight_ref[...], spread), w_ref.shape)


def proto_body(w_hbm, unit_hbm, inverse_ref, w_ref, unit_ref, in_sems, out_sems):
    copies = move(w_hbm, 0, w_ref, in_sems, 8)
    stores = []
    for j, cols in chunks(w_ref):
        copies[j].wait()
        w = w_ref[:, cols].astype(F32)
        inverse = lax.rsqrt(jnp.sum(w * w, axis=0, keepdims=True) + EPS)
        inverse_ref[pl.ds(j, 1), :] = inverse
        unit_ref[:, cols] = (w * inverse).astype(BF16)
        stores.append(store(unit_ref, unit_hbm, cols, out_sems.at[j]))
    for copy in stores:
        copy.wait()


def table_body(rows_ref, unit_hbm, table_ref, sums_ref, unit_ref, sems):
    copies = move(unit_hbm, 0, unit_ref, sems, 8)
    half = rows_ref.shape[1] // 2
    teacher = rows_ref[:, :half, :].reshape(-1, rows_ref.shape[2])
    for j, cols in chunks(table_ref):
        copies[j].wait()
        table = jnp.exp(mm(teacher, unit_ref[:, cols]) * (1.0 / TEACHER_TEMP)).astype(BF16)
        table_ref[:, cols] = table
        sums_ref[pl.ds(j, 1), :] = jnp.sum(table.astype(F32), axis=0, keepdims=True)


def row_pass_body(parts, *refs):
    sums_refs, table_ref, extra_refs, out_ref = refs[:parts], refs[parts], refs[parts + 1 : -1], refs[-1]
    scale = 1.0 / column_sum(sums_refs)
    n = table_ref.shape[0]
    total = jnp.zeros((16, n), F32)
    for j, cols in chunks(table_ref):
        total += mm(three_terms(scale[j : j + 1, :]), table_ref[:, cols], NT)
    write_rows(out_ref, 0, jnp.sum(total, axis=0, keepdims=True))
    write_rows(out_ref, n // LANES, column_sum(extra_refs)[0:1, :])


def col_pass_body(message_ref, table_ref, out_ref):
    terms = three_terms(1.0 / read_rows(message_ref, 0, table_ref.shape[0]))
    for j, cols in chunks(table_ref):
        out_ref[pl.ds(j, 1), :] = jnp.sum(mm(terms, table_ref[:, cols]), axis=0, keepdims=True)


def student_body(first, rows_ref, unit_hbm, table_ref, sums_ref, feature_ref, *refs):
    unit_ref, sems = refs[-2:]
    count = PIECES[first]
    width = table_ref.shape[1] // count
    copies = move(unit_hbm, sum(PIECES[:first]) * width, unit_ref, sems, count)
    half = rows_ref.shape[1] // 2
    student = rows_ref[:, half:, :].reshape(-1, rows_ref.shape[2])
    total = jnp.zeros((16, student.shape[0]), F32)
    for j, cols in chunks(table_ref, count):
        copies[j].wait()
        unit = unit_ref[:, cols]
        table = jnp.exp(mm(student, unit) * (1.0 / STUDENT_TEMP)).astype(BF16)
        table_ref[:, cols] = table
        total += mm(jnp.ones((16, table.shape[1]), BF16), table, NT)
        part = mm(unit, table, NT)
        if j == 0:
            feature_ref[...] = part
        else:
            feature_ref[...] += part
    sums_ref[...] = total[0:8]
    if len(refs) > 2:
        d = student.shape[1]
        eye = (
            lax.broadcasted_iota(jnp.int32, (d, d), 0)
            == lax.broadcasted_iota(jnp.int32, (d, d), 1)
        ).astype(BF16)
        refs[0][...] = mm(eye, student, NT).astype(BF16)


def codes_feature_body(*refs):
    *sums_refs, table_ref, unit_hbm, feature_ref, unit_ref, sems = refs
    copies = move(unit_hbm, 0, unit_ref, sems, 8)
    scale = 1.0 / column_sum(sums_refs)
    for j, cols in chunks(table_ref):
        copies[j].wait()
        scaled = (unit_ref[:, cols].astype(F32) * scale[j : j + 1, :]).astype(BF16)
        part = mm(scaled, table_ref[:, cols], NT)
        if j == 0:
            feature_ref[...] = part
        else:
            feature_ref[...] += part


def row_factors(first_ref, last_ref, n):
    tile = n // LANES
    return read_rows(first_ref, tile, n), read_rows(last_ref, tile, n), read_rows(last_ref, 0, n)


def head_body(parts, *refs):
    place_ref, first_ref, last_ref = refs[:3]
    sums_refs = refs[3 : 3 + parts]
    turned_ref, inverse_ref, codes_ref, *piece_refs, w_hbm = refs[3 + parts : -6]
    own_ref, keep_ref, near_ref, turn_ref, w_ref, sems = refs[-6:]
    x, core = place_ref[1], place_ref[2]
    chips = near_ref.shape[0]
    share = near_ref.shape[1]
    protos = codes_ref.shape[1]
    count = 8
    width = protos // count
    spots = []
    for k in range(chips):
        spots += [2 * (x ^ k) + core, 2 * (x ^ k) + 1 - core]
    copies = []
    for j in range(count):
        copies.append([])
        for m, spot in enumerate(spots):
            copy = pltpu.make_async_copy(
                w_hbm.at[pl.ds(pl.multiple_of(spot * share, share), share), pl.ds(j * width, width)],
                w_ref.at[pl.ds(m * share, share), pl.ds(j * width, width)],
                sems.at[j, m],
            )
            copy.start()
            copies[j].append(copy)
    for m, spot in enumerate(spots):
        turn_ref[pl.ds(m * share, share), :] = turned_ref[
            pl.ds(pl.multiple_of(spot * share, share), share), :
        ]
    weights, exp_total, total = row_factors(first_ref, last_ref, codes_ref.shape[0])
    turned = turn_ref[...].astype(F32)
    left_probs = (turned * (weights / exp_total * (1.0 / STUDENT_TEMP))).astype(BF16)
    left_codes = (turned * (weights / total * (1.0 / STUDENT_TEMP))).astype(BF16)
    scale = 1.0 / column_sum(sums_refs)
    piece, at = 0, 0
    for j, cols in chunks(codes_ref, count):
        probs = piece_refs[piece][:, pl.ds(at * width, width)]
        at += 1
        if at == PIECES[piece]:
            piece, at = piece + 1, 0
        head = mm(left_probs, probs) - scale[j : j + 1, :] * mm(left_codes, codes_ref[:, cols])
        for copy in copies[j]:
            copy.wait()
        inverse = inverse_ref[pl.ds(j, 1), :]
        unit = w_ref[:, cols].astype(F32) * inverse
        inner = jnp.sum(unit * head, axis=0, keepdims=True)
        grad = inverse * (head - unit * inner)
        own_ref[:, cols] = grad[0:share]
        for k in range(chips):
            low = 2 * k * share
            if k:
                keep_ref[k - 1, :, cols] = grad[low : low + share]
            near_ref[k, :, cols] = grad[low + share : low + 2 * share].astype(BF16)


def pair_body(own_ref, keep_ref, near_ref, out_ref, *pair_refs):
    out_ref[...] = own_ref[...] + near_ref[0].astype(F32)
    for k, pair_ref in enumerate(pair_refs):
        pair_ref[...] = (keep_ref[k] + near_ref[k + 1].astype(F32)).astype(BF16)


def final_body(own_ref, *refs):
    *far_refs, out_ref = refs
    total = own_ref[...]
    for far_ref in far_refs:
        total = total + far_ref[...].astype(F32)
    out_ref[...] = total


def owner_body(sent_ref, x_ref, grad_ref, tail_ref):
    sent = jnp.sum(sent_ref[...], axis=0)
    own = x_ref.shape[0]
    x = x_ref[...]
    feature = sent[:own]
    inverse = lax.rsqrt(jnp.sum(x * x, axis=1, keepdims=True) + EPS)
    unit = x * inverse
    grad_ref[...] = inverse * (feature - unit * jnp.sum(unit * feature, axis=1, keepdims=True))
    tail_ref[...] = jnp.broadcast_to(sent[own:, :LANES][None], tail_ref.shape)


def feature_body(first_ref, last_ref, codes_ref, turned_ref, *refs):
    *probs_refs, out_ref = refs
    n = codes_ref.shape[1]
    weights, exp_total, total = row_factors(first_ref, last_ref, n)
    codes = codes_ref[...]
    probs = column_sum(probs_refs)
    over = weights / total * (1.0 / STUDENT_TEMP)
    feature = probs * (weights / exp_total * (1.0 / STUDENT_TEMP)) - codes * over
    own = n // out_ref.shape[0]
    out_ref[:, :own, :] = feature.T.reshape(out_ref.shape[0], own, out_ref.shape[2])
    share = 1.0 / out_ref.shape[0]
    cross = jnp.sum(turned_ref[...].astype(F32) * codes, axis=0, keepdims=True)
    part = jnp.sum(weights * jnp.log(exp_total) * share - over * cross)
    count = jnp.sum(weights) * share
    tail = (out_ref.shape[0], out_ref.shape[1] - own, out_ref.shape[2])
    lane = lax.broadcasted_iota(jnp.int32, tail, 2)
    out_ref[:, own:, :] = jnp.where(lane == 0, part, jnp.where(lane == 1, count, 0.0))


def on_device(student_feats, teacher_feats, proto_weight, mask_index, row_weight):
    n_patch, n_proto = lax.axis_size("patch"), lax.axis_size("proto")
    d, protos = proto_weight.shape
    length = student_feats.shape[0]
    own = mask_index.shape[0]
    rows = own * n_proto
    chips = n_patch // 2
    share = d // n_patch
    width = protos // 8
    patch, proto = lax.axis_index("patch"), lax.axis_index("proto")
    place = jnp.stack([proto, patch // 2, patch % 2]).astype(jnp.int32)
    product = 2 * rows * d * protos

    def exchange(array, axis):
        return lax.all_to_all(array, axis, 0, 0)

    def hop(array, bits):
        return lax.ppermute(array, "patch", [(i, i ^ bits) for i in range(n_patch)])

    own_rows, x_rows, own_weights = call(
        rows_body,
        "own_rows",
        (
            shape((n_proto, 2 * own, d), BF16),
            shape((own, d), F32),
            shape((8, rows), F32),
        ),
        (place, student_feats, teacher_feats, mask_index[None, :], row_weight[None, :]),
        1 << 28,
        specs=[SMEM, HBM, HBM, HBM, HBM],
        scratch=[
            pltpu.VMEM((length, d), BF16),
            pltpu.VMEM((length, d), BF16),
            pltpu.VMEM((1, own), jnp.int32),
            pltpu.VMEM((1, own), BF16),
            pltpu.SemaphoreType.DMA((4,)),
        ],
    )
    all_rows = exchange(own_rows, "proto")
    unit, inverse = call(
        proto_body,
        "proto_unit",
        (pltpu.HBM((d, protos), BF16), shape((8, width), F32)),
        (proto_weight,),
        product,
        specs=[HBM],
        scratch=[
            pltpu.VMEM((d, protos), BF16),
            pltpu.VMEM((d, protos), BF16),
            pltpu.SemaphoreType.DMA((8,)),
            pltpu.SemaphoreType.DMA((8,)),
        ],
    )
    codes, sums = call(
        table_body,
        "teacher_table",
        (shape((rows, protos), BF16), shape((8, width), F32)),
        (all_rows, unit),
        2 * product,
        specs=[VMEM, HBM],
        scratch=[pltpu.VMEM((d, protos), BF16), pltpu.SemaphoreType.DMA((8,))],
    )

    messages = []
    pieces = []
    for sweep in range(SK_ITERS):
        sums = sums + hop(sums, 1)
        parts = [sums] + [hop(sums, 2 * k) for k in range(1, chips)]
        span = PIECES[sweep] * width
        last = sweep == SK_ITERS - 1
        pieces.append(
            call(
                functools.partial(student_body, sweep),
                "student_table",
                (shape((rows, span), BF16), shape((8, rows), F32), shape((d, rows), F32))
                + ((shape((d, rows), BF16),) if last else ()),
                (all_rows, unit),
                product,
                specs=[VMEM, HBM],
                after=(sums,),
                scratch=[pltpu.VMEM((d, span), BF16), pltpu.SemaphoreType.DMA((PIECES[sweep],))],
            )
        )
        part = call(
            functools.partial(row_pass_body, chips),
            "row_pass",
            shape((n_proto, 8, LANES), F32),
            (*parts, codes, *([piece[1] for piece in pieces] if last else [own_weights])),
            product,
            after=() if last else (pieces[-1][1],),
        )
        messages.append(exchange(part, "proto"))
        if not last:
            sums = call(
                col_pass_body,
                "col_pass",
                shape((8, width), F32),
                (messages[-1], codes),
                product // 2,
            )

    turned = pieces[-1][3]
    factors = (messages[0], messages[-1])
    own_block, keep, near = call(
        functools.partial(head_body, chips),
        "head",
        (
            shape((share, protos), F32),
            shape((chips - 1, share, protos), F32),
            shape((chips, share, protos), BF16),
        ),
        (
            place,
            *factors,
            *parts,
            turned,
            inverse,
            codes,
            *[piece[0] for piece in pieces],
            proto_weight,
        ),
        4 * product,
        specs=[SMEM] + [VMEM] * (len(factors) + chips + 3 + len(pieces)) + [HBM],
        scratch=[
            pltpu.VMEM((d, rows), BF16),
            pltpu.VMEM((d, protos), BF16),
            pltpu.SemaphoreType.DMA((8, n_patch)),
        ],
    )
    codes_feature = call(
        codes_feature_body,
        "codes_feature",
        shape((d, rows), F32),
        (*parts, codes, unit),
        product,
        specs=[VMEM] * (chips + 1) + [HBM],
        after=(own_block,),
        scratch=[pltpu.VMEM((d, protos), BF16), pltpu.SemaphoreType.DMA((8,))],
    )
    own_block, *pairs = call(
        pair_body,
        "pair_sums",
        (shape((share, protos), F32),)
        + tuple(shape((share, protos), BF16) for _ in range(chips - 1)),
        (own_block, keep, hop(near, 1)),
        product // 4,
        after=(codes_feature,),
    )
    far = [hop(pair, 2 * (k + 1)) for k, pair in enumerate(pairs)]
    feature_part = call(
        feature_body,
        "feature",
        shape((n_proto, own + 8, d), F32),
        (*factors, codes_feature, turned, *[piece[2] for piece in pieces]),
        product // 4,
        after=(own_block,),
    )
    grad_student, tails = call(
        owner_body,
        "owner",
        (shape((own, d), F32), shape((n_patch, 8, LANES), F32)),
        (exchange(feature_part, "proto"), x_rows),
        product // 8,
    )
    grad_proto = call(
        final_body,
        "assemble",
        shape((share, protos), F32),
        (own_block, *far),
        product // 4,
        after=(tails,),
    )
    losses = jnp.sum(exchange(tails, "patch"), axis=0)
    return (grad_student, grad_proto, losses[0, 0] / losses[0, 1])


def solution(mesh):
    both = ("patch", "proto")
    in_specs = (P(both, None), P(both, None), P(None, "proto"), P(both), P(both))
    out_specs = (P(both, None), P("patch", "proto"), P())
    return jax.shard_map(
        on_device, mesh=mesh, in_specs=in_specs, out_specs=out_specs, check_vma=False
    )
```

```python
import functools

import jax
import jax.numpy as jnp
from jax import lax
from jax.experimental import pallas as pl
from jax.experimental.pallas import tpu as pltpu
from jax.sharding import PartitionSpec as P

SK_ITERS = 3
EPS = 1e-06
TEACHER_TEMP = 0.07
STUDENT_TEMP = 0.1
F32 = jnp.float32
BF16 = jnp.bfloat16
LANES = 128
PIECES = (3, 3, 2)
PARTS = (3, 5)
VMEM_LIMIT = 20 * 1024 * 1024

NN = (((1,), (0,)), ((), ()))
NT = (((1,), (1,)), ((), ()))
TN = (((0,), (0,)), ((), ()))
SMEM = pl.BlockSpec(memory_space=pltpu.SMEM)
VMEM = pl.BlockSpec(memory_space=pltpu.VMEM)
ANY = pl.BlockSpec(memory_space=pl.ANY)
HBM = pl.BlockSpec(memory_space=pltpu.HBM)


def mm(a, b, dims=NN):
    return lax.dot_general(a, b, dims, preferred_element_type=F32)


def shape(dims, dtype):
    return jax.ShapeDtypeStruct(dims, dtype)


def call(body, name, out_shape, args, flops, specs=None, after=(), scratch=(), limit=VMEM_LIMIT):
    specs = specs or [VMEM] * len(args)
    skip = len(after)
    args = [
        pltpu.with_memory_space_constraint(arg, pltpu.HBM) if spec is HBM else arg
        for arg, spec in zip(args, specs)
    ]

    def ordered(*refs):
        body(*refs[skip:])

    def out_spec(out):
        return VMEM if isinstance(out, jax.ShapeDtypeStruct) else HBM

    many = isinstance(out_shape, tuple)
    return pl.pallas_call(
        ordered,
        name=name,
        out_shape=out_shape,
        in_specs=[ANY] * skip + specs,
        out_specs=tuple(map(out_spec, out_shape)) if many else out_spec(out_shape),
        scratch_shapes=list(scratch),
        compiler_params=pltpu.CompilerParams(vmem_limit_bytes=limit),
        cost_estimate=pl.CostEstimate(flops=flops, bytes_accessed=1 << 16, transcendentals=0),
    )(*after, *args)


def three_terms(row):
    high = row.astype(BF16).astype(F32)
    rest = row - high
    mid = rest.astype(BF16).astype(F32)
    low = rest - mid
    index = lax.broadcasted_iota(jnp.int32, (16, row.shape[1]), 0)
    terms = jnp.where(
        index == 0, high, jnp.where(index == 1, mid, jnp.where(index == 2, low, 0.0))
    )
    return terms.astype(BF16)


def column_sum(refs):
    total = refs[0][...]
    for ref in refs[1:]:
        total = total + ref[...]
    return total


def chunks(table_ref, count=8):
    width = table_ref.shape[1] // count
    return [(j, pl.ds(j * width, width)) for j in range(count)]


def move(source, target, sems, count):
    width = target.shape[1] // count
    copies = [
        pltpu.make_async_copy(
            source.at[:, pl.ds(j * width, width)],
            target.at[:, pl.ds(j * width, width)],
            sems.at[j],
        )
        for j in range(count)
    ]
    for copy in copies[:2]:
        copy.start()
    return copies


def arrive(copies, j):
    copies[j].wait()
    if j + 2 < len(copies):
        copies[j + 2].start()


def store(source, target, cols, sem):
    copy = pltpu.make_async_copy(source.at[:, cols], target.at[:, cols], sem)
    copy.start()
    return copy


def read_rows(message_ref, start, n):
    total = jnp.sum(message_ref[...], axis=0)
    pieces = [total[start + k : start + k + 1, :] for k in range(n // LANES)]
    return jnp.concatenate(pieces, axis=1)


def write_rows(message_ref, start, row):
    count = message_ref.shape[0]
    for k in range(row.shape[1] // LANES):
        piece = row[:, k * LANES : (k + 1) * LANES]
        message_ref[:, start + k, :] = jnp.broadcast_to(piece, (count, LANES))


def rows_body(
    place_ref,
    student_hbm,
    teacher_hbm,
    index_hbm,
    weight_hbm,
    rows_ref,
    x_ref,
    w_ref,
    student_ref,
    teacher_ref,
    index_ref,
    weight_ref,
    sems,
):
    copies = [
        pltpu.make_async_copy(index_hbm, index_ref, sems.at[0]),
        pltpu.make_async_copy(teacher_hbm, teacher_ref, sems.at[1]),
        pltpu.make_async_copy(student_hbm, student_ref, sems.at[2]),
        pltpu.make_async_copy(weight_hbm, weight_ref, sems.at[3]),
    ]
    for copy in copies:
        copy.start()
    for copy in copies:
        copy.wait()
    picks = index_ref[...]
    length = student_ref.shape[0]
    count = picks.shape[1]
    one_hot = (lax.broadcasted_iota(jnp.int32, (length, count), 0) == picks).astype(BF16)
    x = mm(one_hot, student_ref[...], TN)
    y = mm(one_hot, teacher_ref[...], TN)
    x_ref[...] = x
    unit_x = x * lax.rsqrt(jnp.sum(x * x, axis=1, keepdims=True) + EPS)
    unit_y = y * lax.rsqrt(jnp.sum(y * y, axis=1, keepdims=True) + EPS)
    both = jnp.concatenate([unit_y.astype(BF16), unit_x.astype(BF16)], axis=0)
    rows_ref[...] = jnp.broadcast_to(both[None], rows_ref.shape)
    lanes = w_ref.shape[1]
    spot = lax.broadcasted_iota(jnp.int32, (count, lanes), 1) - place_ref[0] * count
    spread = (spot == lax.broadcasted_iota(jnp.int32, (count, lanes), 0)).astype(BF16)
    w_ref[...] = jnp.broadcast_to(mm(weight_ref[...], spread), w_ref.shape)


def proto_body(w_hbm, unit_hbm, inverse_ref, w_ref, unit_ref, in_sems, out_sems):
    copies = move(w_hbm, w_ref, in_sems, 8)
    stores = []
    for j, cols in chunks(w_ref):
        arrive(copies, j)
        w = w_ref[:, cols].astype(F32)
        inverse = lax.rsqrt(jnp.sum(w * w, axis=0, keepdims=True) + EPS)
        inverse_ref[pl.ds(j, 1), :] = inverse
        unit_ref[:, cols] = (w * inverse).astype(BF16)
        stores.append(store(unit_ref, unit_hbm, cols, out_sems.at[j]))
    for copy in stores:
        copy.wait()


def table_body(rows_ref, unit_hbm, table_ref, sums_ref, unit_ref, sems):
    copies = move(unit_hbm, unit_ref, sems, 8)
    half = rows_ref.shape[1] // 2
    teacher = rows_ref[:, :half, :].reshape(-1, rows_ref.shape[2])
    for j, cols in chunks(table_ref):
        arrive(copies, j)
        table = jnp.exp(mm(teacher, unit_ref[:, cols]) * (1.0 / TEACHER_TEMP)).astype(BF16)
        table_ref[:, cols] = table
        sums_ref[pl.ds(j, 1), :] = jnp.sum(table.astype(F32), axis=0, keepdims=True)


def row_pass_body(parts, *refs):
    sums_refs, table_ref, extra_refs, out_ref = refs[:parts], refs[parts], refs[parts + 1 : -1], refs[-1]
    scale = 1.0 / column_sum(sums_refs)
    n = table_ref.shape[0]
    total = jnp.zeros((16, n), F32)
    for j, cols in chunks(table_ref):
        total += mm(three_terms(scale[j : j + 1, :]), table_ref[:, cols], NT)
    write_rows(out_ref, 0, jnp.sum(total, axis=0, keepdims=True))
    write_rows(out_ref, n // LANES, column_sum(extra_refs)[0:1, :])


def col_pass_body(message_ref, table_ref, out_ref):
    terms = three_terms(1.0 / read_rows(message_ref, 0, table_ref.shape[0]))
    for j, cols in chunks(table_ref):
        out_ref[pl.ds(j, 1), :] = jnp.sum(mm(terms, table_ref[:, cols]), axis=0, keepdims=True)


def student_body(first, rows_ref, unit_ref, table_ref, sums_ref, feature_ref, *turned_refs):
    count = PIECES[first]
    width = table_ref.shape[1] // count
    start = sum(PIECES[:first]) * width
    half = rows_ref.shape[1] // 2
    student = rows_ref[:, half:, :].reshape(-1, rows_ref.shape[2])
    total = jnp.zeros((16, student.shape[0]), F32)
    for j, cols in chunks(table_ref, count):
        unit = unit_ref[:, pl.ds(start + j * width, width)]
        table = jnp.exp(mm(student, unit) * (1.0 / STUDENT_TEMP)).astype(BF16)
        table_ref[:, cols] = table
        total += mm(jnp.ones((16, table.shape[1]), BF16), table, NT)
        part = mm(unit, table, NT)
        if j == 0:
            feature_ref[...] = part
        else:
            feature_ref[...] += part
    sums_ref[...] = total[0:8]
    for turned_ref in turned_refs:
        d = student.shape[1]
        eye = (
            lax.broadcasted_iota(jnp.int32, (d, d), 0)
            == lax.broadcasted_iota(jnp.int32, (d, d), 1)
        ).astype(BF16)
        turned_ref[...] = mm(eye, student, NT).astype(BF16)


def codes_feature_body(*refs):
    *sums_refs, table_ref, unit_ref, feature_ref = refs
    scale = 1.0 / column_sum(sums_refs)
    for j, cols in chunks(table_ref):
        scaled = (unit_ref[:, cols].astype(F32) * scale[j : j + 1, :]).astype(BF16)
        part = mm(scaled, table_ref[:, cols], NT)
        if j == 0:
            feature_ref[...] = part
        else:
            feature_ref[...] += part


def row_factors(first_ref, last_ref, n):
    tile = n // LANES
    return read_rows(first_ref, tile, n), read_rows(last_ref, tile, n), read_rows(last_ref, 0, n)


def head_body(first, count, parts, *refs):
    place_ref, first_ref, last_ref = refs[:3]
    sums_refs = refs[3 : 3 + parts]
    turned_ref, inverse_ref, codes_ref, *piece_refs, w_ref = refs[3 + parts : -4]
    own_ref, keep_ref, near_ref, turn_ref = refs[-4:]
    x, core = place_ref[1], place_ref[2]
    chips, share, span = near_ref.shape
    width = span // count
    spots = []
    for k in range(chips):
        for side in (core, 1 - core):
            spots.append(pl.ds(pl.multiple_of((2 * (x ^ k) + side) * share, share), share))
    for m, spot in enumerate(spots):
        turn_ref[pl.ds(m * share, share), :] = turned_ref[spot, :]
    weights, exp_total, total = row_factors(first_ref, last_ref, codes_ref.shape[0])
    turned = turn_ref[...].astype(F32)
    left_probs = (turned * (weights / exp_total * (1.0 / STUDENT_TEMP))).astype(BF16)
    left_codes = (turned * (weights / total * (1.0 / STUDENT_TEMP))).astype(BF16)
    scale = 1.0 / column_sum(sums_refs)
    where = [(p, at) for p, size in enumerate(PIECES) for at in range(size)]
    for j, cols in chunks(own_ref, count):
        row = first + j
        here = pl.ds(row * width, width)
        piece, at = where[row]
        head = mm(left_probs, piece_refs[piece][:, pl.ds(at * width, width)]) - scale[
            row : row + 1, :
        ] * mm(left_codes, codes_ref[:, here])
        inverse = inverse_ref[pl.ds(row, 1), :]
        w = jnp.concatenate([w_ref[spot, here] for spot in spots], axis=0)
        unit = w.astype(F32) * inverse
        inner = jnp.sum(unit * head, axis=0, keepdims=True)
        grad = inverse * (head - unit * inner)
        own_ref[:, cols] = grad[0:share]
        for k in range(chips):
            low = 2 * k * share
            if k:
                keep_ref[k - 1, :, cols] = grad[low : low + share]
            near_ref[k, :, cols] = grad[low + share : low + 2 * share].astype(BF16)


def pair_body(own_ref, keep_ref, near_ref, out_ref, *pair_refs):
    out_ref[...] = own_ref[...] + near_ref[0].astype(F32)
    for k, pair_ref in enumerate(pair_refs):
        pair_ref[...] = (keep_ref[k] + near_ref[k + 1].astype(F32)).astype(BF16)


def left_body(*refs):
    own_ref, *far_refs, out_ref = refs
    total = own_ref[...]
    for far_ref in far_refs:
        total = total + far_ref[...].astype(F32)
    out_ref[...] = total


def final_body(left_ref, own_ref, *refs):
    *far_refs, out_ref = refs
    span = left_ref.shape[1]
    total = own_ref[...]
    for far_ref in far_refs:
        total = total + far_ref[...].astype(F32)
    out_ref[:, :span] = left_ref[...]
    out_ref[:, span:] = total


def owner_body(sent_ref, x_ref, grad_ref, tail_ref):
    sent = jnp.sum(sent_ref[...], axis=0)
    own = x_ref.shape[0]
    x = x_ref[...]
    feature = sent[:own]
    inverse = lax.rsqrt(jnp.sum(x * x, axis=1, keepdims=True) + EPS)
    unit = x * inverse
    grad_ref[...] = inverse * (feature - unit * jnp.sum(unit * feature, axis=1, keepdims=True))
    tail_ref[...] = jnp.broadcast_to(sent[own:, :LANES][None], tail_ref.shape)


def feature_body(first_ref, last_ref, codes_ref, turned_ref, *refs):
    *probs_refs, out_ref = refs
    n = codes_ref.shape[1]
    weights, exp_total, total = row_factors(first_ref, last_ref, n)
    codes = codes_ref[...]
    probs = column_sum(probs_refs)
    over = weights / total * (1.0 / STUDENT_TEMP)
    feature = probs * (weights / exp_total * (1.0 / STUDENT_TEMP)) - codes * over
    own = n // out_ref.shape[0]
    out_ref[:, :own, :] = feature.T.reshape(out_ref.shape[0], own, out_ref.shape[2])
    share = 1.0 / out_ref.shape[0]
    cross = jnp.sum(turned_ref[...].astype(F32) * codes, axis=0, keepdims=True)
    part = jnp.sum(weights * jnp.log(exp_total) * share - over * cross)
    count = jnp.sum(weights) * share
    tail = (out_ref.shape[0], out_ref.shape[1] - own, out_ref.shape[2])
    lane = lax.broadcasted_iota(jnp.int32, tail, 2)
    out_ref[:, own:, :] = jnp.where(lane == 0, part, jnp.where(lane == 1, count, 0.0))


def on_device(student_feats, teacher_feats, proto_weight, mask_index, row_weight):
    n_patch, n_proto = lax.axis_size("patch"), lax.axis_size("proto")
    d, protos = proto_weight.shape
    length = student_feats.shape[0]
    own = mask_index.shape[0]
    rows = own * n_proto
    chips = n_patch // 2
    share = d // n_patch
    width = protos // 8
    patch, proto = lax.axis_index("patch"), lax.axis_index("proto")
    place = jnp.stack([proto, patch // 2, patch % 2]).astype(jnp.int32)
    product = 2 * rows * d * protos

    def exchange(array, axis):
        return lax.all_to_all(array, axis, 0, 0)

    def hop(array, bits):
        return lax.ppermute(array, "patch", [(i, i ^ bits) for i in range(n_patch)])

    own_rows, x_rows, own_weights = call(
        rows_body,
        "own_rows",
        (
            shape((n_proto, 2 * own, d), BF16),
            shape((own, d), F32),
            shape((8, rows), F32),
        ),
        (place, student_feats, teacher_feats, mask_index[None, :], row_weight[None, :]),
        1 << 28,
        specs=[SMEM, HBM, HBM, HBM, HBM],
        scratch=[
            pltpu.VMEM((length, d), BF16),
            pltpu.VMEM((length, d), BF16),
            pltpu.VMEM((1, own), jnp.int32),
            pltpu.VMEM((1, own), BF16),
            pltpu.SemaphoreType.DMA((4,)),
        ],
    )
    all_rows = exchange(own_rows, "proto")
    unit, inverse = call(
        proto_body,
        "proto_unit",
        (pltpu.HBM((d, protos), BF16), shape((8, width), F32)),
        (proto_weight,),
        product,
        specs=[HBM],
        scratch=[
            pltpu.VMEM((d, protos), BF16),
            pltpu.VMEM((d, protos), BF16),
            pltpu.SemaphoreType.DMA((8,)),
            pltpu.SemaphoreType.DMA((8,)),
        ],
    )
    codes, sums = call(
        table_body,
        "teacher_table",
        (shape((rows, protos), BF16), shape((8, width), F32)),
        (all_rows, unit),
        2 * product,
        specs=[VMEM, HBM],
        scratch=[pltpu.VMEM((d, protos), BF16), pltpu.SemaphoreType.DMA((8,))],
    )

    messages = []
    pieces = []
    for sweep in range(SK_ITERS):
        sums = sums + hop(sums, 1)
        parts = [sums] + [hop(sums, 2 * k) for k in range(1, chips)]
        span = PIECES[sweep] * width
        last = sweep == SK_ITERS - 1
        pieces.append(
            call(
                functools.partial(student_body, sweep),
                "student_table",
                (shape((rows, span), BF16), shape((8, rows), F32), shape((d, rows), F32))
                + ((shape((d, rows), BF16),) if last else ()),
                (all_rows, unit),
                product,
                after=(sums,),
            )
        )
        part = call(
            functools.partial(row_pass_body, chips),
            "row_pass",
            shape((n_proto, 8, LANES), F32),
            (*parts, codes, *([piece[1] for piece in pieces] if last else [own_weights])),
            product,
            after=() if last else (pieces[-1][1],),
        )
        messages.append(exchange(part, "proto"))
        if not last:
            sums = call(
                col_pass_body,
                "col_pass",
                shape((8, width), F32),
                (messages[-1], codes),
                product // 2,
            )

    turned = pieces[-1][3]
    factors = (messages[0], messages[-1])
    heads = []
    for index, count in enumerate(PARTS):
        span = count * width
        heads.append(
            call(
                functools.partial(head_body, sum(PARTS[:index]), count, chips),
                "head",
                (
                    shape((share, span), F32),
                    shape((chips - 1, share, span), F32),
                    shape((chips, share, span), BF16),
                ),
                (
                    place,
                    *factors,
                    *parts,
                    turned,
                    inverse,
                    codes,
                    *[piece[0] for piece in pieces],
                    proto_weight,
                ),
                2 * product,
                specs=[SMEM] + [VMEM] * (len(factors) + chips + 4 + len(pieces)),
                after=(heads[-1][0],) if heads else (),
                scratch=[pltpu.VMEM((d, rows), BF16)],
            )
        )

    def send_part(index, after):
        own_part, keep, near = heads[index]
        span = own_part.shape[1]
        own_part, *pairs = call(
            pair_body,
            "pair_sums",
            (shape((share, span), F32),)
            + tuple(shape((share, span), BF16) for _ in range(chips - 1)),
            (own_part, keep, hop(near, 1)),
            product // 8,
            after=after,
        )
        return [own_part] + [hop(pair, 2 * (k + 1)) for k, pair in enumerate(pairs)]

    left = send_part(0, (heads[1][0],))
    codes_feature = call(
        codes_feature_body,
        "codes_feature",
        shape((d, rows), F32),
        (*parts, codes, unit),
        product,
        after=(left[0],),
    )
    left_sum = call(
        left_body,
        "left_sum",
        shape((share, PARTS[0] * width), F32),
        tuple(left),
        product // 8,
        after=(codes_feature,),
    )
    feature_part = call(
        feature_body,
        "feature",
        shape((n_proto, own + 8, d), F32),
        (*factors, codes_feature, turned, *[piece[2] for piece in pieces]),
        product // 4,
        after=(left_sum,),
    )
    right = send_part(1, (feature_part,))
    grad_student, tails = call(
        owner_body,
        "owner",
        (shape((own, d), F32), shape((n_patch, 8, LANES), F32)),
        (exchange(feature_part, "proto"), x_rows),
        product // 8,
    )
    grad_proto = call(
        final_body,
        "assemble",
        shape((share, protos), F32),
        (left_sum, *right),
        product // 4,
        after=(tails,),
    )
    losses = jnp.sum(exchange(tails, "patch"), axis=0)
    return (grad_student, grad_proto, losses[0, 0] / losses[0, 1])


def solution(mesh):
    both = ("patch", "proto")
    in_specs = (P(both, None), P(both, None), P(None, "proto"), P(both), P(both))
    out_specs = (P(both, None), P("patch", "proto"), P())
    return jax.shard_map(
        on_device, mesh=mesh, in_specs=in_specs, out_specs=out_specs, check_vma=False
    )
```

```python
import functools

import jax
import jax.numpy as jnp
from jax import lax
from jax.experimental import pallas as pl
from jax.experimental.pallas import tpu as pltpu
from jax.sharding import PartitionSpec as P

SK_ITERS = 3
EPS = 1e-06
TEACHER_TEMP = 0.07
STUDENT_TEMP = 0.1
F32 = jnp.float32
BF16 = jnp.bfloat16
LANES = 128
PIECES = (3, 3, 2)
VMEM_LIMIT = 20 * 1024 * 1024

NN = (((1,), (0,)), ((), ()))
NT = (((1,), (1,)), ((), ()))
TN = (((0,), (0,)), ((), ()))
SMEM = pl.BlockSpec(memory_space=pltpu.SMEM)
VMEM = pl.BlockSpec(memory_space=pltpu.VMEM)
ANY = pl.BlockSpec(memory_space=pl.ANY)
HBM = pl.BlockSpec(memory_space=pltpu.HBM)


def mm(a, b, dims=NN):
    return lax.dot_general(a, b, dims, preferred_element_type=F32)


def shape(dims, dtype):
    return jax.ShapeDtypeStruct(dims, dtype)


def call(body, name, out_shape, args, flops, specs=None, after=(), scratch=(), limit=VMEM_LIMIT):
    specs = specs or [VMEM] * len(args)
    skip = len(after)
    args = [
        pltpu.with_memory_space_constraint(arg, pltpu.HBM) if spec is HBM else arg
        for arg, spec in zip(args, specs)
    ]

    def ordered(*refs):
        body(*refs[skip:])

    def out_spec(out):
        return VMEM if isinstance(out, jax.ShapeDtypeStruct) else HBM

    many = isinstance(out_shape, tuple)
    return pl.pallas_call(
        ordered,
        name=name,
        out_shape=out_shape,
        in_specs=[ANY] * skip + specs,
        out_specs=tuple(map(out_spec, out_shape)) if many else out_spec(out_shape),
        scratch_shapes=list(scratch),
        compiler_params=pltpu.CompilerParams(vmem_limit_bytes=limit),
        cost_estimate=pl.CostEstimate(flops=flops, bytes_accessed=1 << 16, transcendentals=0),
    )(*after, *args)


def three_terms(row):
    high = row.astype(BF16).astype(F32)
    rest = row - high
    mid = rest.astype(BF16).astype(F32)
    low = rest - mid
    index = lax.broadcasted_iota(jnp.int32, (16, row.shape[1]), 0)
    terms = jnp.where(
        index == 0, high, jnp.where(index == 1, mid, jnp.where(index == 2, low, 0.0))
    )
    return terms.astype(BF16)


def column_sum(refs):
    total = refs[0][...]
    for ref in refs[1:]:
        total = total + ref[...]
    return total


def chunks(table_ref, count=8):
    width = table_ref.shape[1] // count
    return [(j, pl.ds(j * width, width)) for j in range(count)]


def arrive(copies, j, ahead):
    if j == 0:
        for copy in copies[:ahead]:
            copy.start()
    copies[j].wait()
    if j + ahead < len(copies):
        copies[j + ahead].start()


def read_rows(message_ref, start, n):
    total = jnp.sum(message_ref[...], axis=0)
    pieces = [total[start + k : start + k + 1, :] for k in range(n // LANES)]
    return jnp.concatenate(pieces, axis=1)


def write_rows(message_ref, start, row):
    count = message_ref.shape[0]
    for k in range(row.shape[1] // LANES):
        piece = row[:, k * LANES : (k + 1) * LANES]
        message_ref[:, start + k, :] = jnp.broadcast_to(piece, (count, LANES))


def rows_body(
    place_ref,
    student_hbm,
    teacher_hbm,
    index_hbm,
    weight_hbm,
    rows_ref,
    x_ref,
    w_ref,
    student_ref,
    teacher_ref,
    index_ref,
    weight_ref,
    sems,
):
    copies = [
        pltpu.make_async_copy(index_hbm, index_ref, sems.at[0]),
        pltpu.make_async_copy(teacher_hbm, teacher_ref, sems.at[1]),
        pltpu.make_async_copy(student_hbm, student_ref, sems.at[2]),
        pltpu.make_async_copy(weight_hbm, weight_ref, sems.at[3]),
    ]
    for copy in copies:
        copy.start()
    for copy in copies:
        copy.wait()
    picks = index_ref[...]
    length = student_ref.shape[0]
    count = picks.shape[1]
    one_hot = (lax.broadcasted_iota(jnp.int32, (length, count), 0) == picks).astype(BF16)
    x = mm(one_hot, student_ref[...], TN)
    y = mm(one_hot, teacher_ref[...], TN)
    x_ref[...] = x
    unit_x = x * lax.rsqrt(jnp.sum(x * x, axis=1, keepdims=True) + EPS)
    unit_y = y * lax.rsqrt(jnp.sum(y * y, axis=1, keepdims=True) + EPS)
    both = jnp.concatenate([unit_y.astype(BF16), unit_x.astype(BF16)], axis=0)
    rows_ref[...] = jnp.broadcast_to(both[None], rows_ref.shape)
    lanes = w_ref.shape[1]
    spot = lax.broadcasted_iota(jnp.int32, (count, lanes), 1) - place_ref[0] * count
    spread = (spot == lax.broadcasted_iota(jnp.int32, (count, lanes), 0)).astype(BF16)
    w_ref[...] = jnp.broadcast_to(mm(weight_ref[...], spread), w_ref.shape)


def proto_body(w_hbm, unit_hbm, inverse_ref, w_ref, unit_ref, in_sems, out_sems):
    count = unit_ref.shape[0]
    copies = [
        pltpu.make_async_copy(w_hbm.at[:, cols], w_ref.at[:, cols], in_sems.at[j])
        for j, cols in chunks(w_ref, count)
    ]
    stores = []
    for j, cols in chunks(w_ref, count):
        arrive(copies, j, 4)
        w = w_ref[:, cols].astype(F32)
        inverse = lax.rsqrt(jnp.sum(w * w, axis=0, keepdims=True) + EPS)
        inverse_ref[pl.ds(j, 1), :] = inverse
        unit_ref[j] = (w * inverse).astype(BF16)
        store = pltpu.make_async_copy(unit_ref.at[j], unit_hbm.at[j], out_sems.at[j])
        store.start()
        stores.append(store)
    for store in stores:
        store.wait()


def table_body(rows_ref, unit_hbm, table_ref, sums_ref, unit_ref, sems):
    copies = [
        pltpu.make_async_copy(unit_hbm.at[j], unit_ref.at[j], sems.at[j])
        for j in range(unit_ref.shape[0])
    ]
    half = rows_ref.shape[1] // 2
    teacher = rows_ref[:, :half, :].reshape(-1, rows_ref.shape[2])
    for j, cols in chunks(table_ref):
        arrive(copies, j, 3)
        table = jnp.exp(mm(teacher, unit_ref[j]) * (1.0 / TEACHER_TEMP)).astype(BF16)
        table_ref[:, cols] = table
        sums_ref[pl.ds(j, 1), :] = jnp.sum(table.astype(F32), axis=0, keepdims=True)


def row_pass_body(parts, *refs):
    sums_refs, table_ref, extra_refs, out_ref = refs[:parts], refs[parts], refs[parts + 1 : -1], refs[-1]
    scale = 1.0 / column_sum(sums_refs)
    n = table_ref.shape[0]
    total = jnp.zeros((16, n), F32)
    for j, cols in chunks(table_ref):
        total += mm(three_terms(scale[j : j + 1, :]), table_ref[:, cols], NT)
    write_rows(out_ref, 0, jnp.sum(total, axis=0, keepdims=True))
    write_rows(out_ref, n // LANES, column_sum(extra_refs)[0:1, :])


def col_pass_body(message_ref, table_ref, out_ref):
    terms = three_terms(1.0 / read_rows(message_ref, 0, table_ref.shape[0]))
    for j, cols in chunks(table_ref):
        out_ref[pl.ds(j, 1), :] = jnp.sum(mm(terms, table_ref[:, cols]), axis=0, keepdims=True)


def student_body(first, rows_ref, unit_ref, table_ref, sums_ref, feature_ref, *turned_refs):
    count = PIECES[first]
    start = sum(PIECES[:first])
    half = rows_ref.shape[1] // 2
    student = rows_ref[:, half:, :].reshape(-1, rows_ref.shape[2])
    total = jnp.zeros((16, student.shape[0]), F32)
    for j, cols in chunks(table_ref, count):
        unit = unit_ref[start + j]
        table = jnp.exp(mm(student, unit) * (1.0 / STUDENT_TEMP)).astype(BF16)
        table_ref[:, cols] = table
        total += mm(jnp.ones((16, table.shape[1]), BF16), table, NT)
        part = mm(unit, table, NT)
        if j == 0:
            feature_ref[...] = part
        else:
            feature_ref[...] += part
    sums_ref[...] = total[0:8]
    for turned_ref in turned_refs:
        d = student.shape[1]
        eye = (
            lax.broadcasted_iota(jnp.int32, (d, d), 0)
            == lax.broadcasted_iota(jnp.int32, (d, d), 1)
        ).astype(BF16)
        turned_ref[...] = mm(eye, student, NT).astype(BF16)


def codes_feature_body(*refs):
    *sums_refs, table_ref, unit_ref, feature_ref = refs
    scale = 1.0 / column_sum(sums_refs)
    for j, cols in chunks(table_ref):
        scaled = (unit_ref[j].astype(F32) * scale[j : j + 1, :]).astype(BF16)
        part = mm(scaled, table_ref[:, cols], NT)
        if j == 0:
            feature_ref[...] = part
        else:
            feature_ref[...] += part


def row_factors(first_ref, last_ref, n):
    tile = n // LANES
    return read_rows(first_ref, tile, n), read_rows(last_ref, tile, n), read_rows(last_ref, 0, n)


def head_body(parts, *refs):
    place_ref, first_ref, last_ref = refs[:3]
    sums_refs = refs[3 : 3 + parts]
    turned_ref, inverse_ref, codes_ref, *piece_refs, w_ref = refs[3 + parts : -7]
    own_hbm, own_near_ref, keep_ref, near_ref, turn_ref, own_ref, sems = refs[-7:]
    x, core = place_ref[1], place_ref[2]
    share = near_ref.shape[1]
    chips = near_ref.shape[0] + 1
    spots = []
    for k in range(chips):
        for side in (core, 1 - core):
            spots.append(pl.ds(pl.multiple_of((2 * (x ^ k) + side) * share, share), share))
    for m, spot in enumerate(spots):
        turn_ref[pl.ds(m * share, share), :] = turned_ref[spot, :]
    weights, exp_total, total = row_factors(first_ref, last_ref, codes_ref.shape[0])
    turned = turn_ref[...].astype(F32)
    left_probs = (turned * (weights / exp_total * (1.0 / STUDENT_TEMP))).astype(BF16)
    left_codes = (turned * (weights / total * (1.0 / STUDENT_TEMP))).astype(BF16)
    scale = 1.0 / column_sum(sums_refs)
    where = [(p, at) for p, size in enumerate(PIECES) for at in range(size)]
    stores = []
    for j, cols in chunks(codes_ref):
        piece, at = where[j]
        width = codes_ref.shape[1] // len(where)
        head = mm(left_probs, piece_refs[piece][:, pl.ds(at * width, width)]) - scale[
            j : j + 1, :
        ] * mm(left_codes, codes_ref[:, cols])
        inverse = inverse_ref[pl.ds(j, 1), :]
        w = jnp.concatenate([w_ref[spot, cols] for spot in spots], axis=0)
        unit = w.astype(F32) * inverse
        inner = jnp.sum(unit * head, axis=0, keepdims=True)
        grad = inverse * (head - unit * inner)
        own_ref[:, cols] = grad[0:share]
        store = pltpu.make_async_copy(own_ref.at[:, cols], own_hbm.at[:, cols], sems.at[j])
        store.start()
        stores.append(store)
        own_near_ref[:, cols] = grad[share : 2 * share].astype(BF16)
        for k in range(1, chips):
            low = 2 * k * share
            keep_ref[k - 1, :, cols] = grad[low : low + share].astype(BF16)
            near_ref[k - 1, :, cols] = grad[low + share : low + 2 * share].astype(BF16)
    for store in stores:
        store.wait()


def pair_body(keep_ref, near_ref, *pair_refs):
    for k, pair_ref in enumerate(pair_refs):
        pair_ref[...] = (keep_ref[k].astype(F32) + near_ref[k].astype(F32)).astype(BF16)


def own_sum_body(own_ref, near_ref, out_ref):
    out_ref[...] = own_ref[...] + near_ref[...].astype(F32)


def final_body(own_ref, *refs):
    *far_refs, out_ref = refs
    total = own_ref[...]
    for far_ref in far_refs:
        total = total + far_ref[...].astype(F32)
    out_ref[...] = total


def owner_body(sent_ref, x_ref, grad_ref, tail_ref):
    sent = jnp.sum(sent_ref[...], axis=0)
    own = x_ref.shape[0]
    x = x_ref[...]
    feature = sent[:own]
    inverse = lax.rsqrt(jnp.sum(x * x, axis=1, keepdims=True) + EPS)
    unit = x * inverse
    grad_ref[...] = inverse * (feature - unit * jnp.sum(unit * feature, axis=1, keepdims=True))
    tail_ref[...] = jnp.broadcast_to(sent[own:, :LANES][None], tail_ref.shape)


def feature_body(first_ref, last_ref, codes_ref, turned_ref, *refs):
    *probs_refs, out_ref = refs
    n = codes_ref.shape[1]
    weights, exp_total, total = row_factors(first_ref, last_ref, n)
    codes = codes_ref[...]
    probs = column_sum(probs_refs)
    over = weights / total * (1.0 / STUDENT_TEMP)
    feature = probs * (weights / exp_total * (1.0 / STUDENT_TEMP)) - codes * over
    own = n // out_ref.shape[0]
    out_ref[:, :own, :] = feature.T.reshape(out_ref.shape[0], own, out_ref.shape[2])
    share = 1.0 / out_ref.shape[0]
    cross = jnp.sum(turned_ref[...].astype(F32) * codes, axis=0, keepdims=True)
    part = jnp.sum(weights * jnp.log(exp_total) * share - over * cross)
    count = jnp.sum(weights) * share
    tail = (out_ref.shape[0], out_ref.shape[1] - own, out_ref.shape[2])
    lane = lax.broadcasted_iota(jnp.int32, tail, 2)
    out_ref[:, own:, :] = jnp.where(lane == 0, part, jnp.where(lane == 1, count, 0.0))


def on_device(student_feats, teacher_feats, proto_weight, mask_index, row_weight):
    n_patch, n_proto = lax.axis_size("patch"), lax.axis_size("proto")
    d, protos = proto_weight.shape
    length = student_feats.shape[0]
    own = mask_index.shape[0]
    rows = own * n_proto
    chips = n_patch // 2
    share = d // n_patch
    width = protos // 8
    patch, proto = lax.axis_index("patch"), lax.axis_index("proto")
    place = jnp.stack([proto, patch // 2, patch % 2]).astype(jnp.int32)
    product = 2 * rows * d * protos

    def exchange(array, axis):
        return lax.all_to_all(array, axis, 0, 0)

    def hop(array, bits):
        return lax.ppermute(array, "patch", [(i, i ^ bits) for i in range(n_patch)])

    own_rows, x_rows, own_weights = call(
        rows_body,
        "own_rows",
        (
            shape((n_proto, 2 * own, d), BF16),
            shape((own, d), F32),
            shape((8, rows), F32),
        ),
        (place, student_feats, teacher_feats, mask_index[None, :], row_weight[None, :]),
        1 << 28,
        specs=[SMEM, HBM, HBM, HBM, HBM],
        scratch=[
            pltpu.VMEM((length, d), BF16),
            pltpu.VMEM((length, d), BF16),
            pltpu.VMEM((1, own), jnp.int32),
            pltpu.VMEM((1, own), BF16),
            pltpu.SemaphoreType.DMA((4,)),
        ],
    )
    all_rows = exchange(own_rows, "proto")
    unit, inverse = call(
        proto_body,
        "proto_unit",
        (pltpu.HBM((8, d, width), BF16), shape((8, width), F32)),
        (proto_weight,),
        product,
        specs=[HBM],
        scratch=[
            pltpu.VMEM((d, protos), BF16),
            pltpu.VMEM((8, d, width), BF16),
            pltpu.SemaphoreType.DMA((8,)),
            pltpu.SemaphoreType.DMA((8,)),
        ],
    )
    codes, sums = call(
        table_body,
        "teacher_table",
        (shape((rows, protos), BF16), shape((8, width), F32)),
        (all_rows, unit),
        2 * product,
        specs=[VMEM, HBM],
        scratch=[pltpu.VMEM((8, d, width), BF16), pltpu.SemaphoreType.DMA((8,))],
    )

    messages = []
    pieces = []
    for sweep in range(SK_ITERS):
        sums = sums + hop(sums, 1)
        parts = [sums] + [hop(sums, 2 * k) for k in range(1, chips)]
        span = PIECES[sweep] * width
        last = sweep == SK_ITERS - 1
        pieces.append(
            call(
                functools.partial(student_body, sweep),
                "student_table",
                (shape((rows, span), BF16), shape((8, rows), F32), shape((d, rows), F32))
                + ((shape((d, rows), BF16),) if last else ()),
                (all_rows, unit),
                product,
                after=(sums,),
            )
        )
        part = call(
            functools.partial(row_pass_body, chips),
            "row_pass",
            shape((n_proto, 8, LANES), F32),
            (*parts, codes, *([piece[1] for piece in pieces] if last else [own_weights])),
            product,
            after=() if last else (pieces[-1][1],),
        )
        messages.append(exchange(part, "proto"))
        if not last:
            sums = call(
                col_pass_body,
                "col_pass",
                shape((8, width), F32),
                (messages[-1], codes),
                product // 2,
            )

    turned = pieces[-1][3]
    factors = (messages[0], messages[-1])
    own_block, own_near, keep, near = call(
        functools.partial(head_body, chips),
        "head",
        (
            pltpu.HBM((share, protos), F32),
            shape((share, protos), BF16),
            shape((chips - 1, share, protos), BF16),
            shape((chips - 1, share, protos), BF16),
        ),
        (
            place,
            *factors,
            *parts,
            turned,
            inverse,
            codes,
            *[piece[0] for piece in pieces],
            proto_weight,
        ),
        4 * product,
        specs=[SMEM] + [VMEM] * (len(factors) + chips + 4 + len(pieces)),
        scratch=[
            pltpu.VMEM((d, rows), BF16),
            pltpu.VMEM((share, protos), F32),
            pltpu.SemaphoreType.DMA((8,)),
        ],
    )
    codes_feature = call(
        codes_feature_body,
        "codes_feature",
        shape((d, rows), F32),
        (*parts, codes, unit),
        product,
        after=(keep,),
    )
    feature_part = call(
        feature_body,
        "feature",
        shape((n_proto, own + 8, d), F32),
        (*factors, codes_feature, turned, *[piece[2] for piece in pieces]),
        product // 4,
    )
    pairs = call(
        pair_body,
        "pair_sums",
        tuple(shape((share, protos), BF16) for _ in range(chips - 1)),
        (keep, hop(near, 1)),
        product // 8,
        after=(feature_part,),
    )
    far = [hop(pair, 2 * (k + 1)) for k, pair in enumerate(pairs)]
    grad_student, tails = call(
        owner_body,
        "owner",
        (shape((own, d), F32), shape((n_patch, 8, LANES), F32)),
        (exchange(feature_part, "proto"), x_rows),
        product // 8,
    )
    own_sum = call(
        own_sum_body,
        "own_sum",
        shape((share, protos), F32),
        (own_block, hop(own_near, 1)),
        product // 8,
        after=(tails,),
    )
    grad_proto = call(
        final_body,
        "assemble",
        shape((share, protos), F32),
        (own_sum, *far),
        product // 4,
    )
    losses = jnp.sum(exchange(tails, "patch"), axis=0)
    return (grad_student, grad_proto, losses[0, 0] / losses[0, 1])


def solution(mesh):
    both = ("patch", "proto")
    in_specs = (P(both, None), P(both, None), P(None, "proto"), P(both), P(both))
    out_specs = (P(both, None), P("patch", "proto"), P())
    return jax.shard_map(
        on_device, mesh=mesh, in_specs=in_specs, out_specs=out_specs, check_vma=False
    )
```

```python
import functools

import jax
import jax.numpy as jnp
from jax import lax
from jax.experimental import pallas as pl
from jax.experimental.pallas import tpu as pltpu
from jax.sharding import PartitionSpec as P

SK_ITERS = 3
EPS = 1e-06
TEACHER_TEMP = 0.07
STUDENT_TEMP = 0.1
F32 = jnp.float32
BF16 = jnp.bfloat16
LANES = 128
PIECES = (3, 3, 2)
FIRST = 2
VMEM_LIMIT = 20 * 1024 * 1024

NN = (((1,), (0,)), ((), ()))
NT = (((1,), (1,)), ((), ()))
TN = (((0,), (0,)), ((), ()))
SMEM = pl.BlockSpec(memory_space=pltpu.SMEM)
VMEM = pl.BlockSpec(memory_space=pltpu.VMEM)
ANY = pl.BlockSpec(memory_space=pl.ANY)
HBM = pl.BlockSpec(memory_space=pltpu.HBM)


def mm(a, b, dims=NN):
    return lax.dot_general(a, b, dims, preferred_element_type=F32)


def shape(dims, dtype):
    return jax.ShapeDtypeStruct(dims, dtype)


def call(body, name, out_shape, args, flops, specs=None, after=(), scratch=(), limit=VMEM_LIMIT):
    specs = specs or [VMEM] * len(args)
    skip = len(after)
    args = [
        pltpu.with_memory_space_constraint(arg, pltpu.HBM) if spec is HBM else arg
        for arg, spec in zip(args, specs)
    ]

    def ordered(*refs):
        body(*refs[skip:])

    def out_spec(out):
        return VMEM if isinstance(out, jax.ShapeDtypeStruct) else HBM

    many = isinstance(out_shape, tuple)
    return pl.pallas_call(
        ordered,
        name=name,
        out_shape=out_shape,
        in_specs=[ANY] * skip + specs,
        out_specs=tuple(map(out_spec, out_shape)) if many else out_spec(out_shape),
        scratch_shapes=list(scratch),
        compiler_params=pltpu.CompilerParams(vmem_limit_bytes=limit),
        cost_estimate=pl.CostEstimate(flops=flops, bytes_accessed=1 << 16, transcendentals=0),
    )(*after, *args)


def three_terms(row):
    high = row.astype(BF16).astype(F32)
    rest = row - high
    mid = rest.astype(BF16).astype(F32)
    low = rest - mid
    index = lax.broadcasted_iota(jnp.int32, (16, row.shape[1]), 0)
    terms = jnp.where(
        index == 0, high, jnp.where(index == 1, mid, jnp.where(index == 2, low, 0.0))
    )
    return terms.astype(BF16)


def column_sum(refs):
    total = refs[0][...]
    for ref in refs[1:]:
        total = total + ref[...]
    return total


def chunks(table_ref, count=8):
    width = table_ref.shape[1] // count
    return [(j, pl.ds(j * width, width)) for j in range(count)]


def arrive(copies, j, ahead):
    if j == 0:
        for copy in copies[:ahead]:
            copy.start()
    copies[j].wait()
    if j + ahead < len(copies):
        copies[j + ahead].start()


def read_rows(message_ref, start, n):
    total = jnp.sum(message_ref[...], axis=0)
    pieces = [total[start + k : start + k + 1, :] for k in range(n // LANES)]
    return jnp.concatenate(pieces, axis=1)


def write_rows(message_ref, start, row):
    count = message_ref.shape[0]
    for k in range(row.shape[1] // LANES):
        piece = row[:, k * LANES : (k + 1) * LANES]
        message_ref[:, start + k, :] = jnp.broadcast_to(piece, (count, LANES))


def rows_body(
    place_ref,
    student_hbm,
    teacher_hbm,
    index_hbm,
    weight_hbm,
    rows_ref,
    x_ref,
    w_ref,
    student_ref,
    teacher_ref,
    index_ref,
    weight_ref,
    sems,
):
    copies = [
        pltpu.make_async_copy(index_hbm, index_ref, sems.at[0]),
        pltpu.make_async_copy(teacher_hbm, teacher_ref, sems.at[1]),
        pltpu.make_async_copy(student_hbm, student_ref, sems.at[2]),
        pltpu.make_async_copy(weight_hbm, weight_ref, sems.at[3]),
    ]
    for copy in copies:
        copy.start()
    for copy in copies:
        copy.wait()
    picks = index_ref[...]
    length = student_ref.shape[0]
    count = picks.shape[1]
    one_hot = (lax.broadcasted_iota(jnp.int32, (length, count), 0) == picks).astype(BF16)
    x = mm(one_hot, student_ref[...], TN)
    y = mm(one_hot, teacher_ref[...], TN)
    x_ref[...] = x
    unit_x = x * lax.rsqrt(jnp.sum(x * x, axis=1, keepdims=True) + EPS)
    unit_y = y * lax.rsqrt(jnp.sum(y * y, axis=1, keepdims=True) + EPS)
    both = jnp.concatenate([unit_y.astype(BF16), unit_x.astype(BF16)], axis=0)
    rows_ref[...] = jnp.broadcast_to(both[None], rows_ref.shape)
    lanes = w_ref.shape[1]
    spot = lax.broadcasted_iota(jnp.int32, (count, lanes), 1) - place_ref[0] * count
    spread = (spot == lax.broadcasted_iota(jnp.int32, (count, lanes), 0)).astype(BF16)
    w_ref[...] = jnp.broadcast_to(mm(weight_ref[...], spread), w_ref.shape)


def proto_body(w_hbm, unit_hbm, first_ref, inverse_ref, w_ref, unit_ref, in_sems, out_sems):
    count = unit_ref.shape[0]
    copies = [
        pltpu.make_async_copy(w_hbm.at[:, cols], w_ref.at[:, cols], in_sems.at[j])
        for j, cols in chunks(w_ref, count)
    ]
    stores = []
    for j, cols in chunks(w_ref, count):
        arrive(copies, j, 4)
        w = w_ref[:, cols].astype(F32)
        inverse = lax.rsqrt(jnp.sum(w * w, axis=0, keepdims=True) + EPS)
        inverse_ref[pl.ds(j, 1), :] = inverse
        unit = (w * inverse).astype(BF16)
        unit_ref[j] = unit
        if j < first_ref.shape[0]:
            first_ref[j] = unit
        store = pltpu.make_async_copy(unit_ref.at[j], unit_hbm.at[j], out_sems.at[j])
        store.start()
        stores.append(store)
    for store in stores:
        store.wait()


def table_body(rows_ref, first_ref, unit_hbm, table_ref, sums_ref, unit_ref, sems):
    skip = first_ref.shape[0]
    copies = [
        pltpu.make_async_copy(unit_hbm.at[skip + j], unit_ref.at[j], sems.at[j])
        for j in range(unit_ref.shape[0])
    ]
    for copy in copies:
        copy.start()
    half = rows_ref.shape[1] // 2
    teacher = rows_ref[:, :half, :].reshape(-1, rows_ref.shape[2])
    for j, cols in chunks(table_ref):
        if j < skip:
            unit = first_ref[j]
        else:
            copies[j - skip].wait()
            unit = unit_ref[j - skip]
        table = jnp.exp(mm(teacher, unit) * (1.0 / TEACHER_TEMP)).astype(BF16)
        table_ref[:, cols] = table
        sums_ref[pl.ds(j, 1), :] = jnp.sum(table.astype(F32), axis=0, keepdims=True)


def row_pass_body(parts, *refs):
    sums_refs, table_ref, extra_refs, out_ref = refs[:parts], refs[parts], refs[parts + 1 : -1], refs[-1]
    scale = 1.0 / column_sum(sums_refs)
    n = table_ref.shape[0]
    total = jnp.zeros((16, n), F32)
    for j, cols in chunks(table_ref):
        total += mm(three_terms(scale[j : j + 1, :]), table_ref[:, cols], NT)
    write_rows(out_ref, 0, jnp.sum(total, axis=0, keepdims=True))
    write_rows(out_ref, n // LANES, column_sum(extra_refs)[0:1, :])


def col_pass_body(message_ref, table_ref, out_ref):
    terms = three_terms(1.0 / read_rows(message_ref, 0, table_ref.shape[0]))
    for j, cols in chunks(table_ref):
        out_ref[pl.ds(j, 1), :] = jnp.sum(mm(terms, table_ref[:, cols]), axis=0, keepdims=True)


def student_body(first, rows_ref, unit_ref, table_ref, sums_ref, feature_ref, *turned_refs):
    count = PIECES[first]
    start = sum(PIECES[:first])
    half = rows_ref.shape[1] // 2
    student = rows_ref[:, half:, :].reshape(-1, rows_ref.shape[2])
    total = jnp.zeros((16, student.shape[0]), F32)
    for j, cols in chunks(table_ref, count):
        unit = unit_ref[start + j]
        table = jnp.exp(mm(student, unit) * (1.0 / STUDENT_TEMP)).astype(BF16)
        table_ref[:, cols] = table
        total += mm(jnp.ones((16, table.shape[1]), BF16), table, NT)
        part = mm(unit, table, NT)
        if j == 0:
            feature_ref[...] = part
        else:
            feature_ref[...] += part
    sums_ref[...] = total[0:8]
    for turned_ref in turned_refs:
        d = student.shape[1]
        eye = (
            lax.broadcasted_iota(jnp.int32, (d, d), 0)
            == lax.broadcasted_iota(jnp.int32, (d, d), 1)
        ).astype(BF16)
        turned_ref[...] = mm(eye, student, NT).astype(BF16)


def codes_feature_body(*refs):
    *sums_refs, table_ref, unit_ref, feature_ref = refs
    scale = 1.0 / column_sum(sums_refs)
    for j, cols in chunks(table_ref):
        scaled = (unit_ref[j].astype(F32) * scale[j : j + 1, :]).astype(BF16)
        part = mm(scaled, table_ref[:, cols], NT)
        if j == 0:
            feature_ref[...] = part
        else:
            feature_ref[...] += part


def row_factors(first_ref, last_ref, n):
    tile = n // LANES
    return read_rows(first_ref, tile, n), read_rows(last_ref, tile, n), read_rows(last_ref, 0, n)


def head_body(parts, *refs):
    place_ref, first_ref, last_ref = refs[:3]
    sums_refs = refs[3 : 3 + parts]
    turned_ref, inverse_ref, codes_ref, *piece_refs, w_ref = refs[3 + parts : -7]
    own_hbm, own_near_ref, keep_ref, near_ref, turn_ref, own_ref, sems = refs[-7:]
    x, core = place_ref[1], place_ref[2]
    share = near_ref.shape[1]
    chips = near_ref.shape[0] + 1
    spots = []
    for k in range(chips):
        for side in (core, 1 - core):
            spots.append(pl.ds(pl.multiple_of((2 * (x ^ k) + side) * share, share), share))
    for m, spot in enumerate(spots):
        turn_ref[pl.ds(m * share, share), :] = turned_ref[spot, :]
    weights, exp_total, total = row_factors(first_ref, last_ref, codes_ref.shape[0])
    turned = turn_ref[...].astype(F32)
    left_probs = (turned * (weights / exp_total * (1.0 / STUDENT_TEMP))).astype(BF16)
    left_codes = (turned * (weights / total * (1.0 / STUDENT_TEMP))).astype(BF16)
    scale = 1.0 / column_sum(sums_refs)
    where = [(p, at) for p, size in enumerate(PIECES) for at in range(size)]
    stores = []
    for j, cols in chunks(codes_ref):
        piece, at = where[j]
        width = codes_ref.shape[1] // len(where)
        head = mm(left_probs, piece_refs[piece][:, pl.ds(at * width, width)]) - scale[
            j : j + 1, :
        ] * mm(left_codes, codes_ref[:, cols])
        inverse = inverse_ref[pl.ds(j, 1), :]
        w = jnp.concatenate([w_ref[spot, cols] for spot in spots], axis=0)
        unit = w.astype(F32) * inverse
        inner = jnp.sum(unit * head, axis=0, keepdims=True)
        grad = inverse * (head - unit * inner)
        own_ref[:, cols] = grad[0:share]
        store = pltpu.make_async_copy(own_ref.at[:, cols], own_hbm.at[:, cols], sems.at[j])
        store.start()
        stores.append(store)
        own_near_ref[:, cols] = grad[share : 2 * share].astype(BF16)
        for k in range(1, chips):
            low = 2 * k * share
            keep_ref[k - 1, :, cols] = grad[low : low + share].astype(BF16)
            near_ref[k - 1, :, cols] = grad[low + share : low + 2 * share].astype(BF16)
    for store in stores:
        store.wait()


def pair_body(keep_ref, near_ref, *pair_refs):
    for k, pair_ref in enumerate(pair_refs):
        pair_ref[...] = (keep_ref[k].astype(F32) + near_ref[k].astype(F32)).astype(BF16)


def own_sum_body(own_ref, near_ref, tails_ref, out_ref, tails_out_ref):
    out_ref[...] = own_ref[...] + near_ref[...].astype(F32)
    tails_out_ref[...] = tails_ref[...]


def final_body(own_ref, *refs):
    *far_refs, out_ref = refs
    total = own_ref[...]
    for far_ref in far_refs:
        total = total + far_ref[...].astype(F32)
    out_ref[...] = total


def owner_body(sent_ref, x_ref, grad_ref, tail_ref):
    sent = jnp.sum(sent_ref[...].astype(F32), axis=0)
    own = x_ref.shape[0]
    x = x_ref[...]
    feature = sent[:own]
    inverse = lax.rsqrt(jnp.sum(x * x, axis=1, keepdims=True) + EPS)
    unit = x * inverse
    grad_ref[...] = inverse * (feature - unit * jnp.sum(unit * feature, axis=1, keepdims=True))
    tail_ref[...] = jnp.broadcast_to(sent[own : own + 8, :LANES][None], tail_ref.shape)


def split(value):
    row = jnp.broadcast_to(value, (8, LANES))
    high = row.astype(BF16).astype(F32)
    mid = (row - high).astype(BF16).astype(F32)
    return [term[0:1, 0:1] for term in (high, mid, row - high - mid)]


def feature_body(first_ref, last_ref, codes_ref, turned_ref, *refs):
    *probs_refs, out_ref = refs
    n = codes_ref.shape[1]
    count = out_ref.shape[0]
    own = n // count
    weights, exp_total, total = row_factors(first_ref, last_ref, n)
    codes = codes_ref[...]
    over = weights / total * (1.0 / STUDENT_TEMP)
    probs = column_sum(probs_refs) * (weights / exp_total * (1.0 / STUDENT_TEMP))
    feature = (probs - codes * over).T.astype(BF16)
    out_ref[:, :own, :] = feature.reshape(count, own, feature.shape[1])
    share = 1.0 / count
    cross = jnp.sum(turned_ref[...].astype(F32) * codes, axis=0, keepdims=True)
    part = jnp.sum(weights * jnp.log(exp_total) * share - over * cross)
    tail = (out_ref.shape[1] - own, out_ref.shape[2])
    lane = lax.broadcasted_iota(jnp.int32, tail, 1)
    row = jnp.zeros(tail, F32)
    for k, term in enumerate(split(part) + split(jnp.sum(weights) * share)):
        row = jnp.where(lane == k, term, row)
    out_ref[:, own:, :] = jnp.broadcast_to(row.astype(BF16)[None], (count,) + tail)


def on_device(student_feats, teacher_feats, proto_weight, mask_index, row_weight):
    n_patch, n_proto = lax.axis_size("patch"), lax.axis_size("proto")
    d, protos = proto_weight.shape
    length = student_feats.shape[0]
    own = mask_index.shape[0]
    rows = own * n_proto
    chips = n_patch // 2
    share = d // n_patch
    width = protos // 8
    patch, proto = lax.axis_index("patch"), lax.axis_index("proto")
    place = jnp.stack([proto, patch // 2, patch % 2]).astype(jnp.int32)
    product = 2 * rows * d * protos

    def exchange(array, axis):
        return lax.all_to_all(array, axis, 0, 0)

    def hop(array, bits):
        return lax.ppermute(array, "patch", [(i, i ^ bits) for i in range(n_patch)])

    own_rows, x_rows, own_weights = call(
        rows_body,
        "own_rows",
        (
            shape((n_proto, 2 * own, d), BF16),
            shape((own, d), F32),
            shape((8, rows), F32),
        ),
        (place, student_feats, teacher_feats, mask_index[None, :], row_weight[None, :]),
        1 << 28,
        specs=[SMEM, HBM, HBM, HBM, HBM],
        scratch=[
            pltpu.VMEM((length, d), BF16),
            pltpu.VMEM((length, d), BF16),
            pltpu.VMEM((1, own), jnp.int32),
            pltpu.VMEM((1, own), BF16),
            pltpu.SemaphoreType.DMA((4,)),
        ],
    )
    all_rows = exchange(own_rows, "proto")
    unit, unit_first, inverse = call(
        proto_body,
        "proto_unit",
        (
            pltpu.HBM((8, d, width), BF16),
            shape((FIRST, d, width), BF16),
            shape((8, width), F32),
        ),
        (proto_weight,),
        product,
        specs=[HBM],
        scratch=[
            pltpu.VMEM((d, protos), BF16),
            pltpu.VMEM((8, d, width), BF16),
            pltpu.SemaphoreType.DMA((8,)),
            pltpu.SemaphoreType.DMA((8,)),
        ],
    )
    codes, sums = call(
        table_body,
        "teacher_table",
        (shape((rows, protos), BF16), shape((8, width), F32)),
        (all_rows, unit_first, unit),
        2 * product,
        specs=[VMEM, VMEM, HBM],
        scratch=[pltpu.VMEM((8 - FIRST, d, width), BF16), pltpu.SemaphoreType.DMA((8 - FIRST,))],
    )

    messages = []
    pieces = []
    for sweep in range(SK_ITERS):
        sums = sums + hop(sums, 1)
        parts = [sums] + [hop(sums, 2 * k) for k in range(1, chips)]
        span = PIECES[sweep] * width
        last = sweep == SK_ITERS - 1
        pieces.append(
            call(
                functools.partial(student_body, sweep),
                "student_table",
                (shape((rows, span), BF16), shape((8, rows), F32), shape((d, rows), F32))
                + ((shape((d, rows), BF16),) if last else ()),
                (all_rows, unit),
                product,
                after=(sums,),
            )
        )
        part = call(
            functools.partial(row_pass_body, chips),
            "row_pass",
            shape((n_proto, 8, LANES), F32),
            (*parts, codes, *([piece[1] for piece in pieces] if last else [own_weights])),
            product,
            after=() if last else (pieces[-1][1],),
        )
        messages.append(exchange(part, "proto"))
        if not last:
            sums = call(
                col_pass_body,
                "col_pass",
                shape((8, width), F32),
                (messages[-1], codes),
                product // 2,
            )

    turned = pieces[-1][3]
    factors = (messages[0], messages[-1])
    own_block, own_near, keep, near = call(
        functools.partial(head_body, chips),
        "head",
        (
            pltpu.HBM((share, protos), F32),
            shape((share, protos), BF16),
            shape((chips - 1, share, protos), BF16),
            shape((chips - 1, share, protos), BF16),
        ),
        (
            place,
            *factors,
            *parts,
            turned,
            inverse,
            codes,
            *[piece[0] for piece in pieces],
            proto_weight,
        ),
        4 * product,
        specs=[SMEM] + [VMEM] * (len(factors) + chips + 4 + len(pieces)),
        scratch=[
            pltpu.VMEM((d, rows), BF16),
            pltpu.VMEM((share, protos), F32),
            pltpu.SemaphoreType.DMA((8,)),
        ],
    )
    codes_feature = call(
        codes_feature_body,
        "codes_feature",
        shape((d, rows), F32),
        (*parts, codes, unit),
        product,
        after=(keep,),
    )
    feature_part = call(
        feature_body,
        "feature",
        shape((n_proto, own + 16, d), BF16),
        (*factors, codes_feature, turned, *[piece[2] for piece in pieces]),
        product // 4,
    )
    pairs = call(
        pair_body,
        "pair_sums",
        tuple(shape((share, protos), BF16) for _ in range(chips - 1)),
        (keep, hop(near, 1)),
        product // 8,
        after=(feature_part,),
    )
    far = [hop(pairs[k - 1], 2 * k) for k in sorted(range(1, chips), key=lambda k: k % 2)]
    grad_student, tails = call(
        owner_body,
        "owner",
        (shape((own, d), F32), shape((n_patch, 8, LANES), F32)),
        (exchange(feature_part, "proto"), x_rows),
        product // 8,
    )
    own_sum, tails = call(
        own_sum_body,
        "own_sum",
        (shape((share, protos), F32), shape((n_patch, 8, LANES), F32)),
        (own_block, hop(own_near, 1), tails),
        product // 8,
    )
    grad_proto = call(
        final_body,
        "assemble",
        shape((share, protos), F32),
        (own_sum, *far),
        product // 4,
    )
    totals = jnp.sum(exchange(tails, "patch"), axis=0)[0]
    loss = jnp.sum(totals[0:3]) / jnp.sum(totals[3:6])
    return (grad_student, grad_proto, loss)


def solution(mesh):
    both = ("patch", "proto")
    in_specs = (P(both, None), P(both, None), P(None, "proto"), P(both), P(both))
    out_specs = (P(both, None), P("patch", "proto"), P())
    return jax.shard_map(
        on_device, mesh=mesh, in_specs=in_specs, out_specs=out_specs, check_vma=False
    )
```

```python
import functools

import jax
import jax.numpy as jnp
from jax import lax
from jax.experimental import pallas as pl
from jax.experimental.pallas import tpu as pltpu
from jax.sharding import PartitionSpec as P

SK_ITERS = 3
EPS = 1e-06
TEACHER_TEMP = 0.07
STUDENT_TEMP = 0.1
F32 = jnp.float32
BF16 = jnp.bfloat16
LANES = 128
PIECES = (3, 3, 2)
FIRST = 2
VMEM_LIMIT = 20 * 1024 * 1024

NN = (((1,), (0,)), ((), ()))
NT = (((1,), (1,)), ((), ()))
TN = (((0,), (0,)), ((), ()))
SMEM = pl.BlockSpec(memory_space=pltpu.SMEM)
VMEM = pl.BlockSpec(memory_space=pltpu.VMEM)
ANY = pl.BlockSpec(memory_space=pl.ANY)
HBM = pl.BlockSpec(memory_space=pltpu.HBM)


def mm(a, b, dims=NN):
    return lax.dot_general(a, b, dims, preferred_element_type=F32)


def shape(dims, dtype):
    return jax.ShapeDtypeStruct(dims, dtype)


def call(body, name, out_shape, args, flops, specs=None, after=(), scratch=(), limit=VMEM_LIMIT):
    specs = specs or [VMEM] * len(args)
    skip = len(after)
    args = [
        pltpu.with_memory_space_constraint(arg, pltpu.HBM) if spec is HBM else arg
        for arg, spec in zip(args, specs)
    ]

    def ordered(*refs):
        body(*refs[skip:])

    def out_spec(out):
        return VMEM if isinstance(out, jax.ShapeDtypeStruct) else HBM

    many = isinstance(out_shape, tuple)
    return pl.pallas_call(
        ordered,
        name=name,
        out_shape=out_shape,
        in_specs=[ANY] * skip + specs,
        out_specs=tuple(map(out_spec, out_shape)) if many else out_spec(out_shape),
        scratch_shapes=list(scratch),
        compiler_params=pltpu.CompilerParams(vmem_limit_bytes=limit),
        cost_estimate=pl.CostEstimate(flops=flops, bytes_accessed=1 << 16, transcendentals=0),
    )(*after, *args)


def three_terms(row):
    high = row.astype(BF16).astype(F32)
    rest = row - high
    mid = rest.astype(BF16).astype(F32)
    low = rest - mid
    index = lax.broadcasted_iota(jnp.int32, (16, row.shape[1]), 0)
    terms = jnp.where(
        index == 0, high, jnp.where(index == 1, mid, jnp.where(index == 2, low, 0.0))
    )
    return terms.astype(BF16)


def column_sum(refs):
    total = refs[0][...]
    for ref in refs[1:]:
        total = total + ref[...]
    return total


def chunks(table_ref, count=8):
    width = table_ref.shape[1] // count
    return [(j, pl.ds(j * width, width)) for j in range(count)]


def arrive(copies, j, ahead):
    if j == 0:
        for copy in copies[:ahead]:
            copy.start()
    copies[j].wait()
    if j + ahead < len(copies):
        copies[j + ahead].start()


def read_rows(message_ref, start, n):
    total = jnp.sum(message_ref[...], axis=0)
    pieces = [total[start + k : start + k + 1, :] for k in range(n // LANES)]
    return jnp.concatenate(pieces, axis=1)


def write_rows(message_ref, start, row):
    count = message_ref.shape[0]
    for k in range(row.shape[1] // LANES):
        piece = row[:, k * LANES : (k + 1) * LANES]
        message_ref[:, start + k, :] = jnp.broadcast_to(piece, (count, LANES))


def rows_body(
    place_ref,
    student_hbm,
    teacher_hbm,
    index_hbm,
    weight_hbm,
    rows_ref,
    x_ref,
    w_ref,
    student_ref,
    teacher_ref,
    index_ref,
    weight_ref,
    sems,
):
    copies = [
        pltpu.make_async_copy(index_hbm, index_ref, sems.at[0]),
        pltpu.make_async_copy(teacher_hbm, teacher_ref, sems.at[1]),
        pltpu.make_async_copy(student_hbm, student_ref, sems.at[2]),
        pltpu.make_async_copy(weight_hbm, weight_ref, sems.at[3]),
    ]
    for copy in copies:
        copy.start()
    for copy in copies:
        copy.wait()
    picks = index_ref[...]
    length = student_ref.shape[0]
    count = picks.shape[1]
    one_hot = (lax.broadcasted_iota(jnp.int32, (length, count), 0) == picks).astype(BF16)
    x = mm(one_hot, student_ref[...], TN)
    y = mm(one_hot, teacher_ref[...], TN)
    x_ref[...] = x
    unit_x = x * lax.rsqrt(jnp.sum(x * x, axis=1, keepdims=True) + EPS)
    unit_y = y * lax.rsqrt(jnp.sum(y * y, axis=1, keepdims=True) + EPS)
    both = jnp.concatenate([unit_y.astype(BF16), unit_x.astype(BF16)], axis=0)
    rows_ref[...] = jnp.broadcast_to(both[None], rows_ref.shape)
    lanes = w_ref.shape[1]
    spot = lax.broadcasted_iota(jnp.int32, (count, lanes), 1) - place_ref[0] * count
    spread = (spot == lax.broadcasted_iota(jnp.int32, (count, lanes), 0)).astype(BF16)
    w_ref[...] = jnp.broadcast_to(mm(weight_ref[...], spread), w_ref.shape)


def proto_body(w_hbm, unit_hbm, first_ref, inverse_ref, w_ref, unit_ref, in_sems, out_sems):
    count = unit_ref.shape[0]
    copies = [
        pltpu.make_async_copy(w_hbm.at[:, cols], w_ref.at[:, cols], in_sems.at[j])
        for j, cols in chunks(w_ref, count)
    ]
    stores = []
    for j, cols in chunks(w_ref, count):
        arrive(copies, j, 4)
        w = w_ref[:, cols].astype(F32)
        inverse = lax.rsqrt(jnp.sum(w * w, axis=0, keepdims=True) + EPS)
        inverse_ref[pl.ds(j, 1), :] = inverse
        unit = (w * inverse).astype(BF16)
        unit_ref[j] = unit
        if j < first_ref.shape[0]:
            first_ref[j] = unit
        store = pltpu.make_async_copy(unit_ref.at[j], unit_hbm.at[j], out_sems.at[j])
        store.start()
        stores.append(store)
    for store in stores:
        store.wait()


def table_body(rows_ref, first_ref, unit_hbm, table_ref, unit_ref, sums_ref, sems):
    skip, count = first_ref.shape[0], unit_ref.shape[0]
    copies = [
        pltpu.make_async_copy(unit_hbm.at[j], unit_ref.at[j], sems.at[j]) for j in range(count)
    ]
    for copy in copies[skip:] + copies[:skip]:
        copy.start()
    half = rows_ref.shape[1] // 2
    teacher = rows_ref[:, :half, :].reshape(-1, rows_ref.shape[2])
    for j, cols in chunks(table_ref, count):
        if j < skip:
            unit = first_ref[j]
        else:
            copies[j].wait()
            unit = unit_ref[j]
        table = jnp.exp(mm(teacher, unit) * (1.0 / TEACHER_TEMP)).astype(BF16)
        table_ref[:, cols] = table
        sums_ref[pl.ds(j, 1), :] = jnp.sum(table.astype(F32), axis=0, keepdims=True)
    for copy in copies[:skip]:
        copy.wait()


def row_pass_body(parts, *refs):
    sums_refs, table_ref, extra_refs, out_ref = refs[:parts], refs[parts], refs[parts + 1 : -1], refs[-1]
    scale = 1.0 / column_sum(sums_refs)
    n = table_ref.shape[0]
    total = jnp.zeros((16, n), F32)
    for j, cols in chunks(table_ref):
        total += mm(three_terms(scale[j : j + 1, :]), table_ref[:, cols], NT)
    write_rows(out_ref, 0, jnp.sum(total, axis=0, keepdims=True))
    write_rows(out_ref, n // LANES, column_sum(extra_refs)[0:1, :])


def col_pass_body(message_ref, table_ref, out_ref):
    terms = three_terms(1.0 / read_rows(message_ref, 0, table_ref.shape[0]))
    for j, cols in chunks(table_ref):
        out_ref[pl.ds(j, 1), :] = jnp.sum(mm(terms, table_ref[:, cols]), axis=0, keepdims=True)


def student_body(first, rows_ref, unit_ref, table_ref, sums_ref, feature_ref, *turned_refs):
    count = PIECES[first]
    start = sum(PIECES[:first])
    half = rows_ref.shape[1] // 2
    student = rows_ref[:, half:, :].reshape(-1, rows_ref.shape[2])
    total = jnp.zeros((16, student.shape[0]), F32)
    for j, cols in chunks(table_ref, count):
        unit = unit_ref[start + j]
        table = jnp.exp(mm(student, unit) * (1.0 / STUDENT_TEMP)).astype(BF16)
        table_ref[:, cols] = table
        total += mm(jnp.ones((16, table.shape[1]), BF16), table, NT)
        part = mm(unit, table, NT)
        if j == 0:
            feature_ref[...] = part
        else:
            feature_ref[...] += part
    sums_ref[...] = total[0:8]
    for turned_ref in turned_refs:
        d = student.shape[1]
        eye = (
            lax.broadcasted_iota(jnp.int32, (d, d), 0)
            == lax.broadcasted_iota(jnp.int32, (d, d), 1)
        ).astype(BF16)
        turned_ref[...] = mm(eye, student, NT).astype(BF16)


def last_row_pass_body(parts, *refs):
    sums_refs, table_ref, unit_ref = refs[:parts], refs[parts], refs[parts + 1]
    *extra_refs, out_ref, feature_ref = refs[parts + 2 :]
    scale = 1.0 / column_sum(sums_refs)
    n, d = table_ref.shape[0], unit_ref.shape[1]
    total = jnp.zeros((16, n), F32)
    for j, cols in chunks(table_ref):
        factor = scale[j : j + 1, :]
        scaled = (unit_ref[j].astype(F32) * factor).astype(BF16)
        left = jnp.concatenate([scaled, three_terms(factor)], axis=0)
        part = mm(left, table_ref[:, cols], NT)
        total += part[d:]
        if j == 0:
            feature_ref[...] = part[:d]
        else:
            feature_ref[...] += part[:d]
    write_rows(out_ref, 0, jnp.sum(total, axis=0, keepdims=True))
    write_rows(out_ref, n // LANES, column_sum(extra_refs)[0:1, :])


def row_factors(first_ref, last_ref, n):
    tile = n // LANES
    return read_rows(first_ref, tile, n), read_rows(last_ref, tile, n), read_rows(last_ref, 0, n)


def head_body(parts, *refs):
    place_ref, first_ref, last_ref = refs[:3]
    sums_refs = refs[3 : 3 + parts]
    turned_ref, inverse_ref, codes_ref, *piece_refs, w_ref = refs[3 + parts : -7]
    own_hbm, own_near_ref, keep_ref, near_ref, turn_ref, own_ref, sems = refs[-7:]
    x, core = place_ref[1], place_ref[2]
    share = near_ref.shape[1]
    chips = near_ref.shape[0] + 1
    spots = []
    for k in range(chips):
        for side in (core, 1 - core):
            spots.append(pl.ds(pl.multiple_of((2 * (x ^ k) + side) * share, share), share))
    for m, spot in enumerate(spots):
        turn_ref[pl.ds(m * share, share), :] = turned_ref[spot, :]
    weights, exp_total, total = row_factors(first_ref, last_ref, codes_ref.shape[0])
    turned = turn_ref[...].astype(F32)
    left_probs = (turned * (weights / exp_total * (1.0 / STUDENT_TEMP))).astype(BF16)
    left_codes = (turned * (weights / total * (1.0 / STUDENT_TEMP))).astype(BF16)
    scale = 1.0 / column_sum(sums_refs)
    where = [(p, at) for p, size in enumerate(PIECES) for at in range(size)]
    stores = []
    for j, cols in chunks(codes_ref):
        piece, at = where[j]
        width = codes_ref.shape[1] // len(where)
        head = mm(left_probs, piece_refs[piece][:, pl.ds(at * width, width)]) - scale[
            j : j + 1, :
        ] * mm(left_codes, codes_ref[:, cols])
        inverse = inverse_ref[pl.ds(j, 1), :]
        w = jnp.concatenate([w_ref[spot, cols] for spot in spots], axis=0)
        unit = w.astype(F32) * inverse
        inner = jnp.sum(unit * head, axis=0, keepdims=True)
        grad = inverse * (head - unit * inner)
        own_ref[:, cols] = grad[0:share]
        store = pltpu.make_async_copy(own_ref.at[:, cols], own_hbm.at[:, cols], sems.at[j])
        store.start()
        stores.append(store)
        own_near_ref[:, cols] = grad[share : 2 * share].astype(BF16)
        for k in range(1, chips):
            low = 2 * k * share
            keep_ref[k - 1, :, cols] = grad[low : low + share].astype(BF16)
            near_ref[k - 1, :, cols] = grad[low + share : low + 2 * share].astype(BF16)
    for store in stores:
        store.wait()


def pair_body(keep_ref, near_ref, *pair_refs):
    for k, pair_ref in enumerate(pair_refs):
        pair_ref[...] = (keep_ref[k].astype(F32) + near_ref[k].astype(F32)).astype(BF16)


def own_sum_body(own_ref, near_ref, tails_ref, out_ref, tails_out_ref):
    out_ref[...] = own_ref[...] + near_ref[...].astype(F32)
    tails_out_ref[...] = tails_ref[...]


def final_body(own_ref, tails_ref, *refs):
    *far_refs, out_ref, loss_ref = refs
    total = own_ref[...]
    for far_ref in far_refs:
        total = total + far_ref[...].astype(F32)
    out_ref[...] = total
    terms = jnp.sum(tails_ref[...], axis=0)[0:1, :]
    lane = lax.broadcasted_iota(jnp.int32, terms.shape, 1)
    part = jnp.sum(jnp.where(lane < 3, terms, 0.0), axis=1, keepdims=True)
    count = jnp.sum(jnp.where((lane >= 3) & (lane < 6), terms, 0.0), axis=1, keepdims=True)
    loss_ref[...] = part / count


def owner_body(sent_ref, x_ref, grad_ref, tail_ref):
    sent = jnp.sum(sent_ref[...].astype(F32), axis=0)
    own = x_ref.shape[0]
    x = x_ref[...]
    feature = sent[:own]
    inverse = lax.rsqrt(jnp.sum(x * x, axis=1, keepdims=True) + EPS)
    unit = x * inverse
    grad_ref[...] = inverse * (feature - unit * jnp.sum(unit * feature, axis=1, keepdims=True))
    tail_ref[...] = jnp.broadcast_to(sent[own : own + 8, :LANES][None], tail_ref.shape)


def split(value):
    row = jnp.broadcast_to(value, (8, LANES))
    high = row.astype(BF16).astype(F32)
    mid = (row - high).astype(BF16).astype(F32)
    return [term[0:1, 0:1] for term in (high, mid, row - high - mid)]


def feature_body(first_ref, last_ref, codes_ref, turned_ref, *refs):
    *probs_refs, out_ref = refs
    n = codes_ref.shape[1]
    count = out_ref.shape[0]
    own = n // count
    weights, exp_total, total = row_factors(first_ref, last_ref, n)
    codes = codes_ref[...]
    over = weights / total * (1.0 / STUDENT_TEMP)
    probs = column_sum(probs_refs) * (weights / exp_total * (1.0 / STUDENT_TEMP))
    feature = (probs - codes * over).T.astype(BF16)
    out_ref[:, :own, :] = feature.reshape(count, own, feature.shape[1])
    share = 1.0 / count
    cross = jnp.sum(turned_ref[...].astype(F32) * codes, axis=0, keepdims=True)
    part = jnp.sum(weights * jnp.log(exp_total) * share - over * cross)
    tail = (out_ref.shape[1] - own, out_ref.shape[2])
    lane = lax.broadcasted_iota(jnp.int32, tail, 1)
    row = jnp.zeros(tail, F32)
    for k, term in enumerate(split(part) + split(jnp.sum(weights) * share)):
        row = jnp.where(lane == k, term, row)
    out_ref[:, own:, :] = jnp.broadcast_to(row.astype(BF16)[None], (count,) + tail)


def on_device(student_feats, teacher_feats, proto_weight, mask_index, row_weight):
    n_patch, n_proto = lax.axis_size("patch"), lax.axis_size("proto")
    d, protos = proto_weight.shape
    length = student_feats.shape[0]
    own = mask_index.shape[0]
    rows = own * n_proto
    chips = n_patch // 2
    share = d // n_patch
    width = protos // 8
    patch, proto = lax.axis_index("patch"), lax.axis_index("proto")
    place = jnp.stack([proto, patch // 2, patch % 2]).astype(jnp.int32)
    product = 2 * rows * d * protos

    def exchange(array, axis):
        return lax.all_to_all(array, axis, 0, 0)

    def hop(array, bits):
        return lax.ppermute(array, "patch", [(i, i ^ bits) for i in range(n_patch)])

    own_rows, x_rows, own_weights = call(
        rows_body,
        "own_rows",
        (
            shape((n_proto, 2 * own, d), BF16),
            shape((own, d), F32),
            shape((8, rows), F32),
        ),
        (place, student_feats, teacher_feats, mask_index[None, :], row_weight[None, :]),
        1 << 28,
        specs=[SMEM, HBM, HBM, HBM, HBM],
        scratch=[
            pltpu.VMEM((length, d), BF16),
            pltpu.VMEM((length, d), BF16),
            pltpu.VMEM((1, own), jnp.int32),
            pltpu.VMEM((1, own), BF16),
            pltpu.SemaphoreType.DMA((4,)),
        ],
    )
    all_rows = exchange(own_rows, "proto")
    unit, unit_first, inverse = call(
        proto_body,
        "proto_unit",
        (
            pltpu.HBM((8, d, width), BF16),
            shape((FIRST, d, width), BF16),
            shape((8, width), F32),
        ),
        (proto_weight,),
        product,
        specs=[HBM],
        scratch=[
            pltpu.VMEM((d, protos), BF16),
            pltpu.VMEM((8, d, width), BF16),
            pltpu.SemaphoreType.DMA((8,)),
            pltpu.SemaphoreType.DMA((8,)),
        ],
    )
    codes, unit, sums = call(
        table_body,
        "teacher_table",
        (
            shape((rows, protos), BF16),
            shape((8, d, width), BF16),
            shape((8, width), F32),
        ),
        (all_rows, unit_first, unit),
        2 * product,
        specs=[VMEM, VMEM, HBM],
        scratch=[pltpu.SemaphoreType.DMA((8,))],
    )

    messages = []
    pieces = []
    for sweep in range(SK_ITERS):
        sums = sums + hop(sums, 1)
        parts = [sums] + [hop(sums, 2 * k) for k in range(1, chips)]
        span = PIECES[sweep] * width
        last = sweep == SK_ITERS - 1
        pieces.append(
            call(
                functools.partial(student_body, sweep),
                "student_table",
                (shape((rows, span), BF16), shape((8, rows), F32), shape((d, rows), F32))
                + ((shape((d, rows), BF16),) if last else ()),
                (all_rows, unit),
                product,
                after=(sums,),
            )
        )
        if last:
            part, codes_feature = call(
                functools.partial(last_row_pass_body, chips),
                "last_row_pass",
                (shape((n_proto, 8, LANES), F32), shape((d, rows), F32)),
                (*parts, codes, unit, *[piece[1] for piece in pieces]),
                product,
            )
        else:
            part = call(
                functools.partial(row_pass_body, chips),
                "row_pass",
                shape((n_proto, 8, LANES), F32),
                (*parts, codes, own_weights),
                product,
                after=(pieces[-1][1],),
            )
        messages.append(exchange(part, "proto"))
        if not last:
            sums = call(
                col_pass_body,
                "col_pass",
                shape((8, width), F32),
                (messages[-1], codes),
                product // 2,
            )

    turned = pieces[-1][3]
    factors = (messages[0], messages[-1])
    own_block, own_near, keep, near = call(
        functools.partial(head_body, chips),
        "head",
        (
            pltpu.HBM((share, protos), F32),
            shape((share, protos), BF16),
            shape((chips - 1, share, protos), BF16),
            shape((chips - 1, share, protos), BF16),
        ),
        (
            place,
            *factors,
            *parts,
            turned,
            inverse,
            codes,
            *[piece[0] for piece in pieces],
            proto_weight,
        ),
        4 * product,
        specs=[SMEM] + [VMEM] * (len(factors) + chips + 4 + len(pieces)),
        scratch=[
            pltpu.VMEM((d, rows), BF16),
            pltpu.VMEM((share, protos), F32),
            pltpu.SemaphoreType.DMA((8,)),
        ],
    )
    feature_part = call(
        feature_body,
        "feature",
        shape((n_proto, own + 16, d), BF16),
        (*factors, codes_feature, turned, *[piece[2] for piece in pieces]),
        product // 4,
        after=(keep,),
    )
    pairs = call(
        pair_body,
        "pair_sums",
        tuple(shape((share, protos), BF16) for _ in range(chips - 1)),
        (keep, hop(near, 1)),
        product // 8,
        after=(feature_part,),
    )
    far = [hop(pairs[k - 1], 2 * k) for k in sorted(range(1, chips), key=lambda k: k % 2)]
    grad_student, tails = call(
        owner_body,
        "owner",
        (shape((own, d), F32), shape((n_patch, 8, LANES), F32)),
        (exchange(feature_part, "proto"), x_rows),
        product // 8,
    )
    own_sum, tails = call(
        own_sum_body,
        "own_sum",
        (shape((share, protos), F32), shape((n_patch, 8, LANES), F32)),
        (own_block, hop(own_near, 1), tails),
        product // 8,
    )
    grad_proto, loss = call(
        final_body,
        "assemble",
        (shape((share, protos), F32), shape((1, 1), F32)),
        (own_sum, exchange(tails, "patch"), *far),
        product // 4,
    )
    return (grad_student, grad_proto, loss.reshape(()))


def solution(mesh):
    both = ("patch", "proto")
    in_specs = (P(both, None), P(both, None), P(None, "proto"), P(both), P(both))
    out_specs = (P(both, None), P("patch", "proto"), P())
    return jax.shard_map(
        on_device, mesh=mesh, in_specs=in_specs, out_specs=out_specs, check_vma=False
    )
```

```python
import functools

import jax
import jax.numpy as jnp
from jax import lax
from jax.experimental import pallas as pl
from jax.experimental.pallas import tpu as pltpu
from jax.sharding import PartitionSpec as P

SK_ITERS = 3
EPS = 1e-06
TEACHER_TEMP = 0.07
STUDENT_TEMP = 0.1
F32 = jnp.float32
BF16 = jnp.bfloat16
LANES = 128
PIECES = (3, 3, 2)
FIRST = 2
PARTS = (6, 2)
VMEM_LIMIT = 20 * 1024 * 1024

NN = (((1,), (0,)), ((), ()))
NT = (((1,), (1,)), ((), ()))
TN = (((0,), (0,)), ((), ()))
SMEM = pl.BlockSpec(memory_space=pltpu.SMEM)
VMEM = pl.BlockSpec(memory_space=pltpu.VMEM)
ANY = pl.BlockSpec(memory_space=pl.ANY)
HBM = pl.BlockSpec(memory_space=pltpu.HBM)


def mm(a, b, dims=NN):
    return lax.dot_general(a, b, dims, preferred_element_type=F32)


def shape(dims, dtype):
    return jax.ShapeDtypeStruct(dims, dtype)


def call(body, name, out_shape, args, flops, specs=None, after=(), scratch=(), limit=VMEM_LIMIT):
    specs = specs or [VMEM] * len(args)
    skip = len(after)
    args = [
        pltpu.with_memory_space_constraint(arg, pltpu.HBM) if spec is HBM else arg
        for arg, spec in zip(args, specs)
    ]

    def ordered(*refs):
        body(*refs[skip:])

    def out_spec(out):
        return VMEM if isinstance(out, jax.ShapeDtypeStruct) else HBM

    many = isinstance(out_shape, tuple)
    return pl.pallas_call(
        ordered,
        name=name,
        out_shape=out_shape,
        in_specs=[ANY] * skip + specs,
        out_specs=tuple(map(out_spec, out_shape)) if many else out_spec(out_shape),
        scratch_shapes=list(scratch),
        compiler_params=pltpu.CompilerParams(vmem_limit_bytes=limit),
        cost_estimate=pl.CostEstimate(flops=flops, bytes_accessed=1 << 16, transcendentals=0),
    )(*after, *args)


def three_terms(row):
    high = row.astype(BF16).astype(F32)
    rest = row - high
    mid = rest.astype(BF16).astype(F32)
    low = rest - mid
    index = lax.broadcasted_iota(jnp.int32, (16, row.shape[1]), 0)
    terms = jnp.where(
        index == 0, high, jnp.where(index == 1, mid, jnp.where(index == 2, low, 0.0))
    )
    return terms.astype(BF16)


def column_sum(refs):
    total = refs[0][...]
    for ref in refs[1:]:
        total = total + ref[...]
    return total


def chunks(table_ref, count=8):
    width = table_ref.shape[1] // count
    return [(j, pl.ds(j * width, width)) for j in range(count)]


def arrive(copies, j, ahead):
    if j == 0:
        for copy in copies[:ahead]:
            copy.start()
    copies[j].wait()
    if j + ahead < len(copies):
        copies[j + ahead].start()


def read_rows(message_ref, start, n):
    total = jnp.sum(message_ref[...], axis=0)
    pieces = [total[start + k : start + k + 1, :] for k in range(n // LANES)]
    return jnp.concatenate(pieces, axis=1)


def write_rows(message_ref, start, row):
    count = message_ref.shape[0]
    for k in range(row.shape[1] // LANES):
        piece = row[:, k * LANES : (k + 1) * LANES]
        message_ref[:, start + k, :] = jnp.broadcast_to(piece, (count, LANES))


def rows_body(
    place_ref,
    student_hbm,
    teacher_hbm,
    index_hbm,
    weight_hbm,
    rows_ref,
    x_ref,
    w_ref,
    student_ref,
    teacher_ref,
    index_ref,
    weight_ref,
    sems,
):
    copies = [
        pltpu.make_async_copy(index_hbm, index_ref, sems.at[0]),
        pltpu.make_async_copy(teacher_hbm, teacher_ref, sems.at[1]),
        pltpu.make_async_copy(student_hbm, student_ref, sems.at[2]),
        pltpu.make_async_copy(weight_hbm, weight_ref, sems.at[3]),
    ]
    for copy in copies:
        copy.start()
    for copy in copies:
        copy.wait()
    picks = index_ref[...]
    length = student_ref.shape[0]
    count = picks.shape[1]
    one_hot = (lax.broadcasted_iota(jnp.int32, (length, count), 0) == picks).astype(BF16)
    x = mm(one_hot, student_ref[...], TN)
    y = mm(one_hot, teacher_ref[...], TN)
    x_ref[...] = x
    unit_x = x * lax.rsqrt(jnp.sum(x * x, axis=1, keepdims=True) + EPS)
    unit_y = y * lax.rsqrt(jnp.sum(y * y, axis=1, keepdims=True) + EPS)
    both = jnp.concatenate([unit_y.astype(BF16), unit_x.astype(BF16)], axis=0)
    rows_ref[...] = jnp.broadcast_to(both[None], rows_ref.shape)
    lanes = w_ref.shape[1]
    spot = lax.broadcasted_iota(jnp.int32, (count, lanes), 1) - place_ref[0] * count
    spread = (spot == lax.broadcasted_iota(jnp.int32, (count, lanes), 0)).astype(BF16)
    w_ref[...] = jnp.broadcast_to(mm(weight_ref[...], spread), w_ref.shape)


def proto_body(w_hbm, unit_hbm, first_ref, inverse_ref, w_ref, unit_ref, in_sems, out_sems):
    count = unit_ref.shape[0]
    copies = [
        pltpu.make_async_copy(w_hbm.at[:, cols], w_ref.at[:, cols], in_sems.at[j])
        for j, cols in chunks(w_ref, count)
    ]
    stores = []
    for j, cols in chunks(w_ref, count):
        arrive(copies, j, 4)
        w = w_ref[:, cols].astype(F32)
        inverse = lax.rsqrt(jnp.sum(w * w, axis=0, keepdims=True) + EPS)
        inverse_ref[pl.ds(j, 1), :] = inverse
        unit = (w * inverse).astype(BF16)
        unit_ref[j] = unit
        if j < first_ref.shape[0]:
            first_ref[j] = unit
        store = pltpu.make_async_copy(unit_ref.at[j], unit_hbm.at[j], out_sems.at[j])
        store.start()
        stores.append(store)
    for store in stores:
        store.wait()


def table_body(rows_ref, first_ref, unit_hbm, table_ref, unit_ref, sums_ref, sems):
    skip, count = first_ref.shape[0], unit_ref.shape[0]
    copies = [
        pltpu.make_async_copy(unit_hbm.at[j], unit_ref.at[j], sems.at[j]) for j in range(count)
    ]
    for copy in copies[skip:] + copies[:skip]:
        copy.start()
    half = rows_ref.shape[1] // 2
    teacher = rows_ref[:, :half, :].reshape(-1, rows_ref.shape[2])
    for j, cols in chunks(table_ref, count):
        if j < skip:
            unit = first_ref[j]
        else:
            copies[j].wait()
            unit = unit_ref[j]
        table = jnp.exp(mm(teacher, unit) * (1.0 / TEACHER_TEMP)).astype(BF16)
        table_ref[:, cols] = table
        sums_ref[pl.ds(j, 1), :] = jnp.sum(table.astype(F32), axis=0, keepdims=True)
    for copy in copies[:skip]:
        copy.wait()


def row_pass_body(parts, *refs):
    sums_refs, table_ref, extra_refs, out_ref = refs[:parts], refs[parts], refs[parts + 1 : -1], refs[-1]
    scale = 1.0 / column_sum(sums_refs)
    n = table_ref.shape[0]
    total = jnp.zeros((16, n), F32)
    for j, cols in chunks(table_ref):
        total += mm(three_terms(scale[j : j + 1, :]), table_ref[:, cols], NT)
    write_rows(out_ref, 0, jnp.sum(total, axis=0, keepdims=True))
    write_rows(out_ref, n // LANES, column_sum(extra_refs)[0:1, :])


def col_pass_body(message_ref, table_ref, out_ref):
    terms = three_terms(1.0 / read_rows(message_ref, 0, table_ref.shape[0]))
    for j, cols in chunks(table_ref):
        out_ref[pl.ds(j, 1), :] = jnp.sum(mm(terms, table_ref[:, cols]), axis=0, keepdims=True)


def student_body(first, rows_ref, unit_ref, table_ref, sums_ref, feature_ref, *turned_refs):
    count = PIECES[first]
    start = sum(PIECES[:first])
    half = rows_ref.shape[1] // 2
    student = rows_ref[:, half:, :].reshape(-1, rows_ref.shape[2])
    total = jnp.zeros((16, student.shape[0]), F32)
    for j, cols in chunks(table_ref, count):
        unit = unit_ref[start + j]
        table = jnp.exp(mm(student, unit) * (1.0 / STUDENT_TEMP)).astype(BF16)
        table_ref[:, cols] = table
        total += mm(jnp.ones((16, table.shape[1]), BF16), table, NT)
        part = mm(unit, table, NT)
        if j == 0:
            feature_ref[...] = part
        else:
            feature_ref[...] += part
    sums_ref[...] = total[0:8]
    for turned_ref in turned_refs:
        d = student.shape[1]
        eye = (
            lax.broadcasted_iota(jnp.int32, (d, d), 0)
            == lax.broadcasted_iota(jnp.int32, (d, d), 1)
        ).astype(BF16)
        turned_ref[...] = mm(eye, student, NT).astype(BF16)


def last_row_pass_body(parts, *refs):
    sums_refs, table_ref, unit_ref = refs[:parts], refs[parts], refs[parts + 1]
    *extra_refs, out_ref, feature_ref = refs[parts + 2 :]
    scale = 1.0 / column_sum(sums_refs)
    n, d = table_ref.shape[0], unit_ref.shape[1]
    total = jnp.zeros((16, n), F32)
    for j, cols in chunks(table_ref):
        factor = scale[j : j + 1, :]
        scaled = (unit_ref[j].astype(F32) * factor).astype(BF16)
        left = jnp.concatenate([scaled, three_terms(factor)], axis=0)
        part = mm(left, table_ref[:, cols], NT)
        total += part[d:]
        if j == 0:
            feature_ref[...] = part[:d]
        else:
            feature_ref[...] += part[:d]
    write_rows(out_ref, 0, jnp.sum(total, axis=0, keepdims=True))
    write_rows(out_ref, n // LANES, column_sum(extra_refs)[0:1, :])


def row_factors(first_ref, last_ref, n):
    tile = n // LANES
    return read_rows(first_ref, tile, n), read_rows(last_ref, tile, n), read_rows(last_ref, 0, n)


def head_body(first, parts, *refs):
    place_ref, first_ref, last_ref = refs[:3]
    sums_refs = refs[3 : 3 + parts]
    turned_ref, inverse_ref, codes_ref, *piece_refs, w_ref = refs[3 + parts : -6]
    own_hbm, keep_ref, near_ref, turn_ref, own_ref, sems = refs[-6:]
    x, core = place_ref[1], place_ref[2]
    chips, share = near_ref.shape[:2]
    width = inverse_ref.shape[1]
    spots = []
    for k in range(chips):
        for side in (core, 1 - core):
            spots.append(pl.ds(pl.multiple_of((2 * (x ^ k) + side) * share, share), share))
    for m, spot in enumerate(spots):
        turn_ref[pl.ds(m * share, share), :] = turned_ref[spot, :]
    weights, exp_total, total = row_factors(first_ref, last_ref, codes_ref.shape[0])
    turned = turn_ref[...].astype(F32)
    left_probs = (turned * (weights / exp_total * (1.0 / STUDENT_TEMP))).astype(BF16)
    left_codes = (turned * (weights / total * (1.0 / STUDENT_TEMP))).astype(BF16)
    scale = 1.0 / column_sum(sums_refs)
    where = [(p, at) for p, size in enumerate(PIECES) for at in range(size)]
    stores = []
    for j, cols in chunks(own_ref, own_ref.shape[1] // width):
        row = first + j
        here = pl.ds(row * width, width)
        piece, at = where[row]
        inverse = inverse_ref[pl.ds(row, 1), :]
        head = inverse * mm(left_probs, piece_refs[piece][:, pl.ds(at * width, width)]) - (
            inverse * scale[row : row + 1, :]
        ) * mm(left_codes, codes_ref[:, here])
        w = jnp.concatenate([w_ref[spot, here] for spot in spots], axis=0).astype(F32)
        inner = jnp.sum(w * head, axis=0, keepdims=True)
        grad = head - w * (inverse * inverse * inner)
        own_ref[:, cols] = grad[0:share]
        store = pltpu.make_async_copy(own_ref.at[:, cols], own_hbm.at[:, cols], sems.at[j])
        store.start()
        stores.append(store)
        for k in range(chips):
            low = 2 * k * share
            if k:
                keep_ref[k - 1, :, cols] = grad[low : low + share].astype(BF16)
            near_ref[k, :, cols] = grad[low + share : low + 2 * share].astype(BF16)
    for store in stores:
        store.wait()


def pair_body(*refs):
    count = len(PARTS)
    start = 0
    for part in range(count):
        keep_ref, near_ref = refs[2 * part : 2 * part + 2]
        span = keep_ref.shape[2]
        for k, pair_ref in enumerate(refs[2 * count :]):
            total = keep_ref[k].astype(F32) + near_ref[k + 1].astype(F32)
            pair_ref[:, start : start + span] = total.astype(BF16)
        start += span


def own_sum_body(tails_ref, *refs):
    count = len(PARTS)
    start = 0
    for part in range(count):
        own_ref, near_ref = refs[2 * part : 2 * part + 2]
        span = own_ref.shape[1]
        refs[-2][:, start : start + span] = own_ref[...] + near_ref[0].astype(F32)
        start += span
    refs[-1][...] = tails_ref[...]


def final_body(own_ref, tails_ref, *refs):
    *far_refs, out_ref, loss_ref = refs
    total = own_ref[...]
    for far_ref in far_refs:
        total = total + far_ref[...].astype(F32)
    out_ref[...] = total
    terms = jnp.sum(tails_ref[...], axis=0)[0:1, :]
    lane = lax.broadcasted_iota(jnp.int32, terms.shape, 1)
    part = jnp.sum(jnp.where(lane < 3, terms, 0.0), axis=1, keepdims=True)
    count = jnp.sum(jnp.where((lane >= 3) & (lane < 6), terms, 0.0), axis=1, keepdims=True)
    loss_ref[...] = part / count


def owner_body(sent_ref, x_ref, grad_ref, tail_ref):
    sent = jnp.sum(sent_ref[...].astype(F32), axis=0)
    own = x_ref.shape[0]
    x = x_ref[...]
    feature = sent[:own]
    inverse = lax.rsqrt(jnp.sum(x * x, axis=1, keepdims=True) + EPS)
    unit = x * inverse
    grad_ref[...] = inverse * (feature - unit * jnp.sum(unit * feature, axis=1, keepdims=True))
    tail_ref[...] = jnp.broadcast_to(sent[own : own + 8, :LANES][None], tail_ref.shape)


def split(value):
    row = jnp.broadcast_to(value, (8, LANES))
    high = row.astype(BF16).astype(F32)
    mid = (row - high).astype(BF16).astype(F32)
    return [term[0:1, 0:1] for term in (high, mid, row - high - mid)]


def feature_body(first_ref, last_ref, codes_ref, turned_ref, *refs):
    *probs_refs, out_ref = refs
    n = codes_ref.shape[1]
    count = out_ref.shape[0]
    own = n // count
    weights, exp_total, total = row_factors(first_ref, last_ref, n)
    codes = codes_ref[...]
    over = weights / total * (1.0 / STUDENT_TEMP)
    probs = column_sum(probs_refs) * (weights / exp_total * (1.0 / STUDENT_TEMP))
    feature = (probs - codes * over).T.astype(BF16)
    out_ref[:, :own, :] = feature.reshape(count, own, feature.shape[1])
    share = 1.0 / count
    cross = jnp.sum(turned_ref[...].astype(F32) * codes, axis=0, keepdims=True)
    part = jnp.sum(weights * jnp.log(exp_total) * share - over * cross)
    tail = (out_ref.shape[1] - own, out_ref.shape[2])
    lane = lax.broadcasted_iota(jnp.int32, tail, 1)
    row = jnp.zeros(tail, F32)
    for k, term in enumerate(split(part) + split(jnp.sum(weights) * share)):
        row = jnp.where(lane == k, term, row)
    out_ref[:, own:, :] = jnp.broadcast_to(row.astype(BF16)[None], (count,) + tail)


def on_device(student_feats, teacher_feats, proto_weight, mask_index, row_weight):
    n_patch, n_proto = lax.axis_size("patch"), lax.axis_size("proto")
    d, protos = proto_weight.shape
    length = student_feats.shape[0]
    own = mask_index.shape[0]
    rows = own * n_proto
    chips = n_patch // 2
    share = d // n_patch
    width = protos // 8
    patch, proto = lax.axis_index("patch"), lax.axis_index("proto")
    place = jnp.stack([proto, patch // 2, patch % 2]).astype(jnp.int32)
    product = 2 * rows * d * protos

    def exchange(array, axis):
        return lax.all_to_all(array, axis, 0, 0)

    def hop(array, bits):
        return lax.ppermute(array, "patch", [(i, i ^ bits) for i in range(n_patch)])

    own_rows, x_rows, own_weights = call(
        rows_body,
        "own_rows",
        (
            shape((n_proto, 2 * own, d), BF16),
            shape((own, d), F32),
            shape((8, rows), F32),
        ),
        (place, student_feats, teacher_feats, mask_index[None, :], row_weight[None, :]),
        1 << 28,
        specs=[SMEM, HBM, HBM, HBM, HBM],
        scratch=[
            pltpu.VMEM((length, d), BF16),
            pltpu.VMEM((length, d), BF16),
            pltpu.VMEM((1, own), jnp.int32),
            pltpu.VMEM((1, own), BF16),
            pltpu.SemaphoreType.DMA((4,)),
        ],
    )
    all_rows = exchange(own_rows, "proto")
    unit, unit_first, inverse = call(
        proto_body,
        "proto_unit",
        (
            pltpu.HBM((8, d, width), BF16),
            shape((FIRST, d, width), BF16),
            shape((8, width), F32),
        ),
        (proto_weight,),
        product,
        specs=[HBM],
        scratch=[
            pltpu.VMEM((d, protos), BF16),
            pltpu.VMEM((8, d, width), BF16),
            pltpu.SemaphoreType.DMA((8,)),
            pltpu.SemaphoreType.DMA((8,)),
        ],
    )
    codes, unit, sums = call(
        table_body,
        "teacher_table",
        (
            shape((rows, protos), BF16),
            shape((8, d, width), BF16),
            shape((8, width), F32),
        ),
        (all_rows, unit_first, unit),
        2 * product,
        specs=[VMEM, VMEM, HBM],
        scratch=[pltpu.SemaphoreType.DMA((8,))],
    )

    messages = []
    pieces = []
    for sweep in range(SK_ITERS):
        sums = sums + hop(sums, 1)
        parts = [sums] + [hop(sums, 2 * k) for k in range(1, chips)]
        span = PIECES[sweep] * width
        last = sweep == SK_ITERS - 1
        pieces.append(
            call(
                functools.partial(student_body, sweep),
                "student_table",
                (shape((rows, span), BF16), shape((8, rows), F32), shape((d, rows), F32))
                + ((shape((d, rows), BF16),) if last else ()),
                (all_rows, unit),
                product,
                after=(sums,),
            )
        )
        if last:
            part, codes_feature = call(
                functools.partial(last_row_pass_body, chips),
                "last_row_pass",
                (shape((n_proto, 8, LANES), F32), shape((d, rows), F32)),
                (*parts, codes, unit, *[piece[1] for piece in pieces]),
                product,
            )
        else:
            part = call(
                functools.partial(row_pass_body, chips),
                "row_pass",
                shape((n_proto, 8, LANES), F32),
                (*parts, codes, own_weights),
                product,
                after=(pieces[-1][1],),
            )
        messages.append(exchange(part, "proto"))
        if not last:
            sums = call(
                col_pass_body,
                "col_pass",
                shape((8, width), F32),
                (messages[-1], codes),
                product // 2,
            )

    turned = pieces[-1][3]
    factors = (messages[0], messages[-1])
    heads = []
    for index, count in enumerate(PARTS):
        span = count * width
        heads.append(
            call(
                functools.partial(head_body, sum(PARTS[:index]), chips),
                "head",
                (
                    pltpu.HBM((share, span), F32),
                    shape((chips - 1, share, span), BF16),
                    shape((chips, share, span), BF16),
                ),
                (
                    place,
                    *factors,
                    *parts,
                    turned,
                    inverse,
                    codes,
                    *[piece[0] for piece in pieces],
                    proto_weight,
                ),
                2 * product,
                specs=[SMEM] + [VMEM] * (len(factors) + chips + 4 + len(pieces)),
                after=(heads[-1][1],) if heads else (),
                scratch=[
                    pltpu.VMEM((d, rows), BF16),
                    pltpu.VMEM((share, span), F32),
                    pltpu.SemaphoreType.DMA((count,)),
                ],
            )
        )
    feature_part = call(
        feature_body,
        "feature",
        shape((n_proto, own + 16, d), BF16),
        (*factors, codes_feature, turned, *[piece[2] for piece in pieces]),
        product // 4,
        after=(heads[-1][1],),
    )
    ends, nears = [], []
    for own_block, keep, near in heads:
        near = hop(near, 1)
        ends += [keep, near]
        nears += [own_block, near]
    pairs = call(
        pair_body,
        "pair_sums",
        tuple(shape((share, protos), BF16) for _ in range(chips - 1)),
        tuple(ends),
        product // 8,
        after=(feature_part,),
    )
    far = [hop(pairs[k - 1], 2 * k) for k in sorted(range(1, chips), key=lambda k: k % 2)]
    grad_student, tails = call(
        owner_body,
        "owner",
        (shape((own, d), F32), shape((n_patch, 8, LANES), F32)),
        (exchange(feature_part, "proto"), x_rows),
        product // 8,
    )
    own_sum, tails = call(
        own_sum_body,
        "own_sum",
        (shape((share, protos), F32), shape((n_patch, 8, LANES), F32)),
        (tails, *nears),
        product // 8,
    )
    grad_proto, loss = call(
        final_body,
        "assemble",
        (shape((share, protos), F32), shape((1, 1), F32)),
        (own_sum, exchange(tails, "patch"), *far),
        product // 4,
    )
    return (grad_student, grad_proto, loss.reshape(()))


def solution(mesh):
    both = ("patch", "proto")
    in_specs = (P(both, None), P(both, None), P(None, "proto"), P(both), P(both))
    out_specs = (P(both, None), P("patch", "proto"), P())
    return jax.shard_map(
        on_device, mesh=mesh, in_specs=in_specs, out_specs=out_specs, check_vma=False
    )
```

```python
import functools

import jax
import jax.numpy as jnp
from jax import lax
from jax.experimental import pallas as pl
from jax.experimental.pallas import tpu as pltpu
from jax.sharding import PartitionSpec as P

SK_ITERS = 3
EPS = 1e-06
TEACHER_TEMP = 0.07
STUDENT_TEMP = 0.1
F32 = jnp.float32
BF16 = jnp.bfloat16
LANES = 128
PIECES = (3, 3, 2)
FIRST = 2
PARTS = (6, 2)
VMEM_LIMIT = 20 * 1024 * 1024

NN = (((1,), (0,)), ((), ()))
NT = (((1,), (1,)), ((), ()))
TN = (((0,), (0,)), ((), ()))
SMEM = pl.BlockSpec(memory_space=pltpu.SMEM)
VMEM = pl.BlockSpec(memory_space=pltpu.VMEM)
ANY = pl.BlockSpec(memory_space=pl.ANY)
HBM = pl.BlockSpec(memory_space=pltpu.HBM)


def mm(a, b, dims=NN):
    return lax.dot_general(a, b, dims, preferred_element_type=F32)


def shape(dims, dtype):
    return jax.ShapeDtypeStruct(dims, dtype)


def call(body, name, out_shape, args, flops, specs=None, after=(), scratch=(), limit=VMEM_LIMIT):
    specs = specs or [VMEM] * len(args)
    skip = len(after)
    args = [
        pltpu.with_memory_space_constraint(arg, pltpu.HBM) if spec is HBM else arg
        for arg, spec in zip(args, specs)
    ]

    def ordered(*refs):
        body(*refs[skip:])

    def out_spec(out):
        return VMEM if isinstance(out, jax.ShapeDtypeStruct) else HBM

    many = isinstance(out_shape, tuple)
    return pl.pallas_call(
        ordered,
        name=name,
        out_shape=out_shape,
        in_specs=[ANY] * skip + specs,
        out_specs=tuple(map(out_spec, out_shape)) if many else out_spec(out_shape),
        scratch_shapes=list(scratch),
        compiler_params=pltpu.CompilerParams(vmem_limit_bytes=limit),
        cost_estimate=pl.CostEstimate(flops=flops, bytes_accessed=1 << 16, transcendentals=0),
    )(*after, *args)


def three_terms(row):
    high = row.astype(BF16).astype(F32)
    rest = row - high
    mid = rest.astype(BF16).astype(F32)
    low = rest - mid
    index = lax.broadcasted_iota(jnp.int32, (16, row.shape[1]), 0)
    terms = jnp.where(
        index == 0, high, jnp.where(index == 1, mid, jnp.where(index == 2, low, 0.0))
    )
    return terms.astype(BF16)


def column_sum(refs):
    total = refs[0][...]
    for ref in refs[1:]:
        total = total + ref[...]
    return total


def chunks(table_ref, count=8):
    width = table_ref.shape[1] // count
    return [(j, pl.ds(j * width, width)) for j in range(count)]


def arrive(copies, j, ahead):
    if j == 0:
        for copy in copies[:ahead]:
            copy.start()
    copies[j].wait()
    if j + ahead < len(copies):
        copies[j + ahead].start()


def read_rows(message_ref, start, n):
    total = jnp.sum(message_ref[...], axis=0)
    pieces = [total[start + k : start + k + 1, :] for k in range(n // LANES)]
    return jnp.concatenate(pieces, axis=1)


def write_rows(message_ref, start, row):
    count = message_ref.shape[0]
    for k in range(row.shape[1] // LANES):
        piece = row[:, k * LANES : (k + 1) * LANES]
        message_ref[:, start + k, :] = jnp.broadcast_to(piece, (count, LANES))


def rows_body(
    place_ref,
    student_hbm,
    teacher_hbm,
    index_hbm,
    weight_hbm,
    rows_ref,
    x_ref,
    w_ref,
    student_ref,
    teacher_ref,
    index_ref,
    weight_ref,
    sems,
):
    copies = [
        pltpu.make_async_copy(index_hbm, index_ref, sems.at[0]),
        pltpu.make_async_copy(teacher_hbm, teacher_ref, sems.at[1]),
        pltpu.make_async_copy(student_hbm, student_ref, sems.at[2]),
        pltpu.make_async_copy(weight_hbm, weight_ref, sems.at[3]),
    ]
    for copy in copies:
        copy.start()
    for copy in copies:
        copy.wait()
    picks = index_ref[...]
    length = student_ref.shape[0]
    count = picks.shape[1]
    one_hot = (lax.broadcasted_iota(jnp.int32, (length, count), 0) == picks).astype(BF16)
    x = mm(one_hot, student_ref[...], TN)
    y = mm(one_hot, teacher_ref[...], TN)
    x_ref[...] = x
    unit_x = x * lax.rsqrt(jnp.sum(x * x, axis=1, keepdims=True) + EPS)
    unit_y = y * lax.rsqrt(jnp.sum(y * y, axis=1, keepdims=True) + EPS)
    both = jnp.concatenate([unit_y.astype(BF16), unit_x.astype(BF16)], axis=0)
    rows_ref[...] = jnp.broadcast_to(both[None], rows_ref.shape)
    lanes = w_ref.shape[1]
    spot = lax.broadcasted_iota(jnp.int32, (count, lanes), 1) - place_ref[0] * count
    spread = (spot == lax.broadcasted_iota(jnp.int32, (count, lanes), 0)).astype(BF16)
    w_ref[...] = jnp.broadcast_to(mm(weight_ref[...], spread), w_ref.shape)


def proto_body(w_hbm, unit_hbm, first_ref, inverse_ref, w_ref, unit_ref, in_sems, out_sems):
    count = unit_ref.shape[0]
    copies = [
        pltpu.make_async_copy(w_hbm.at[:, cols], w_ref.at[:, cols], in_sems.at[j])
        for j, cols in chunks(w_ref, count)
    ]
    stores = []
    for j, cols in chunks(w_ref, count):
        arrive(copies, j, 4)
        w = w_ref[:, cols].astype(F32)
        inverse = lax.rsqrt(jnp.sum(w * w, axis=0, keepdims=True) + EPS)
        inverse_ref[pl.ds(j, 1), :] = inverse
        unit = (w * inverse).astype(BF16)
        unit_ref[j] = unit
        if j < first_ref.shape[0]:
            first_ref[j] = unit
        store = pltpu.make_async_copy(unit_ref.at[j], unit_hbm.at[j], out_sems.at[j])
        store.start()
        stores.append(store)
    for store in stores:
        store.wait()


def table_body(rows_ref, first_ref, unit_hbm, table_ref, unit_ref, sums_ref, sems):
    skip, count = first_ref.shape[0], unit_ref.shape[0]
    copies = [
        pltpu.make_async_copy(unit_hbm.at[j], unit_ref.at[j], sems.at[j]) for j in range(count)
    ]
    for copy in copies[skip:] + copies[:skip]:
        copy.start()
    half = rows_ref.shape[1] // 2
    teacher = rows_ref[:, :half, :].reshape(-1, rows_ref.shape[2])
    for j, cols in chunks(table_ref, count):
        if j < skip:
            unit = first_ref[j]
        else:
            copies[j].wait()
            unit = unit_ref[j]
        table = jnp.exp(mm(teacher, unit) * (1.0 / TEACHER_TEMP)).astype(BF16)
        table_ref[:, cols] = table
        sums_ref[pl.ds(j, 1), :] = jnp.sum(table.astype(F32), axis=0, keepdims=True)
    for copy in copies[:skip]:
        copy.wait()


def row_pass_body(parts, *refs):
    sums_refs, table_ref, extra_refs, out_ref = refs[:parts], refs[parts], refs[parts + 1 : -1], refs[-1]
    scale = 1.0 / column_sum(sums_refs)
    n = table_ref.shape[0]
    total = jnp.zeros((16, n), F32)
    for j, cols in chunks(table_ref):
        total += mm(three_terms(scale[j : j + 1, :]), table_ref[:, cols], NT)
    write_rows(out_ref, 0, jnp.sum(total, axis=0, keepdims=True))
    write_rows(out_ref, n // LANES, column_sum(extra_refs)[0:1, :])


def col_pass_body(message_ref, table_ref, out_ref):
    terms = three_terms(1.0 / read_rows(message_ref, 0, table_ref.shape[0]))
    for j, cols in chunks(table_ref):
        out_ref[pl.ds(j, 1), :] = jnp.sum(mm(terms, table_ref[:, cols]), axis=0, keepdims=True)


def student_body(first, rows_ref, unit_ref, table_ref, sums_ref, feature_ref, *turned_refs):
    count = PIECES[first]
    start = sum(PIECES[:first])
    half = rows_ref.shape[1] // 2
    student = rows_ref[:, half:, :].reshape(-1, rows_ref.shape[2])
    total = jnp.zeros((16, student.shape[0]), F32)
    for j, cols in chunks(table_ref, count):
        unit = unit_ref[start + j]
        table = jnp.exp(mm(student, unit) * (1.0 / STUDENT_TEMP)).astype(BF16)
        table_ref[:, cols] = table
        total += mm(jnp.ones((16, table.shape[1]), BF16), table, NT)
        part = mm(unit, table, NT)
        if j == 0:
            feature_ref[...] = part
        else:
            feature_ref[...] += part
    sums_ref[...] = total[0:8]
    for turned_ref in turned_refs:
        d = student.shape[1]
        eye = (
            lax.broadcasted_iota(jnp.int32, (d, d), 0)
            == lax.broadcasted_iota(jnp.int32, (d, d), 1)
        ).astype(BF16)
        turned_ref[...] = mm(eye, student, NT).astype(BF16)


def last_row_pass_body(parts, *refs):
    sums_refs, table_ref, unit_ref = refs[:parts], refs[parts], refs[parts + 1]
    *extra_refs, out_ref, feature_ref = refs[parts + 2 :]
    scale = 1.0 / column_sum(sums_refs)
    n, d = table_ref.shape[0], unit_ref.shape[1]
    total = jnp.zeros((16, n), F32)
    for j, cols in chunks(table_ref):
        factor = scale[j : j + 1, :]
        scaled = (unit_ref[j].astype(F32) * factor).astype(BF16)
        left = jnp.concatenate([scaled, three_terms(factor)], axis=0)
        part = mm(left, table_ref[:, cols], NT)
        total += part[d:]
        if j == 0:
            feature_ref[...] = part[:d]
        else:
            feature_ref[...] += part[:d]
    write_rows(out_ref, 0, jnp.sum(total, axis=0, keepdims=True))
    write_rows(out_ref, n // LANES, column_sum(extra_refs)[0:1, :])


def row_factors(first_ref, last_ref, n):
    tile = n // LANES
    return read_rows(first_ref, tile, n), read_rows(last_ref, tile, n), read_rows(last_ref, 0, n)


def targets(place_ref, chips, share):
    x, core = place_ref[1], place_ref[2]
    spots = []
    for k in range(chips):
        for side in (core, 1 - core):
            spots.append(pl.ds(pl.multiple_of((2 * (x ^ k) + side) * share, share), share))
    return spots


def left_body(chips, place_ref, first_ref, last_ref, turned_ref, probs_ref, codes_ref):
    share = turned_ref.shape[0] // (2 * chips)
    weights, exp_total, total = row_factors(first_ref, last_ref, turned_ref.shape[1])
    over_probs = weights / exp_total * (1.0 / STUDENT_TEMP)
    over_codes = weights / total * (1.0 / STUDENT_TEMP)
    for m, spot in enumerate(targets(place_ref, chips, share)):
        rows = pl.ds(m * share, share)
        turned = turned_ref[spot, :].astype(F32)
        probs_ref[rows, :] = (turned * over_probs).astype(BF16)
        codes_ref[rows, :] = (turned * over_codes).astype(BF16)


def head_body(first, parts, *refs):
    place_ref, left_probs_ref, left_codes_ref = refs[:3]
    sums_refs = refs[3 : 3 + parts]
    inverse_ref, codes_ref, *piece_refs, w_ref = refs[3 + parts : -3]
    own_ref, keep_ref, near_ref = refs[-3:]
    chips, share = near_ref.shape[:2]
    width = inverse_ref.shape[1]
    spots = targets(place_ref, chips, share)
    left_probs, left_codes = left_probs_ref[...], left_codes_ref[...]
    scale = 1.0 / column_sum(sums_refs)
    where = [(p, at) for p, size in enumerate(PIECES) for at in range(size)]
    for j, cols in chunks(own_ref, own_ref.shape[1] // width):
        row = first + j
        here = pl.ds(row * width, width)
        piece, at = where[row]
        inverse = inverse_ref[pl.ds(row, 1), :]
        head = inverse * mm(left_probs, piece_refs[piece][:, pl.ds(at * width, width)]) - (
            inverse * scale[row : row + 1, :]
        ) * mm(left_codes, codes_ref[:, here])
        w = jnp.concatenate([w_ref[spot, here] for spot in spots], axis=0).astype(F32)
        inner = jnp.sum(w * head, axis=0, keepdims=True)
        grad = head - w * (inverse * inverse * inner)
        own_ref[:, cols] = grad[0:share]
        for k in range(chips):
            low = 2 * k * share
            if k:
                keep_ref[k - 1, :, cols] = grad[low : low + share].astype(BF16)
            near_ref[k, :, cols] = grad[low + share : low + 2 * share].astype(BF16)


def pair_body(*refs):
    count = len(PARTS)
    start = 0
    for part in range(count):
        keep_ref, near_ref = refs[2 * part : 2 * part + 2]
        span = keep_ref.shape[2]
        for k, pair_ref in enumerate(refs[2 * count :]):
            total = keep_ref[k].astype(F32) + near_ref[k + 1].astype(F32)
            pair_ref[:, start : start + span] = total.astype(BF16)
        start += span


def own_sum_body(tails_ref, *refs):
    count = len(PARTS)
    start = 0
    for part in range(count):
        own_ref, near_ref = refs[2 * part : 2 * part + 2]
        span = own_ref.shape[1]
        refs[-2][:, start : start + span] = own_ref[...] + near_ref[0].astype(F32)
        start += span
    refs[-1][...] = tails_ref[...]


def final_body(own_ref, tails_ref, *refs):
    *far_refs, out_ref, loss_ref = refs
    total = own_ref[...]
    for far_ref in far_refs:
        total = total + far_ref[...].astype(F32)
    out_ref[...] = total
    terms = jnp.sum(tails_ref[...], axis=0)[0:1, :]
    lane = lax.broadcasted_iota(jnp.int32, terms.shape, 1)
    part = jnp.sum(jnp.where(lane < 3, terms, 0.0), axis=1, keepdims=True)
    count = jnp.sum(jnp.where((lane >= 3) & (lane < 6), terms, 0.0), axis=1, keepdims=True)
    loss_ref[...] = part / count


def owner_body(sent_ref, x_ref, grad_ref, tail_ref):
    sent = jnp.sum(sent_ref[...].astype(F32), axis=0)
    own = x_ref.shape[0]
    x = x_ref[...]
    feature = sent[:own]
    inverse = lax.rsqrt(jnp.sum(x * x, axis=1, keepdims=True) + EPS)
    unit = x * inverse
    grad_ref[...] = inverse * (feature - unit * jnp.sum(unit * feature, axis=1, keepdims=True))
    tail_ref[...] = jnp.broadcast_to(sent[own : own + 8, :LANES][None], tail_ref.shape)


def split(value):
    row = jnp.broadcast_to(value, (8, LANES))
    high = row.astype(BF16).astype(F32)
    mid = (row - high).astype(BF16).astype(F32)
    return [term[0:1, 0:1] for term in (high, mid, row - high - mid)]


def feature_body(first_ref, last_ref, codes_ref, turned_ref, *refs):
    *probs_refs, out_ref = refs
    n = codes_ref.shape[1]
    count = out_ref.shape[0]
    own = n // count
    weights, exp_total, total = row_factors(first_ref, last_ref, n)
    codes = codes_ref[...]
    over = weights / total * (1.0 / STUDENT_TEMP)
    probs = column_sum(probs_refs) * (weights / exp_total * (1.0 / STUDENT_TEMP))
    feature = (probs - codes * over).T.astype(BF16)
    out_ref[:, :own, :] = feature.reshape(count, own, feature.shape[1])
    share = 1.0 / count
    cross = jnp.sum(turned_ref[...].astype(F32) * codes, axis=0, keepdims=True)
    part = jnp.sum(weights * jnp.log(exp_total) * share - over * cross)
    tail = (out_ref.shape[1] - own, out_ref.shape[2])
    lane = lax.broadcasted_iota(jnp.int32, tail, 1)
    row = jnp.zeros(tail, F32)
    for k, term in enumerate(split(part) + split(jnp.sum(weights) * share)):
        row = jnp.where(lane == k, term, row)
    out_ref[:, own:, :] = jnp.broadcast_to(row.astype(BF16)[None], (count,) + tail)


def on_device(student_feats, teacher_feats, proto_weight, mask_index, row_weight):
    n_patch, n_proto = lax.axis_size("patch"), lax.axis_size("proto")
    d, protos = proto_weight.shape
    length = student_feats.shape[0]
    own = mask_index.shape[0]
    rows = own * n_proto
    chips = n_patch // 2
    share = d // n_patch
    width = protos // 8
    patch, proto = lax.axis_index("patch"), lax.axis_index("proto")
    place = jnp.stack([proto, patch // 2, patch % 2]).astype(jnp.int32)
    product = 2 * rows * d * protos

    def exchange(array, axis):
        return lax.all_to_all(array, axis, 0, 0)

    def hop(array, bits):
        return lax.ppermute(array, "patch", [(i, i ^ bits) for i in range(n_patch)])

    own_rows, x_rows, own_weights = call(
        rows_body,
        "own_rows",
        (
            shape((n_proto, 2 * own, d), BF16),
            shape((own, d), F32),
            shape((8, rows), F32),
        ),
        (place, student_feats, teacher_feats, mask_index[None, :], row_weight[None, :]),
        1 << 28,
        specs=[SMEM, HBM, HBM, HBM, HBM],
        scratch=[
            pltpu.VMEM((length, d), BF16),
            pltpu.VMEM((length, d), BF16),
            pltpu.VMEM((1, own), jnp.int32),
            pltpu.VMEM((1, own), BF16),
            pltpu.SemaphoreType.DMA((4,)),
        ],
    )
    all_rows = exchange(own_rows, "proto")
    unit, unit_first, inverse = call(
        proto_body,
        "proto_unit",
        (
            pltpu.HBM((8, d, width), BF16),
            shape((FIRST, d, width), BF16),
            shape((8, width), F32),
        ),
        (proto_weight,),
        product,
        specs=[HBM],
        scratch=[
            pltpu.VMEM((d, protos), BF16),
            pltpu.VMEM((8, d, width), BF16),
            pltpu.SemaphoreType.DMA((8,)),
            pltpu.SemaphoreType.DMA((8,)),
        ],
    )
    codes, unit, sums = call(
        table_body,
        "teacher_table",
        (
            shape((rows, protos), BF16),
            shape((8, d, width), BF16),
            shape((8, width), F32),
        ),
        (all_rows, unit_first, unit),
        2 * product,
        specs=[VMEM, VMEM, HBM],
        scratch=[pltpu.SemaphoreType.DMA((8,))],
    )

    messages = []
    pieces = []
    for sweep in range(SK_ITERS):
        sums = sums + hop(sums, 1)
        parts = [sums] + [hop(sums, 2 * k) for k in range(1, chips)]
        span = PIECES[sweep] * width
        last = sweep == SK_ITERS - 1
        pieces.append(
            call(
                functools.partial(student_body, sweep),
                "student_table",
                (shape((rows, span), BF16), shape((8, rows), F32), shape((d, rows), F32))
                + ((shape((d, rows), BF16),) if last else ()),
                (all_rows, unit),
                product,
                after=(sums,),
            )
        )
        if last:
            part, codes_feature = call(
                functools.partial(last_row_pass_body, chips),
                "last_row_pass",
                (shape((n_proto, 8, LANES), F32), shape((d, rows), F32)),
                (*parts, codes, unit, *[piece[1] for piece in pieces]),
                product,
            )
        else:
            part = call(
                functools.partial(row_pass_body, chips),
                "row_pass",
                shape((n_proto, 8, LANES), F32),
                (*parts, codes, own_weights),
                product,
                after=(pieces[-1][1],),
            )
        messages.append(exchange(part, "proto"))
        if not last:
            sums = call(
                col_pass_body,
                "col_pass",
                shape((8, width), F32),
                (messages[-1], codes),
                product // 2,
            )

    turned = pieces[-1][3]
    factors = (messages[0], messages[-1])
    lefts = call(
        functools.partial(left_body, chips),
        "row_factors",
        (shape((d, rows), BF16), shape((d, rows), BF16)),
        (place, *factors, turned),
        product // 8,
        specs=[SMEM] + [VMEM] * (len(factors) + 1),
    )
    heads = []
    for index, count in enumerate(PARTS):
        span = count * width
        heads.append(
            call(
                functools.partial(head_body, sum(PARTS[:index]), chips),
                "head",
                (
                    shape((share, span), F32),
                    shape((chips - 1, share, span), BF16),
                    shape((chips, share, span), BF16),
                ),
                (
                    place,
                    *lefts,
                    *parts,
                    inverse,
                    codes,
                    *[piece[0] for piece in pieces],
                    proto_weight,
                ),
                2 * product,
                specs=[SMEM] + [VMEM] * (chips + 5 + len(pieces)),
                after=(heads[-1][1],) if heads else (),
            )
        )
    feature_part = call(
        feature_body,
        "feature",
        shape((n_proto, own + 16, d), BF16),
        (*factors, codes_feature, turned, *[piece[2] for piece in pieces]),
        product // 4,
        after=(heads[-1][1],),
    )
    ends, nears = [], []
    for own_block, keep, near in heads:
        near = hop(near, 1)
        ends += [keep, near]
        nears += [own_block, near]
    pairs = call(
        pair_body,
        "pair_sums",
        tuple(shape((share, protos), BF16) for _ in range(chips - 1)),
        tuple(ends),
        product // 8,
        after=(feature_part,),
    )
    far = [hop(pairs[k - 1], 2 * k) for k in sorted(range(1, chips), key=lambda k: k % 2)]
    grad_student, tails = call(
        owner_body,
        "owner",
        (shape((own, d), F32), shape((n_patch, 8, LANES), F32)),
        (exchange(feature_part, "proto"), x_rows),
        product // 8,
    )
    own_sum, tails = call(
        own_sum_body,
        "own_sum",
        (shape((share, protos), F32), shape((n_patch, 8, LANES), F32)),
        (tails, *nears),
        product // 8,
    )
    grad_proto, loss = call(
        final_body,
        "assemble",
        (shape((share, protos), F32), shape((1, 1), F32)),
        (own_sum, exchange(tails, "patch"), *far),
        product // 4,
    )
    return (grad_student, grad_proto, loss.reshape(()))


def solution(mesh):
    both = ("patch", "proto")
    in_specs = (P(both, None), P(both, None), P(None, "proto"), P(both), P(both))
    out_specs = (P(both, None), P("patch", "proto"), P())
    return jax.shard_map(
        on_device, mesh=mesh, in_specs=in_specs, out_specs=out_specs, check_vma=False
    )
```

```python
import functools

import jax
import jax.numpy as jnp
from jax import lax
from jax.experimental import pallas as pl
from jax.experimental.pallas import tpu as pltpu
from jax.sharding import PartitionSpec as P

SK_ITERS = 3
EPS = 1e-06
TEACHER_TEMP = 0.07
STUDENT_TEMP = 0.1
F32 = jnp.float32
BF16 = jnp.bfloat16
LANES = 128
PIECES = (3, 3, 2)
FIRST = 2
PARTS = (6, 2)
VMEM_LIMIT = 20 * 1024 * 1024

NN = (((1,), (0,)), ((), ()))
NT = (((1,), (1,)), ((), ()))
TN = (((0,), (0,)), ((), ()))
SMEM = pl.BlockSpec(memory_space=pltpu.SMEM)
VMEM = pl.BlockSpec(memory_space=pltpu.VMEM)
ANY = pl.BlockSpec(memory_space=pl.ANY)
HBM = pl.BlockSpec(memory_space=pltpu.HBM)


def mm(a, b, dims=NN):
    return lax.dot_general(a, b, dims, preferred_element_type=F32)


def shape(dims, dtype):
    return jax.ShapeDtypeStruct(dims, dtype)


def call(body, name, out_shape, args, flops, specs=None, after=(), scratch=(), limit=VMEM_LIMIT):
    specs = specs or [VMEM] * len(args)
    skip = len(after)
    args = [
        pltpu.with_memory_space_constraint(arg, pltpu.HBM) if spec is HBM else arg
        for arg, spec in zip(args, specs)
    ]

    def ordered(*refs):
        body(*refs[skip:])

    def out_spec(out):
        return VMEM if isinstance(out, jax.ShapeDtypeStruct) else HBM

    many = isinstance(out_shape, tuple)
    return pl.pallas_call(
        ordered,
        name=name,
        out_shape=out_shape,
        in_specs=[ANY] * skip + specs,
        out_specs=tuple(map(out_spec, out_shape)) if many else out_spec(out_shape),
        scratch_shapes=list(scratch),
        compiler_params=pltpu.CompilerParams(vmem_limit_bytes=limit),
        cost_estimate=pl.CostEstimate(flops=flops, bytes_accessed=1 << 16, transcendentals=0),
    )(*after, *args)


def three_terms(row):
    high = row.astype(BF16).astype(F32)
    rest = row - high
    mid = rest.astype(BF16).astype(F32)
    low = rest - mid
    index = lax.broadcasted_iota(jnp.int32, (16, row.shape[1]), 0)
    terms = jnp.where(
        index == 0, high, jnp.where(index == 1, mid, jnp.where(index == 2, low, 0.0))
    )
    return terms.astype(BF16)


def column_sum(refs):
    total = refs[0][...]
    for ref in refs[1:]:
        total = total + ref[...]
    return total


def chunks(table_ref, count=8):
    width = table_ref.shape[1] // count
    return [(j, pl.ds(j * width, width)) for j in range(count)]


def arrive(copies, j, ahead):
    if j == 0:
        for copy in copies[:ahead]:
            copy.start()
    copies[j].wait()
    if j + ahead < len(copies):
        copies[j + ahead].start()


def read_rows(message_ref, start, n):
    total = jnp.sum(message_ref[...], axis=0)
    pieces = [total[start + k : start + k + 1, :] for k in range(n // LANES)]
    return jnp.concatenate(pieces, axis=1)


def write_rows(message_ref, start, row):
    count = message_ref.shape[0]
    for k in range(row.shape[1] // LANES):
        piece = row[:, k * LANES : (k + 1) * LANES]
        message_ref[:, start + k, :] = jnp.broadcast_to(piece, (count, LANES))


def rows_body(
    place_ref,
    student_hbm,
    teacher_hbm,
    index_hbm,
    weight_hbm,
    rows_ref,
    x_ref,
    w_ref,
    student_ref,
    teacher_ref,
    index_ref,
    weight_ref,
    sems,
):
    copies = [
        pltpu.make_async_copy(index_hbm, index_ref, sems.at[0]),
        pltpu.make_async_copy(teacher_hbm, teacher_ref, sems.at[1]),
        pltpu.make_async_copy(student_hbm, student_ref, sems.at[2]),
        pltpu.make_async_copy(weight_hbm, weight_ref, sems.at[3]),
    ]
    for copy in copies:
        copy.start()
    for copy in copies:
        copy.wait()
    picks = index_ref[...]
    length = student_ref.shape[0]
    count = picks.shape[1]
    one_hot = (lax.broadcasted_iota(jnp.int32, (length, count), 0) == picks).astype(BF16)
    x = mm(one_hot, student_ref[...], TN)
    y = mm(one_hot, teacher_ref[...], TN)
    x_ref[...] = x
    unit_x = x * lax.rsqrt(jnp.sum(x * x, axis=1, keepdims=True) + EPS)
    unit_y = y * lax.rsqrt(jnp.sum(y * y, axis=1, keepdims=True) + EPS)
    both = jnp.concatenate([unit_y.astype(BF16), unit_x.astype(BF16)], axis=0)
    rows_ref[...] = jnp.broadcast_to(both[None], rows_ref.shape)
    lanes = w_ref.shape[1]
    spot = lax.broadcasted_iota(jnp.int32, (count, lanes), 1) - place_ref[0] * count
    spread = (spot == lax.broadcasted_iota(jnp.int32, (count, lanes), 0)).astype(BF16)
    w_ref[...] = jnp.broadcast_to(mm(weight_ref[...], spread), w_ref.shape)


def proto_body(w_hbm, unit_hbm, first_ref, inverse_ref, w_ref, unit_ref, in_sems, out_sems):
    count = unit_ref.shape[0]
    copies = [
        pltpu.make_async_copy(w_hbm.at[:, cols], w_ref.at[:, cols], in_sems.at[j])
        for j, cols in chunks(w_ref, count)
    ]
    stores = []
    for j, cols in chunks(w_ref, count):
        arrive(copies, j, 4)
        w = w_ref[:, cols].astype(F32)
        inverse = lax.rsqrt(jnp.sum(w * w, axis=0, keepdims=True) + EPS)
        inverse_ref[pl.ds(j, 1), :] = inverse
        unit = (w * inverse).astype(BF16)
        unit_ref[j] = unit
        if j < first_ref.shape[0]:
            first_ref[j] = unit
        store = pltpu.make_async_copy(unit_ref.at[j], unit_hbm.at[j], out_sems.at[j])
        store.start()
        stores.append(store)
    for store in stores:
        store.wait()


def table_body(rows_ref, first_ref, unit_hbm, table_ref, unit_ref, sums_ref, sems):
    skip, count = first_ref.shape[0], unit_ref.shape[0]
    copies = [
        pltpu.make_async_copy(unit_hbm.at[j], unit_ref.at[j], sems.at[j]) for j in range(count)
    ]
    for copy in copies[skip:] + copies[:skip]:
        copy.start()
    half = rows_ref.shape[1] // 2
    teacher = rows_ref[:, :half, :].reshape(-1, rows_ref.shape[2])
    for j, cols in chunks(table_ref, count):
        if j < skip:
            unit = first_ref[j]
        else:
            copies[j].wait()
            unit = unit_ref[j]
        table = jnp.exp(mm(teacher, unit) * (1.0 / TEACHER_TEMP)).astype(BF16)
        table_ref[:, cols] = table
        sums_ref[pl.ds(j, 1), :] = jnp.sum(table.astype(F32), axis=0, keepdims=True)
    for copy in copies[:skip]:
        copy.wait()


def row_pass_body(parts, *refs):
    sums_refs, table_ref, extra_refs, out_ref = refs[:parts], refs[parts], refs[parts + 1 : -1], refs[-1]
    scale = 1.0 / column_sum(sums_refs)
    n = table_ref.shape[0]
    total = jnp.zeros((16, n), F32)
    for j, cols in chunks(table_ref):
        total += mm(three_terms(scale[j : j + 1, :]), table_ref[:, cols], NT)
    write_rows(out_ref, 0, jnp.sum(total, axis=0, keepdims=True))
    write_rows(out_ref, n // LANES, column_sum(extra_refs)[0:1, :])


def col_pass_body(message_ref, table_ref, out_ref):
    terms = three_terms(1.0 / read_rows(message_ref, 0, table_ref.shape[0]))
    for j, cols in chunks(table_ref):
        out_ref[pl.ds(j, 1), :] = jnp.sum(mm(terms, table_ref[:, cols]), axis=0, keepdims=True)


def student_body(first, rows_ref, unit_ref, table_ref, sums_ref, feature_ref, *turned_refs):
    count = PIECES[first]
    start = sum(PIECES[:first])
    half = rows_ref.shape[1] // 2
    student = rows_ref[:, half:, :].reshape(-1, rows_ref.shape[2])
    total = jnp.zeros((16, student.shape[0]), F32)
    for j, cols in chunks(table_ref, count):
        unit = unit_ref[start + j]
        table = jnp.exp(mm(student, unit) * (1.0 / STUDENT_TEMP)).astype(BF16)
        table_ref[:, cols] = table
        total += mm(jnp.ones((16, table.shape[1]), BF16), table, NT)
        part = mm(unit, table, NT)
        if j == 0:
            feature_ref[...] = part
        else:
            feature_ref[...] += part
    sums_ref[...] = total[0:8]
    for turned_ref in turned_refs:
        d = student.shape[1]
        eye = (
            lax.broadcasted_iota(jnp.int32, (d, d), 0)
            == lax.broadcasted_iota(jnp.int32, (d, d), 1)
        ).astype(BF16)
        turned_ref[...] = mm(eye, student, NT).astype(BF16)


def last_row_pass_body(parts, *refs):
    sums_refs, table_ref, unit_ref = refs[:parts], refs[parts], refs[parts + 1]
    *extra_refs, out_ref, feature_ref = refs[parts + 2 :]
    scale = 1.0 / column_sum(sums_refs)
    n, d = table_ref.shape[0], unit_ref.shape[1]
    total = jnp.zeros((16, n), F32)
    for j, cols in chunks(table_ref):
        factor = scale[j : j + 1, :]
        scaled = (unit_ref[j].astype(F32) * factor).astype(BF16)
        left = jnp.concatenate([scaled, three_terms(factor)], axis=0)
        part = mm(left, table_ref[:, cols], NT)
        total += part[d:]
        if j == 0:
            feature_ref[...] = part[:d]
        else:
            feature_ref[...] += part[:d]
    write_rows(out_ref, 0, jnp.sum(total, axis=0, keepdims=True))
    write_rows(out_ref, n // LANES, column_sum(extra_refs)[0:1, :])


def row_factors(first_ref, last_ref, n):
    tile = n // LANES
    return read_rows(first_ref, tile, n), read_rows(last_ref, tile, n), read_rows(last_ref, 0, n)


def targets(place_ref, chips, share):
    x, core = place_ref[1], place_ref[2]
    spots = []
    for k in range(chips):
        for side in (core, 1 - core):
            spots.append(pl.ds(pl.multiple_of((2 * (x ^ k) + side) * share, share), share))
    return spots


def left_body(chips, place_ref, first_ref, last_ref, turned_ref, probs_ref, codes_ref):
    share = turned_ref.shape[0] // (2 * chips)
    weights, exp_total, total = row_factors(first_ref, last_ref, turned_ref.shape[1])
    over_probs = weights / exp_total * (1.0 / STUDENT_TEMP)
    over_codes = weights / total * (1.0 / STUDENT_TEMP)
    for m, spot in enumerate(targets(place_ref, chips, share)):
        rows = pl.ds(m * share, share)
        turned = turned_ref[spot, :].astype(F32)
        probs_ref[rows, :] = (turned * over_probs).astype(BF16)
        codes_ref[rows, :] = (turned * over_codes).astype(BF16)


def head_body(first, parts, *refs):
    place_ref, left_probs_ref, left_codes_ref = refs[:3]
    sums_refs = refs[3 : 3 + parts]
    inverse_ref, codes_ref, *piece_refs, w_ref = refs[3 + parts : -3]
    own_ref, keep_ref, near_ref = refs[-3:]
    chips, share = near_ref.shape[:2]
    width = inverse_ref.shape[1]
    spots = targets(place_ref, chips, share)
    left_probs, left_codes = left_probs_ref[...], left_codes_ref[...]
    scale = 1.0 / column_sum(sums_refs)
    where = [(p, at) for p, size in enumerate(PIECES) for at in range(size)]
    for j, cols in chunks(own_ref, own_ref.shape[1] // width):
        row = first + j
        here = pl.ds(row * width, width)
        piece, at = where[row]
        inverse = inverse_ref[pl.ds(row, 1), :]
        head = mm(left_probs, piece_refs[piece][:, pl.ds(at * width, width)]) - scale[
            row : row + 1, :
        ] * mm(left_codes, codes_ref[:, here])
        w = jnp.concatenate([w_ref[spot, here] for spot in spots], axis=0)
        unit = w.astype(F32) * inverse
        inner = jnp.sum(unit * head, axis=0, keepdims=True)
        grad = inverse * (head - unit * inner)
        own_ref[:, cols] = grad[0:share]
        for k in range(chips):
            low = 2 * k * share
            if k:
                keep_ref[k - 1, :, cols] = grad[low : low + share].astype(BF16)
            near_ref[k, :, cols] = grad[low + share : low + 2 * share].astype(BF16)


def pair_body(*refs):
    count = len(PARTS)
    start = 0
    for part in range(count):
        keep_ref, near_ref = refs[2 * part : 2 * part + 2]
        span = keep_ref.shape[2]
        for k, pair_ref in enumerate(refs[2 * count :]):
            total = keep_ref[k].astype(F32) + near_ref[k + 1].astype(F32)
            pair_ref[:, start : start + span] = total.astype(BF16)
        start += span


def own_sum_body(tails_ref, *refs):
    count = len(PARTS)
    start = 0
    for part in range(count):
        own_ref, near_ref = refs[2 * part : 2 * part + 2]
        span = own_ref.shape[1]
        refs[-2][:, start : start + span] = own_ref[...] + near_ref[0].astype(F32)
        start += span
    refs[-1][...] = tails_ref[...]


def final_body(own_ref, tails_ref, *refs):
    *far_refs, out_ref, loss_ref = refs
    total = own_ref[...]
    for far_ref in far_refs:
        total = total + far_ref[...].astype(F32)
    out_ref[...] = total
    terms = jnp.sum(tails_ref[...], axis=0)[0:1, :]
    lane = lax.broadcasted_iota(jnp.int32, terms.shape, 1)
    part = jnp.sum(jnp.where(lane < 3, terms, 0.0), axis=1, keepdims=True)
    count = jnp.sum(jnp.where((lane >= 3) & (lane < 6), terms, 0.0), axis=1, keepdims=True)
    loss_ref[...] = part / count


def owner_body(sent_ref, x_ref, grad_ref, tail_ref):
    sent = jnp.sum(sent_ref[...].astype(F32), axis=0)
    own = x_ref.shape[0]
    x = x_ref[...]
    feature = sent[:own]
    inverse = lax.rsqrt(jnp.sum(x * x, axis=1, keepdims=True) + EPS)
    unit = x * inverse
    grad_ref[...] = inverse * (feature - unit * jnp.sum(unit * feature, axis=1, keepdims=True))
    tail_ref[...] = jnp.broadcast_to(sent[own : own + 8, :LANES][None], tail_ref.shape)


def split(value):
    row = jnp.broadcast_to(value, (8, LANES))
    high = row.astype(BF16).astype(F32)
    mid = (row - high).astype(BF16).astype(F32)
    return [term[0:1, 0:1] for term in (high, mid, row - high - mid)]


def feature_body(first_ref, last_ref, codes_ref, turned_ref, *refs):
    *probs_refs, out_ref = refs
    n = codes_ref.shape[1]
    count = out_ref.shape[0]
    own = n // count
    weights, exp_total, total = row_factors(first_ref, last_ref, n)
    codes = codes_ref[...]
    over = weights / total * (1.0 / STUDENT_TEMP)
    probs = column_sum(probs_refs) * (weights / exp_total * (1.0 / STUDENT_TEMP))
    feature = (probs - codes * over).T.astype(BF16)
    out_ref[:, :own, :] = feature.reshape(count, own, feature.shape[1])
    share = 1.0 / count
    cross = jnp.sum(turned_ref[...].astype(F32) * codes, axis=0, keepdims=True)
    part = jnp.sum(weights * jnp.log(exp_total) * share - over * cross)
    tail = (out_ref.shape[1] - own, out_ref.shape[2])
    lane = lax.broadcasted_iota(jnp.int32, tail, 1)
    row = jnp.zeros(tail, F32)
    for k, term in enumerate(split(part) + split(jnp.sum(weights) * share)):
        row = jnp.where(lane == k, term, row)
    out_ref[:, own:, :] = jnp.broadcast_to(row.astype(BF16)[None], (count,) + tail)


def on_device(student_feats, teacher_feats, proto_weight, mask_index, row_weight):
    n_patch, n_proto = lax.axis_size("patch"), lax.axis_size("proto")
    d, protos = proto_weight.shape
    length = student_feats.shape[0]
    own = mask_index.shape[0]
    rows = own * n_proto
    chips = n_patch // 2
    share = d // n_patch
    width = protos // 8
    patch, proto = lax.axis_index("patch"), lax.axis_index("proto")
    place = jnp.stack([proto, patch // 2, patch % 2]).astype(jnp.int32)
    product = 2 * rows * d * protos

    def exchange(array, axis):
        return lax.all_to_all(array, axis, 0, 0)

    def hop(array, bits):
        return lax.ppermute(array, "patch", [(i, i ^ bits) for i in range(n_patch)])

    own_rows, x_rows, own_weights = call(
        rows_body,
        "own_rows",
        (
            shape((n_proto, 2 * own, d), BF16),
            shape((own, d), F32),
            shape((8, rows), F32),
        ),
        (place, student_feats, teacher_feats, mask_index[None, :], row_weight[None, :]),
        1 << 28,
        specs=[SMEM, HBM, HBM, HBM, HBM],
        scratch=[
            pltpu.VMEM((length, d), BF16),
            pltpu.VMEM((length, d), BF16),
            pltpu.VMEM((1, own), jnp.int32),
            pltpu.VMEM((1, own), BF16),
            pltpu.SemaphoreType.DMA((4,)),
        ],
    )
    all_rows = exchange(own_rows, "proto")
    unit, unit_first, inverse = call(
        proto_body,
        "proto_unit",
        (
            pltpu.HBM((8, d, width), BF16),
            shape((FIRST, d, width), BF16),
            shape((8, width), F32),
        ),
        (proto_weight,),
        product,
        specs=[HBM],
        scratch=[
            pltpu.VMEM((d, protos), BF16),
            pltpu.VMEM((8, d, width), BF16),
            pltpu.SemaphoreType.DMA((8,)),
            pltpu.SemaphoreType.DMA((8,)),
        ],
    )
    codes, unit, sums = call(
        table_body,
        "teacher_table",
        (
            shape((rows, protos), BF16),
            shape((8, d, width), BF16),
            shape((8, width), F32),
        ),
        (all_rows, unit_first, unit),
        2 * product,
        specs=[VMEM, VMEM, HBM],
        scratch=[pltpu.SemaphoreType.DMA((8,))],
    )

    messages = []
    pieces = []
    for sweep in range(SK_ITERS):
        sums = sums + hop(sums, 1)
        parts = [sums] + [hop(sums, 2 * k) for k in range(1, chips)]
        span = PIECES[sweep] * width
        last = sweep == SK_ITERS - 1
        pieces.append(
            call(
                functools.partial(student_body, sweep),
                "student_table",
                (shape((rows, span), BF16), shape((8, rows), F32), shape((d, rows), F32))
                + ((shape((d, rows), BF16),) if last else ()),
                (all_rows, unit),
                product,
                after=(sums,),
            )
        )
        if last:
            part, codes_feature = call(
                functools.partial(last_row_pass_body, chips),
                "last_row_pass",
                (shape((n_proto, 8, LANES), F32), shape((d, rows), F32)),
                (*parts, codes, unit, *[piece[1] for piece in pieces]),
                product,
            )
        else:
            part = call(
                functools.partial(row_pass_body, chips),
                "row_pass",
                shape((n_proto, 8, LANES), F32),
                (*parts, codes, own_weights),
                product,
                after=(pieces[-1][1],),
            )
        messages.append(exchange(part, "proto"))
        if not last:
            sums = call(
                col_pass_body,
                "col_pass",
                shape((8, width), F32),
                (messages[-1], codes),
                product // 2,
            )

    turned = pieces[-1][3]
    factors = (messages[0], messages[-1])
    lefts = call(
        functools.partial(left_body, chips),
        "row_factors",
        (shape((d, rows), BF16), shape((d, rows), BF16)),
        (place, *factors, turned),
        product // 8,
        specs=[SMEM] + [VMEM] * (len(factors) + 1),
    )
    heads = []
    for index, count in enumerate(PARTS):
        span = count * width
        heads.append(
            call(
                functools.partial(head_body, sum(PARTS[:index]), chips),
                "head",
                (
                    shape((share, span), F32),
                    shape((chips - 1, share, span), BF16),
                    shape((chips, share, span), BF16),
                ),
                (
                    place,
                    *lefts,
                    *parts,
                    inverse,
                    codes,
                    *[piece[0] for piece in pieces],
                    proto_weight,
                ),
                2 * product,
                specs=[SMEM] + [VMEM] * (chips + 5 + len(pieces)),
                after=(heads[-1][1],) if heads else (),
            )
        )
    feature_part = call(
        feature_body,
        "feature",
        shape((n_proto, own + 16, d), BF16),
        (*factors, codes_feature, turned, *[piece[2] for piece in pieces]),
        product // 4,
        after=(heads[-1][1],),
    )
    ends, nears = [], []
    for own_block, keep, near in heads:
        near = hop(near, 1)
        ends += [keep, near]
        nears += [own_block, near]
    pairs = call(
        pair_body,
        "pair_sums",
        tuple(shape((share, protos), BF16) for _ in range(chips - 1)),
        tuple(ends),
        product // 8,
        after=(feature_part,),
    )
    far = [hop(pairs[k - 1], 2 * k) for k in sorted(range(1, chips), key=lambda k: k % 2)]
    grad_student, tails = call(
        owner_body,
        "owner",
        (shape((own, d), F32), shape((n_patch, 8, LANES), F32)),
        (exchange(feature_part, "proto"), x_rows),
        product // 8,
    )
    own_sum, tails = call(
        own_sum_body,
        "own_sum",
        (shape((share, protos), F32), shape((n_patch, 8, LANES), F32)),
        (tails, *nears),
        product // 8,
    )
    grad_proto, loss = call(
        final_body,
        "assemble",
        (shape((share, protos), F32), shape((1, 1), F32)),
        (own_sum, exchange(tails, "patch"), *far),
        product // 4,
    )
    return (grad_student, grad_proto, loss.reshape(()))


def solution(mesh):
    both = ("patch", "proto")
    in_specs = (P(both, None), P(both, None), P(None, "proto"), P(both), P(both))
    out_specs = (P(both, None), P("patch", "proto"), P())
    return jax.shard_map(
        on_device, mesh=mesh, in_specs=in_specs, out_specs=out_specs, check_vma=False
    )
```

```python
import functools

import jax
import jax.numpy as jnp
from jax import lax
from jax.experimental import pallas as pl
from jax.experimental.pallas import tpu as pltpu
from jax.sharding import PartitionSpec as P

SK_ITERS = 3
EPS = 1e-06
TEACHER_TEMP = 0.07
STUDENT_TEMP = 0.1
F32 = jnp.float32
BF16 = jnp.bfloat16
LANES = 128
PIECES = (3, 3, 2)
FIRST = 2
PARTS = (6, 2)
VMEM_LIMIT = 20 * 1024 * 1024

NN = (((1,), (0,)), ((), ()))
NT = (((1,), (1,)), ((), ()))
TN = (((0,), (0,)), ((), ()))
SMEM = pl.BlockSpec(memory_space=pltpu.SMEM)
VMEM = pl.BlockSpec(memory_space=pltpu.VMEM)
ANY = pl.BlockSpec(memory_space=pl.ANY)
HBM = pl.BlockSpec(memory_space=pltpu.HBM)


def mm(a, b, dims=NN):
    return lax.dot_general(a, b, dims, preferred_element_type=F32)


def shape(dims, dtype):
    return jax.ShapeDtypeStruct(dims, dtype)


def call(body, name, out_shape, args, flops, specs=None, after=(), scratch=(), limit=VMEM_LIMIT):
    specs = specs or [VMEM] * len(args)
    skip = len(after)
    args = [
        pltpu.with_memory_space_constraint(arg, pltpu.HBM) if spec is HBM else arg
        for arg, spec in zip(args, specs)
    ]

    def ordered(*refs):
        body(*refs[skip:])

    def out_spec(out):
        return VMEM if isinstance(out, jax.ShapeDtypeStruct) else HBM

    many = isinstance(out_shape, tuple)
    return pl.pallas_call(
        ordered,
        name=name,
        out_shape=out_shape,
        in_specs=[ANY] * skip + specs,
        out_specs=tuple(map(out_spec, out_shape)) if many else out_spec(out_shape),
        scratch_shapes=list(scratch),
        compiler_params=pltpu.CompilerParams(vmem_limit_bytes=limit),
        cost_estimate=pl.CostEstimate(flops=flops, bytes_accessed=1 << 16, transcendentals=0),
    )(*after, *args)


def three_terms(row):
    high = row.astype(BF16).astype(F32)
    rest = row - high
    mid = rest.astype(BF16).astype(F32)
    low = rest - mid
    index = lax.broadcasted_iota(jnp.int32, (16, row.shape[1]), 0)
    terms = jnp.where(
        index == 0, high, jnp.where(index == 1, mid, jnp.where(index == 2, low, 0.0))
    )
    return terms.astype(BF16)


def column_sum(refs):
    total = refs[0][...]
    for ref in refs[1:]:
        total = total + ref[...]
    return total


def chunks(table_ref, count=8):
    width = table_ref.shape[1] // count
    return [(j, pl.ds(j * width, width)) for j in range(count)]


def arrive(copies, j, ahead):
    if j == 0:
        for copy in copies[:ahead]:
            copy.start()
    copies[j].wait()
    if j + ahead < len(copies):
        copies[j + ahead].start()


def read_rows(message_ref, start, n):
    total = jnp.sum(message_ref[...], axis=0)
    pieces = [total[start + k : start + k + 1, :] for k in range(n // LANES)]
    return jnp.concatenate(pieces, axis=1)


def write_rows(message_ref, start, row):
    count = message_ref.shape[0]
    for k in range(row.shape[1] // LANES):
        piece = row[:, k * LANES : (k + 1) * LANES]
        message_ref[:, start + k, :] = jnp.broadcast_to(piece, (count, LANES))


def rows_body(
    place_ref,
    student_hbm,
    teacher_hbm,
    index_hbm,
    weight_hbm,
    rows_ref,
    x_ref,
    w_ref,
    student_ref,
    teacher_ref,
    index_ref,
    weight_ref,
    sems,
):
    copies = [
        pltpu.make_async_copy(index_hbm, index_ref, sems.at[0]),
        pltpu.make_async_copy(teacher_hbm, teacher_ref, sems.at[1]),
        pltpu.make_async_copy(student_hbm, student_ref, sems.at[2]),
        pltpu.make_async_copy(weight_hbm, weight_ref, sems.at[3]),
    ]
    for copy in copies:
        copy.start()
    for copy in copies:
        copy.wait()
    picks = index_ref[...]
    length = student_ref.shape[0]
    count = picks.shape[1]
    one_hot = (lax.broadcasted_iota(jnp.int32, (length, count), 0) == picks).astype(BF16)
    x = mm(one_hot, student_ref[...], TN)
    y = mm(one_hot, teacher_ref[...], TN)
    x_ref[...] = x
    unit_x = x * lax.rsqrt(jnp.sum(x * x, axis=1, keepdims=True) + EPS)
    unit_y = y * lax.rsqrt(jnp.sum(y * y, axis=1, keepdims=True) + EPS)
    both = jnp.concatenate([unit_y.astype(BF16), unit_x.astype(BF16)], axis=0)
    rows_ref[...] = jnp.broadcast_to(both[None], rows_ref.shape)
    lanes = w_ref.shape[1]
    spot = lax.broadcasted_iota(jnp.int32, (count, lanes), 1) - place_ref[0] * count
    spread = (spot == lax.broadcasted_iota(jnp.int32, (count, lanes), 0)).astype(BF16)
    w_ref[...] = jnp.broadcast_to(mm(weight_ref[...], spread), w_ref.shape)


def proto_body(w_hbm, unit_hbm, first_ref, inverse_ref, w_ref, unit_ref, in_sems, out_sems):
    count = unit_ref.shape[0]
    copies = [
        pltpu.make_async_copy(w_hbm.at[:, cols], w_ref.at[:, cols], in_sems.at[j])
        for j, cols in chunks(w_ref, count)
    ]
    stores = []
    for j, cols in chunks(w_ref, count):
        arrive(copies, j, 4)
        w = w_ref[:, cols].astype(F32)
        inverse = lax.rsqrt(jnp.sum(w * w, axis=0, keepdims=True) + EPS)
        inverse_ref[pl.ds(j, 1), :] = inverse
        unit = (w * inverse).astype(BF16)
        unit_ref[j] = unit
        if j < first_ref.shape[0]:
            first_ref[j] = unit
        store = pltpu.make_async_copy(unit_ref.at[j], unit_hbm.at[j], out_sems.at[j])
        store.start()
        stores.append(store)
    for store in stores:
        store.wait()


def table_body(rows_ref, first_ref, unit_hbm, table_ref, unit_ref, sums_ref, sems):
    skip, count = first_ref.shape[0], unit_ref.shape[0]
    copies = [
        pltpu.make_async_copy(unit_hbm.at[j], unit_ref.at[j], sems.at[j]) for j in range(count)
    ]
    for copy in copies[skip:] + copies[:skip]:
        copy.start()
    half = rows_ref.shape[1] // 2
    teacher = rows_ref[:, :half, :].reshape(-1, rows_ref.shape[2])
    for j, cols in chunks(table_ref, count):
        if j < skip:
            unit = first_ref[j]
        else:
            copies[j].wait()
            unit = unit_ref[j]
        table = jnp.exp(mm(teacher, unit) * (1.0 / TEACHER_TEMP)).astype(BF16)
        table_ref[:, cols] = table
        sums_ref[pl.ds(j, 1), :] = jnp.sum(table.astype(F32), axis=0, keepdims=True)
    for copy in copies[:skip]:
        copy.wait()


def row_pass_body(parts, *refs):
    sums_refs, table_ref, extra_refs, out_ref = refs[:parts], refs[parts], refs[parts + 1 : -1], refs[-1]
    scale = 1.0 / column_sum(sums_refs)
    n = table_ref.shape[0]
    total = jnp.zeros((16, n), F32)
    for j, cols in chunks(table_ref):
        total += mm(three_terms(scale[j : j + 1, :]), table_ref[:, cols], NT)
    write_rows(out_ref, 0, jnp.sum(total, axis=0, keepdims=True))
    write_rows(out_ref, n // LANES, column_sum(extra_refs)[0:1, :])


def col_pass_body(message_ref, table_ref, out_ref):
    terms = three_terms(1.0 / read_rows(message_ref, 0, table_ref.shape[0]))
    for j, cols in chunks(table_ref):
        out_ref[pl.ds(j, 1), :] = jnp.sum(mm(terms, table_ref[:, cols]), axis=0, keepdims=True)


def student_body(first, rows_ref, unit_ref, table_ref, sums_ref, feature_ref, *turned_refs):
    count = PIECES[first]
    start = sum(PIECES[:first])
    half = rows_ref.shape[1] // 2
    student = rows_ref[:, half:, :].reshape(-1, rows_ref.shape[2])
    total = jnp.zeros((16, student.shape[0]), F32)
    for j, cols in chunks(table_ref, count):
        unit = unit_ref[start + j]
        table = jnp.exp(mm(student, unit) * (1.0 / STUDENT_TEMP)).astype(BF16)
        table_ref[:, cols] = table
        total += mm(jnp.ones((16, table.shape[1]), BF16), table, NT)
        part = mm(unit, table, NT)
        if j == 0:
            feature_ref[...] = part
        else:
            feature_ref[...] += part
    sums_ref[...] = total[0:8]
    for turned_ref in turned_refs:
        d = student.shape[1]
        eye = (
            lax.broadcasted_iota(jnp.int32, (d, d), 0)
            == lax.broadcasted_iota(jnp.int32, (d, d), 1)
        ).astype(BF16)
        turned_ref[...] = mm(eye, student, NT).astype(BF16)


def last_row_pass_body(parts, *refs):
    sums_refs, table_ref, unit_ref = refs[:parts], refs[parts], refs[parts + 1]
    *extra_refs, out_ref, feature_ref = refs[parts + 2 :]
    scale = 1.0 / column_sum(sums_refs)
    n, d = table_ref.shape[0], unit_ref.shape[1]
    total = jnp.zeros((16, n), F32)
    for j, cols in chunks(table_ref):
        factor = scale[j : j + 1, :]
        scaled = (unit_ref[j].astype(F32) * factor).astype(BF16)
        left = jnp.concatenate([scaled, three_terms(factor)], axis=0)
        part = mm(left, table_ref[:, cols], NT)
        total += part[d:]
        if j == 0:
            feature_ref[...] = part[:d]
        else:
            feature_ref[...] += part[:d]
    write_rows(out_ref, 0, jnp.sum(total, axis=0, keepdims=True))
    write_rows(out_ref, n // LANES, column_sum(extra_refs)[0:1, :])


def row_factors(first_ref, last_ref, n):
    tile = n // LANES
    return read_rows(first_ref, tile, n), read_rows(last_ref, tile, n), read_rows(last_ref, 0, n)


def targets(place_ref, chips, share):
    x, core = place_ref[1], place_ref[2]
    spots = []
    for k in range(chips):
        for side in (core, 1 - core):
            spots.append(pl.ds(pl.multiple_of((2 * (x ^ k) + side) * share, share), share))
    return spots


def left_body(chips, place_ref, first_ref, last_ref, turned_ref, probs_ref, codes_ref):
    share = turned_ref.shape[0] // (2 * chips)
    weights, exp_total, total = row_factors(first_ref, last_ref, turned_ref.shape[1])
    over_probs = weights / exp_total * (1.0 / STUDENT_TEMP)
    over_codes = weights / total * (1.0 / STUDENT_TEMP)
    for m, spot in enumerate(targets(place_ref, chips, share)):
        rows = pl.ds(m * share, share)
        turned = turned_ref[spot, :].astype(F32)
        probs_ref[rows, :] = (turned * over_probs).astype(BF16)
        codes_ref[rows, :] = (turned * over_codes).astype(BF16)


def head_body(first, parts, *refs):
    place_ref, left_probs_ref, left_codes_ref = refs[:3]
    sums_refs = refs[3 : 3 + parts]
    inverse_ref, codes_ref, *piece_refs, w_ref = refs[3 + parts : -3]
    own_ref, keep_ref, near_ref = refs[-3:]
    chips, share = near_ref.shape[:2]
    width = inverse_ref.shape[1]
    spots = targets(place_ref, chips, share)
    left_probs, left_codes = left_probs_ref[...], left_codes_ref[...]
    scale = 1.0 / column_sum(sums_refs)
    where = [(p, at) for p, size in enumerate(PIECES) for at in range(size)]
    for j, cols in chunks(own_ref, own_ref.shape[1] // width):
        row = first + j
        here = pl.ds(row * width, width)
        piece, at = where[row]
        inverse = inverse_ref[pl.ds(row, 1), :]
        head = mm(left_probs, piece_refs[piece][:, pl.ds(at * width, width)]) - scale[
            row : row + 1, :
        ] * mm(left_codes, codes_ref[:, here])
        w = jnp.concatenate([w_ref[spot, here] for spot in spots], axis=0)
        unit = w.astype(F32) * inverse
        inner = jnp.sum(unit * head, axis=0, keepdims=True)
        grad = inverse * (head - unit * inner)
        own_ref[:, cols] = grad[0:share]
        for k in range(chips):
            low = 2 * k * share
            if k:
                keep_ref[k - 1, :, cols] = grad[low : low + share].astype(BF16)
            near_ref[k, :, cols] = grad[low + share : low + 2 * share].astype(BF16)


def pair_body(*refs):
    count = len(PARTS)
    start = 0
    for part in range(count):
        keep_ref, near_ref = refs[2 * part : 2 * part + 2]
        span = keep_ref.shape[2]
        for k, pair_ref in enumerate(refs[2 * count :]):
            total = keep_ref[k].astype(F32) + near_ref[k + 1].astype(F32)
            pair_ref[:, start : start + span] = total.astype(BF16)
        start += span


def own_sum_body(tails_ref, *refs):
    count = len(PARTS)
    start = 0
    for part in range(count):
        own_ref, near_ref = refs[2 * part : 2 * part + 2]
        span = own_ref.shape[1]
        refs[-2][:, start : start + span] = own_ref[...] + near_ref[0].astype(F32)
        start += span
    refs[-1][...] = tails_ref[...]


def final_body(own_ref, tails_ref, *refs):
    *far_refs, out_ref, loss_ref = refs
    total = own_ref[...]
    for far_ref in far_refs:
        total = total + far_ref[...].astype(F32)
    out_ref[...] = total
    terms = jnp.sum(tails_ref[...], axis=0)[0:1, :]
    lane = lax.broadcasted_iota(jnp.int32, terms.shape, 1)
    part = jnp.sum(jnp.where(lane < 3, terms, 0.0), axis=1, keepdims=True)
    count = jnp.sum(jnp.where((lane >= 3) & (lane < 6), terms, 0.0), axis=1, keepdims=True)
    loss_ref[...] = part / count


def owner_body(sent_ref, x_ref, grad_ref, tail_ref):
    sent = jnp.sum(sent_ref[...].astype(F32), axis=0)
    own = x_ref.shape[0]
    x = x_ref[...]
    feature = sent[:own]
    inverse = lax.rsqrt(jnp.sum(x * x, axis=1, keepdims=True) + EPS)
    unit = x * inverse
    grad_ref[...] = inverse * (feature - unit * jnp.sum(unit * feature, axis=1, keepdims=True))
    tail_ref[...] = jnp.broadcast_to(sent[own : own + 8, :LANES][None], tail_ref.shape)


def split(value):
    row = jnp.broadcast_to(value, (8, LANES))
    high = row.astype(BF16).astype(F32)
    mid = (row - high).astype(BF16).astype(F32)
    return [term[0:1, 0:1] for term in (high, mid, row - high - mid)]


def feature_body(first_ref, last_ref, codes_ref, turned_ref, *refs):
    *probs_refs, out_ref = refs
    n = codes_ref.shape[1]
    count = out_ref.shape[0]
    own = n // count
    weights, exp_total, total = row_factors(first_ref, last_ref, n)
    codes = codes_ref[...]
    over = weights / total * (1.0 / STUDENT_TEMP)
    probs = column_sum(probs_refs) * (weights / exp_total * (1.0 / STUDENT_TEMP))
    feature = (probs - codes * over).T.astype(BF16)
    out_ref[:, :own, :] = feature.reshape(count, own, feature.shape[1])
    share = 1.0 / count
    cross = jnp.sum(turned_ref[...].astype(F32) * codes, axis=0, keepdims=True)
    part = jnp.sum(weights * jnp.log(exp_total) * share - over * cross)
    tail = (out_ref.shape[1] - own, out_ref.shape[2])
    lane = lax.broadcasted_iota(jnp.int32, tail, 1)
    row = jnp.zeros(tail, F32)
    for k, term in enumerate(split(part) + split(jnp.sum(weights) * share)):
        row = jnp.where(lane == k, term, row)
    out_ref[:, own:, :] = jnp.broadcast_to(row.astype(BF16)[None], (count,) + tail)


def on_device(student_feats, teacher_feats, proto_weight, mask_index, row_weight):
    n_patch, n_proto = lax.axis_size("patch"), lax.axis_size("proto")
    d, protos = proto_weight.shape
    length = student_feats.shape[0]
    own = mask_index.shape[0]
    rows = own * n_proto
    chips = n_patch // 2
    share = d // n_patch
    width = protos // 8
    patch, proto = lax.axis_index("patch"), lax.axis_index("proto")
    place = jnp.stack([proto, patch // 2, patch % 2]).astype(jnp.int32)
    product = 2 * rows * d * protos

    def exchange(array, axis):
        return lax.all_to_all(array, axis, 0, 0)

    def hop(array, bits):
        return lax.ppermute(array, "patch", [(i, i ^ bits) for i in range(n_patch)])

    own_rows, x_rows, own_weights = call(
        rows_body,
        "own_rows",
        (
            shape((n_proto, 2 * own, d), BF16),
            shape((own, d), F32),
            shape((8, rows), F32),
        ),
        (place, student_feats, teacher_feats, mask_index[None, :], row_weight[None, :]),
        1 << 28,
        specs=[SMEM, HBM, HBM, HBM, HBM],
        scratch=[
            pltpu.VMEM((length, d), BF16),
            pltpu.VMEM((length, d), BF16),
            pltpu.VMEM((1, own), jnp.int32),
            pltpu.VMEM((1, own), BF16),
            pltpu.SemaphoreType.DMA((4,)),
        ],
    )
    all_rows = exchange(own_rows, "proto")
    unit, unit_first, inverse = call(
        proto_body,
        "proto_unit",
        (
            pltpu.HBM((8, d, width), BF16),
            shape((FIRST, d, width), BF16),
            shape((8, width), F32),
        ),
        (proto_weight,),
        product,
        specs=[HBM],
        scratch=[
            pltpu.VMEM((d, protos), BF16),
            pltpu.VMEM((8, d, width), BF16),
            pltpu.SemaphoreType.DMA((8,)),
            pltpu.SemaphoreType.DMA((8,)),
        ],
    )
    codes, unit, sums = call(
        table_body,
        "teacher_table",
        (
            shape((rows, protos), BF16),
            shape((8, d, width), BF16),
            shape((8, width), F32),
        ),
        (all_rows, unit_first, unit),
        2 * product,
        specs=[VMEM, VMEM, HBM],
        scratch=[pltpu.SemaphoreType.DMA((8,))],
    )

    messages = []
    pieces = []
    for sweep in range(SK_ITERS):
        sums = sums + hop(sums, 1)
        steps = sorted(range(1, chips), key=lambda k: k % 2, reverse=True)
        parts = [sums] + [hop(sums, 2 * k) for k in steps]
        span = PIECES[sweep] * width
        last = sweep == SK_ITERS - 1
        pieces.append(
            call(
                functools.partial(student_body, sweep),
                "student_table",
                (shape((rows, span), BF16), shape((8, rows), F32), shape((d, rows), F32))
                + ((shape((d, rows), BF16),) if last else ()),
                (all_rows, unit),
                product,
                after=(sums,),
            )
        )
        if last:
            part, codes_feature = call(
                functools.partial(last_row_pass_body, chips),
                "last_row_pass",
                (shape((n_proto, 8, LANES), F32), shape((d, rows), F32)),
                (*parts, codes, unit, *[piece[1] for piece in pieces]),
                product,
            )
        else:
            part = call(
                functools.partial(row_pass_body, chips),
                "row_pass",
                shape((n_proto, 8, LANES), F32),
                (*parts, codes, own_weights),
                product,
                after=(pieces[-1][1],),
            )
        messages.append(exchange(part, "proto"))
        if not last:
            sums = call(
                col_pass_body,
                "col_pass",
                shape((8, width), F32),
                (messages[-1], codes),
                product // 2,
            )

    turned = pieces[-1][3]
    factors = (messages[0], messages[-1])
    lefts = call(
        functools.partial(left_body, chips),
        "row_factors",
        (shape((d, rows), BF16), shape((d, rows), BF16)),
        (place, *factors, turned),
        product // 8,
        specs=[SMEM] + [VMEM] * (len(factors) + 1),
    )
    heads = []
    for index, count in enumerate(PARTS):
        span = count * width
        heads.append(
            call(
                functools.partial(head_body, sum(PARTS[:index]), chips),
                "head",
                (
                    shape((share, span), F32),
                    shape((chips - 1, share, span), BF16),
                    shape((chips, share, span), BF16),
                ),
                (
                    place,
                    *lefts,
                    *parts,
                    inverse,
                    codes,
                    *[piece[0] for piece in pieces],
                    proto_weight,
                ),
                2 * product,
                specs=[SMEM] + [VMEM] * (chips + 5 + len(pieces)),
                after=(heads[-1][1],) if heads else (),
            )
        )
    feature_part = call(
        feature_body,
        "feature",
        shape((n_proto, own + 16, d), BF16),
        (*factors, codes_feature, turned, *[piece[2] for piece in pieces]),
        product // 4,
        after=(heads[-1][1],),
    )
    ends, nears = [], []
    for own_block, keep, near in heads:
        near = hop(near, 1)
        ends += [keep, near]
        nears += [own_block, near]
    pairs = call(
        pair_body,
        "pair_sums",
        tuple(shape((share, protos), BF16) for _ in range(chips - 1)),
        tuple(ends),
        product // 8,
        after=(feature_part,),
    )
    far = [hop(pairs[k - 1], 2 * k) for k in sorted(range(1, chips), key=lambda k: k % 2)]
    grad_student, tails = call(
        owner_body,
        "owner",
        (shape((own, d), F32), shape((n_patch, 8, LANES), F32)),
        (exchange(feature_part, "proto"), x_rows),
        product // 8,
    )
    own_sum, tails = call(
        own_sum_body,
        "own_sum",
        (shape((share, protos), F32), shape((n_patch, 8, LANES), F32)),
        (tails, *nears),
        product // 8,
    )
    grad_proto, loss = call(
        final_body,
        "assemble",
        (shape((share, protos), F32), shape((1, 1), F32)),
        (own_sum, exchange(tails, "patch"), *far),
        product // 4,
    )
    return (grad_student, grad_proto, loss.reshape(()))


def solution(mesh):
    both = ("patch", "proto")
    in_specs = (P(both, None), P(both, None), P(None, "proto"), P(both), P(both))
    out_specs = (P(both, None), P("patch", "proto"), P())
    return jax.shard_map(
        on_device, mesh=mesh, in_specs=in_specs, out_specs=out_specs, check_vma=False
    )
```

```python
import functools

import jax
import jax.numpy as jnp
from jax import lax
from jax.experimental import pallas as pl
from jax.experimental.pallas import tpu as pltpu
from jax.sharding import PartitionSpec as P

SK_ITERS = 3
EPS = 1e-06
TEACHER_TEMP = 0.07
STUDENT_TEMP = 0.1
F32 = jnp.float32
BF16 = jnp.bfloat16
LANES = 128
PIECES = (3, 3, 2)
FIRST = 2
PARTS = (6, 2)
VMEM_LIMIT = 20 * 1024 * 1024

NN = (((1,), (0,)), ((), ()))
NT = (((1,), (1,)), ((), ()))
TN = (((0,), (0,)), ((), ()))
SMEM = pl.BlockSpec(memory_space=pltpu.SMEM)
VMEM = pl.BlockSpec(memory_space=pltpu.VMEM)
ANY = pl.BlockSpec(memory_space=pl.ANY)
HBM = pl.BlockSpec(memory_space=pltpu.HBM)


def mm(a, b, dims=NN):
    return lax.dot_general(a, b, dims, preferred_element_type=F32)


def shape(dims, dtype):
    return jax.ShapeDtypeStruct(dims, dtype)


def call(body, name, out_shape, args, flops, specs=None, after=(), scratch=(), limit=VMEM_LIMIT):
    specs = specs or [VMEM] * len(args)
    skip = len(after)
    args = [
        pltpu.with_memory_space_constraint(arg, pltpu.HBM) if spec is HBM else arg
        for arg, spec in zip(args, specs)
    ]

    def ordered(*refs):
        body(*refs[skip:])

    def out_spec(out):
        return VMEM if isinstance(out, jax.ShapeDtypeStruct) else HBM

    many = isinstance(out_shape, tuple)
    return pl.pallas_call(
        ordered,
        name=name,
        out_shape=out_shape,
        in_specs=[ANY] * skip + specs,
        out_specs=tuple(map(out_spec, out_shape)) if many else out_spec(out_shape),
        scratch_shapes=list(scratch),
        compiler_params=pltpu.CompilerParams(vmem_limit_bytes=limit),
        cost_estimate=pl.CostEstimate(flops=flops, bytes_accessed=1 << 16, transcendentals=0),
    )(*after, *args)


def three_terms(row):
    high = row.astype(BF16).astype(F32)
    rest = row - high
    mid = rest.astype(BF16).astype(F32)
    low = rest - mid
    index = lax.broadcasted_iota(jnp.int32, (16, row.shape[1]), 0)
    terms = jnp.where(
        index == 0, high, jnp.where(index == 1, mid, jnp.where(index == 2, low, 0.0))
    )
    return terms.astype(BF16)


def column_sum(refs):
    total = refs[0][...]
    for ref in refs[1:]:
        total = total + ref[...]
    return total


def chunks(table_ref, count=8):
    width = table_ref.shape[1] // count
    return [(j, pl.ds(j * width, width)) for j in range(count)]


def arrive(copies, j, ahead):
    if j == 0:
        for copy in copies[:ahead]:
            copy.start()
    copies[j].wait()
    if j + ahead < len(copies):
        copies[j + ahead].start()


def read_rows(message_ref, start, n):
    total = jnp.sum(message_ref[...], axis=0)
    pieces = [total[start + k : start + k + 1, :] for k in range(n // LANES)]
    return jnp.concatenate(pieces, axis=1)


def write_rows(message_ref, start, row):
    count = message_ref.shape[0]
    for k in range(row.shape[1] // LANES):
        piece = row[:, k * LANES : (k + 1) * LANES]
        message_ref[:, start + k, :] = jnp.broadcast_to(piece, (count, LANES))


def rows_body(
    place_ref,
    student_hbm,
    teacher_hbm,
    index_hbm,
    weight_hbm,
    rows_ref,
    x_ref,
    w_ref,
    student_ref,
    teacher_ref,
    index_ref,
    weight_ref,
    sems,
):
    copies = [
        pltpu.make_async_copy(index_hbm, index_ref, sems.at[0]),
        pltpu.make_async_copy(teacher_hbm, teacher_ref, sems.at[1]),
        pltpu.make_async_copy(student_hbm, student_ref, sems.at[2]),
        pltpu.make_async_copy(weight_hbm, weight_ref, sems.at[3]),
    ]
    for copy in copies:
        copy.start()
    for copy in copies:
        copy.wait()
    picks = index_ref[...]
    length = student_ref.shape[0]
    count = picks.shape[1]
    one_hot = (lax.broadcasted_iota(jnp.int32, (length, count), 0) == picks).astype(BF16)
    x = mm(one_hot, student_ref[...], TN)
    y = mm(one_hot, teacher_ref[...], TN)
    x_ref[...] = x
    unit_x = x * lax.rsqrt(jnp.sum(x * x, axis=1, keepdims=True) + EPS)
    unit_y = y * lax.rsqrt(jnp.sum(y * y, axis=1, keepdims=True) + EPS)
    both = jnp.concatenate([unit_y.astype(BF16), unit_x.astype(BF16)], axis=0)
    rows_ref[...] = jnp.broadcast_to(both[None], rows_ref.shape)
    lanes = w_ref.shape[1]
    spot = lax.broadcasted_iota(jnp.int32, (count, lanes), 1) - place_ref[0] * count
    spread = (spot == lax.broadcasted_iota(jnp.int32, (count, lanes), 0)).astype(BF16)
    w_ref[...] = jnp.broadcast_to(mm(weight_ref[...], spread), w_ref.shape)


def proto_body(w_hbm, unit_hbm, first_ref, inverse_ref, w_ref, unit_ref, in_sems, out_sems):
    count = unit_ref.shape[0]
    copies = [
        pltpu.make_async_copy(w_hbm.at[:, cols], w_ref.at[:, cols], in_sems.at[j])
        for j, cols in chunks(w_ref, count)
    ]
    stores = []
    for j, cols in chunks(w_ref, count):
        arrive(copies, j, 4)
        w = w_ref[:, cols].astype(F32)
        inverse = lax.rsqrt(jnp.sum(w * w, axis=0, keepdims=True) + EPS)
        inverse_ref[pl.ds(j, 1), :] = inverse
        unit = (w * inverse).astype(BF16)
        unit_ref[j] = unit
        if j < first_ref.shape[0]:
            first_ref[j] = unit
        store = pltpu.make_async_copy(unit_ref.at[j], unit_hbm.at[j], out_sems.at[j])
        store.start()
        stores.append(store)
    for store in stores:
        store.wait()


def table_body(rows_ref, first_ref, unit_hbm, table_ref, unit_ref, sums_ref, sems):
    skip, count = first_ref.shape[0], unit_ref.shape[0]
    copies = [
        pltpu.make_async_copy(unit_hbm.at[j], unit_ref.at[j], sems.at[j]) for j in range(count)
    ]
    for copy in copies[skip:] + copies[:skip]:
        copy.start()
    half = rows_ref.shape[1] // 2
    teacher = rows_ref[:, :half, :].reshape(-1, rows_ref.shape[2])
    for j, cols in chunks(table_ref, count):
        if j < skip:
            unit = first_ref[j]
        else:
            copies[j].wait()
            unit = unit_ref[j]
        table = jnp.exp(mm(teacher, unit) * (1.0 / TEACHER_TEMP)).astype(BF16)
        table_ref[:, cols] = table
        sums_ref[pl.ds(j, 1), :] = jnp.sum(table.astype(F32), axis=0, keepdims=True)
    for copy in copies[:skip]:
        copy.wait()


def row_pass_body(parts, *refs):
    sums_refs, table_ref, extra_refs, out_ref = refs[:parts], refs[parts], refs[parts + 1 : -1], refs[-1]
    scale = 1.0 / column_sum(sums_refs)
    n = table_ref.shape[0]
    total = jnp.zeros((16, n), F32)
    for j, cols in chunks(table_ref):
        total += mm(three_terms(scale[j : j + 1, :]), table_ref[:, cols], NT)
    write_rows(out_ref, 0, jnp.sum(total, axis=0, keepdims=True))
    write_rows(out_ref, n // LANES, column_sum(extra_refs)[0:1, :])


def col_pass_body(message_ref, table_ref, out_ref):
    terms = three_terms(1.0 / read_rows(message_ref, 0, table_ref.shape[0]))
    for j, cols in chunks(table_ref):
        out_ref[pl.ds(j, 1), :] = jnp.sum(mm(terms, table_ref[:, cols]), axis=0, keepdims=True)


def student_body(first, rows_ref, unit_ref, table_ref, sums_ref, feature_ref, *turned_refs):
    count = PIECES[first]
    start = sum(PIECES[:first])
    half = rows_ref.shape[1] // 2
    student = rows_ref[:, half:, :].reshape(-1, rows_ref.shape[2])
    total = jnp.zeros((16, student.shape[0]), F32)
    for j, cols in chunks(table_ref, count):
        unit = unit_ref[start + j]
        table = jnp.exp(mm(student, unit) * (1.0 / STUDENT_TEMP)).astype(BF16)
        table_ref[:, cols] = table
        left = jnp.concatenate([unit, jnp.ones((16, unit.shape[1]), BF16)], axis=0)
        part = mm(left, table, NT)
        total += part[unit.shape[0] :]
        if j == 0:
            feature_ref[...] = part[: unit.shape[0]]
        else:
            feature_ref[...] += part[: unit.shape[0]]
    sums_ref[...] = total[0:8]
    for turned_ref in turned_refs:
        d = student.shape[1]
        eye = (
            lax.broadcasted_iota(jnp.int32, (d, d), 0)
            == lax.broadcasted_iota(jnp.int32, (d, d), 1)
        ).astype(BF16)
        turned_ref[...] = mm(eye, student, NT).astype(BF16)


def last_row_pass_body(parts, *refs):
    sums_refs, table_ref, unit_ref = refs[:parts], refs[parts], refs[parts + 1]
    *extra_refs, out_ref, feature_ref = refs[parts + 2 :]
    scale = 1.0 / column_sum(sums_refs)
    n, d = table_ref.shape[0], unit_ref.shape[1]
    total = jnp.zeros((16, n), F32)
    for j, cols in chunks(table_ref):
        factor = scale[j : j + 1, :]
        scaled = (unit_ref[j].astype(F32) * factor).astype(BF16)
        left = jnp.concatenate([scaled, three_terms(factor)], axis=0)
        part = mm(left, table_ref[:, cols], NT)
        total += part[d:]
        if j == 0:
            feature_ref[...] = part[:d]
        else:
            feature_ref[...] += part[:d]
    write_rows(out_ref, 0, jnp.sum(total, axis=0, keepdims=True))
    write_rows(out_ref, n // LANES, column_sum(extra_refs)[0:1, :])


def row_factors(first_ref, last_ref, n):
    tile = n // LANES
    return read_rows(first_ref, tile, n), read_rows(last_ref, tile, n), read_rows(last_ref, 0, n)


def targets(place_ref, chips, share):
    x, core = place_ref[1], place_ref[2]
    spots = []
    for k in range(chips):
        for side in (core, 1 - core):
            spots.append(pl.ds(pl.multiple_of((2 * (x ^ k) + side) * share, share), share))
    return spots


def left_body(chips, place_ref, first_ref, last_ref, turned_ref, probs_ref, codes_ref):
    share = turned_ref.shape[0] // (2 * chips)
    weights, exp_total, total = row_factors(first_ref, last_ref, turned_ref.shape[1])
    over_probs = weights / exp_total * (1.0 / STUDENT_TEMP)
    over_codes = weights / total * (1.0 / STUDENT_TEMP)
    for m, spot in enumerate(targets(place_ref, chips, share)):
        rows = pl.ds(m * share, share)
        turned = turned_ref[spot, :].astype(F32)
        probs_ref[rows, :] = (turned * over_probs).astype(BF16)
        codes_ref[rows, :] = (turned * over_codes).astype(BF16)


def head_body(first, parts, *refs):
    place_ref, left_probs_ref, left_codes_ref = refs[:3]
    sums_refs = refs[3 : 3 + parts]
    inverse_ref, codes_ref, *piece_refs, w_ref = refs[3 + parts : -3]
    own_ref, keep_ref, near_ref = refs[-3:]
    chips, share = near_ref.shape[:2]
    width = inverse_ref.shape[1]
    spots = targets(place_ref, chips, share)
    left_probs, left_codes = left_probs_ref[...], left_codes_ref[...]
    scale = 1.0 / column_sum(sums_refs)
    where = [(p, at) for p, size in enumerate(PIECES) for at in range(size)]
    for j, cols in chunks(own_ref, own_ref.shape[1] // width):
        row = first + j
        here = pl.ds(row * width, width)
        piece, at = where[row]
        inverse = inverse_ref[pl.ds(row, 1), :]
        head = mm(left_probs, piece_refs[piece][:, pl.ds(at * width, width)]) - scale[
            row : row + 1, :
        ] * mm(left_codes, codes_ref[:, here])
        w = jnp.concatenate([w_ref[spot, here] for spot in spots], axis=0)
        unit = w.astype(F32) * inverse
        inner = jnp.sum(unit * head, axis=0, keepdims=True)
        grad = inverse * (head - unit * inner)
        own_ref[:, cols] = grad[0:share]
        for k in range(chips):
            low = 2 * k * share
            if k:
                keep_ref[k - 1, :, cols] = grad[low : low + share].astype(BF16)
            near_ref[k, :, cols] = grad[low + share : low + 2 * share].astype(BF16)


def pair_body(*refs):
    count = len(PARTS)
    start = 0
    for part in range(count):
        keep_ref, near_ref = refs[2 * part : 2 * part + 2]
        span = keep_ref.shape[2]
        for k, pair_ref in enumerate(refs[2 * count :]):
            total = keep_ref[k].astype(F32) + near_ref[k + 1].astype(F32)
            pair_ref[:, start : start + span] = total.astype(BF16)
        start += span


def own_sum_body(tails_ref, *refs):
    count = len(PARTS)
    start = 0
    for part in range(count):
        own_ref, near_ref = refs[2 * part : 2 * part + 2]
        span = own_ref.shape[1]
        refs[-2][:, start : start + span] = own_ref[...] + near_ref[0].astype(F32)
        start += span
    refs[-1][...] = tails_ref[...]


def final_body(own_ref, tails_ref, *refs):
    *far_refs, out_ref, loss_ref = refs
    total = own_ref[...]
    for far_ref in far_refs:
        total = total + far_ref[...].astype(F32)
    out_ref[...] = total
    terms = jnp.sum(tails_ref[...], axis=0)[0:1, :]
    lane = lax.broadcasted_iota(jnp.int32, terms.shape, 1)
    part = jnp.sum(jnp.where(lane < 3, terms, 0.0), axis=1, keepdims=True)
    count = jnp.sum(jnp.where((lane >= 3) & (lane < 6), terms, 0.0), axis=1, keepdims=True)
    loss_ref[...] = part / count


def owner_body(sent_ref, x_ref, grad_ref, tail_ref):
    sent = jnp.sum(sent_ref[...].astype(F32), axis=0)
    own = x_ref.shape[0]
    x = x_ref[...]
    feature = sent[:own]
    inverse = lax.rsqrt(jnp.sum(x * x, axis=1, keepdims=True) + EPS)
    unit = x * inverse
    grad_ref[...] = inverse * (feature - unit * jnp.sum(unit * feature, axis=1, keepdims=True))
    tail_ref[...] = jnp.broadcast_to(sent[own : own + 8, :LANES][None], tail_ref.shape)


def split(value):
    row = jnp.broadcast_to(value, (8, LANES))
    high = row.astype(BF16).astype(F32)
    mid = (row - high).astype(BF16).astype(F32)
    return [term[0:1, 0:1] for term in (high, mid, row - high - mid)]


def feature_body(first_ref, last_ref, codes_ref, turned_ref, *refs):
    *probs_refs, out_ref = refs
    n = codes_ref.shape[1]
    count = out_ref.shape[0]
    own = n // count
    weights, exp_total, total = row_factors(first_ref, last_ref, n)
    codes = codes_ref[...]
    over = weights / total * (1.0 / STUDENT_TEMP)
    probs = column_sum(probs_refs) * (weights / exp_total * (1.0 / STUDENT_TEMP))
    feature = (probs - codes * over).T.astype(BF16)
    out_ref[:, :own, :] = feature.reshape(count, own, feature.shape[1])
    share = 1.0 / count
    cross = jnp.sum(turned_ref[...].astype(F32) * codes, axis=0, keepdims=True)
    part = jnp.sum(weights * jnp.log(exp_total) * share - over * cross)
    tail = (out_ref.shape[1] - own, out_ref.shape[2])
    lane = lax.broadcasted_iota(jnp.int32, tail, 1)
    row = jnp.zeros(tail, F32)
    for k, term in enumerate(split(part) + split(jnp.sum(weights) * share)):
        row = jnp.where(lane == k, term, row)
    out_ref[:, own:, :] = jnp.broadcast_to(row.astype(BF16)[None], (count,) + tail)


def on_device(student_feats, teacher_feats, proto_weight, mask_index, row_weight):
    n_patch, n_proto = lax.axis_size("patch"), lax.axis_size("proto")
    d, protos = proto_weight.shape
    length = student_feats.shape[0]
    own = mask_index.shape[0]
    rows = own * n_proto
    chips = n_patch // 2
    share = d // n_patch
    width = protos // 8
    patch, proto = lax.axis_index("patch"), lax.axis_index("proto")
    place = jnp.stack([proto, patch // 2, patch % 2]).astype(jnp.int32)
    product = 2 * rows * d * protos

    def exchange(array, axis):
        return lax.all_to_all(array, axis, 0, 0)

    def hop(array, bits):
        return lax.ppermute(array, "patch", [(i, i ^ bits) for i in range(n_patch)])

    own_rows, x_rows, own_weights = call(
        rows_body,
        "own_rows",
        (
            shape((n_proto, 2 * own, d), BF16),
            shape((own, d), F32),
            shape((8, rows), F32),
        ),
        (place, student_feats, teacher_feats, mask_index[None, :], row_weight[None, :]),
        1 << 28,
        specs=[SMEM, HBM, HBM, HBM, HBM],
        scratch=[
            pltpu.VMEM((length, d), BF16),
            pltpu.VMEM((length, d), BF16),
            pltpu.VMEM((1, own), jnp.int32),
            pltpu.VMEM((1, own), BF16),
            pltpu.SemaphoreType.DMA((4,)),
        ],
    )
    all_rows = exchange(own_rows, "proto")
    unit, unit_first, inverse = call(
        proto_body,
        "proto_unit",
        (
            pltpu.HBM((8, d, width), BF16),
            shape((FIRST, d, width), BF16),
            shape((8, width), F32),
        ),
        (proto_weight,),
        product,
        specs=[HBM],
        scratch=[
            pltpu.VMEM((d, protos), BF16),
            pltpu.VMEM((8, d, width), BF16),
            pltpu.SemaphoreType.DMA((8,)),
            pltpu.SemaphoreType.DMA((8,)),
        ],
    )
    codes, unit, sums = call(
        table_body,
        "teacher_table",
        (
            shape((rows, protos), BF16),
            shape((8, d, width), BF16),
            shape((8, width), F32),
        ),
        (all_rows, unit_first, unit),
        2 * product,
        specs=[VMEM, VMEM, HBM],
        scratch=[pltpu.SemaphoreType.DMA((8,))],
    )

    messages = []
    pieces = []
    for sweep in range(SK_ITERS):
        sums = sums + hop(sums, 1)
        parts = [sums] + [hop(sums, 2 * k) for k in range(1, chips)]
        span = PIECES[sweep] * width
        last = sweep == SK_ITERS - 1
        pieces.append(
            call(
                functools.partial(student_body, sweep),
                "student_table",
                (shape((rows, span), BF16), shape((8, rows), F32), shape((d, rows), F32))
                + ((shape((d, rows), BF16),) if last else ()),
                (all_rows, unit),
                product,
                after=(sums,),
            )
        )
        if last:
            part, codes_feature = call(
                functools.partial(last_row_pass_body, chips),
                "last_row_pass",
                (shape((n_proto, 8, LANES), F32), shape((d, rows), F32)),
                (*parts, codes, unit, *[piece[1] for piece in pieces]),
                product,
            )
        else:
            part = call(
                functools.partial(row_pass_body, chips),
                "row_pass",
                shape((n_proto, 8, LANES), F32),
                (*parts, codes, own_weights),
                product,
                after=(pieces[-1][1],),
            )
        messages.append(exchange(part, "proto"))
        if not last:
            sums = call(
                col_pass_body,
                "col_pass",
                shape((8, width), F32),
                (messages[-1], codes),
                product // 2,
            )

    turned = pieces[-1][3]
    factors = (messages[0], messages[-1])
    lefts = call(
        functools.partial(left_body, chips),
        "row_factors",
        (shape((d, rows), BF16), shape((d, rows), BF16)),
        (place, *factors, turned),
        product // 8,
        specs=[SMEM] + [VMEM] * (len(factors) + 1),
    )
    heads = []
    for index, count in enumerate(PARTS):
        span = count * width
        heads.append(
            call(
                functools.partial(head_body, sum(PARTS[:index]), chips),
                "head",
                (
                    shape((share, span), F32),
                    shape((chips - 1, share, span), BF16),
                    shape((chips, share, span), BF16),
                ),
                (
                    place,
                    *lefts,
                    *parts,
                    inverse,
                    codes,
                    *[piece[0] for piece in pieces],
                    proto_weight,
                ),
                2 * product,
                specs=[SMEM] + [VMEM] * (chips + 5 + len(pieces)),
                after=(heads[-1][1],) if heads else (),
            )
        )
    feature_part = call(
        feature_body,
        "feature",
        shape((n_proto, own + 16, d), BF16),
        (*factors, codes_feature, turned, *[piece[2] for piece in pieces]),
        product // 4,
        after=(heads[-1][1],),
    )
    ends, nears = [], []
    for own_block, keep, near in heads:
        near = hop(near, 1)
        ends += [keep, near]
        nears += [own_block, near]
    pairs = call(
        pair_body,
        "pair_sums",
        tuple(shape((share, protos), BF16) for _ in range(chips - 1)),
        tuple(ends),
        product // 8,
        after=(feature_part,),
    )
    far = [hop(pairs[k - 1], 2 * k) for k in sorted(range(1, chips), key=lambda k: k % 2)]
    grad_student, tails = call(
        owner_body,
        "owner",
        (shape((own, d), F32), shape((n_patch, 8, LANES), F32)),
        (exchange(feature_part, "proto"), x_rows),
        product // 8,
    )
    own_sum, tails = call(
        own_sum_body,
        "own_sum",
        (shape((share, protos), F32), shape((n_patch, 8, LANES), F32)),
        (tails, *nears),
        product // 8,
    )
    grad_proto, loss = call(
        final_body,
        "assemble",
        (shape((share, protos), F32), shape((1, 1), F32)),
        (own_sum, exchange(tails, "patch"), *far),
        product // 4,
    )
    return (grad_student, grad_proto, loss.reshape(()))


def solution(mesh):
    both = ("patch", "proto")
    in_specs = (P(both, None), P(both, None), P(None, "proto"), P(both), P(both))
    out_specs = (P(both, None), P("patch", "proto"), P())
    return jax.shard_map(
        on_device, mesh=mesh, in_specs=in_specs, out_specs=out_specs, check_vma=False
    )
```

```python
import functools

import jax
import jax.numpy as jnp
from jax import lax
from jax.experimental import pallas as pl
from jax.experimental.pallas import tpu as pltpu
from jax.sharding import PartitionSpec as P

SK_ITERS = 3
EPS = 1e-06
TEACHER_TEMP = 0.07
STUDENT_TEMP = 0.1
F32 = jnp.float32
BF16 = jnp.bfloat16
LANES = 128
PIECES = (3, 3, 2)
FIRST = 4
PARTS = (6, 2)
VMEM_LIMIT = 20 * 1024 * 1024

NN = (((1,), (0,)), ((), ()))
NT = (((1,), (1,)), ((), ()))
TN = (((0,), (0,)), ((), ()))
SMEM = pl.BlockSpec(memory_space=pltpu.SMEM)
VMEM = pl.BlockSpec(memory_space=pltpu.VMEM)
ANY = pl.BlockSpec(memory_space=pl.ANY)
HBM = pl.BlockSpec(memory_space=pltpu.HBM)


def mm(a, b, dims=NN):
    return lax.dot_general(a, b, dims, preferred_element_type=F32)


def shape(dims, dtype):
    return jax.ShapeDtypeStruct(dims, dtype)


def call(body, name, out_shape, args, flops, specs=None, after=(), scratch=(), limit=VMEM_LIMIT):
    specs = specs or [VMEM] * len(args)
    skip = len(after)
    args = [
        pltpu.with_memory_space_constraint(arg, pltpu.HBM) if spec is HBM else arg
        for arg, spec in zip(args, specs)
    ]

    def ordered(*refs):
        body(*refs[skip:])

    def out_spec(out):
        return VMEM if isinstance(out, jax.ShapeDtypeStruct) else HBM

    many = isinstance(out_shape, tuple)
    return pl.pallas_call(
        ordered,
        name=name,
        out_shape=out_shape,
        in_specs=[ANY] * skip + specs,
        out_specs=tuple(map(out_spec, out_shape)) if many else out_spec(out_shape),
        scratch_shapes=list(scratch),
        compiler_params=pltpu.CompilerParams(vmem_limit_bytes=limit),
        cost_estimate=pl.CostEstimate(flops=flops, bytes_accessed=1 << 16, transcendentals=0),
    )(*after, *args)


def three_terms(row):
    high = row.astype(BF16).astype(F32)
    rest = row - high
    mid = rest.astype(BF16).astype(F32)
    low = rest - mid
    index = lax.broadcasted_iota(jnp.int32, (16, row.shape[1]), 0)
    terms = jnp.where(
        index == 0, high, jnp.where(index == 1, mid, jnp.where(index == 2, low, 0.0))
    )
    return terms.astype(BF16)


def column_sum(refs):
    total = refs[0][...]
    for ref in refs[1:]:
        total = total + ref[...]
    return total


def chunks(table_ref, count=8):
    width = table_ref.shape[1] // count
    return [(j, pl.ds(j * width, width)) for j in range(count)]


def arrive(copies, j, ahead):
    if j == 0:
        for copy in copies[:ahead]:
            copy.start()
    copies[j].wait()
    if j + ahead < len(copies):
        copies[j + ahead].start()


def read_rows(message_ref, start, n):
    total = jnp.sum(message_ref[...], axis=0)
    pieces = [total[start + k : start + k + 1, :] for k in range(n // LANES)]
    return jnp.concatenate(pieces, axis=1)


def write_rows(message_ref, start, row):
    count = message_ref.shape[0]
    for k in range(row.shape[1] // LANES):
        piece = row[:, k * LANES : (k + 1) * LANES]
        message_ref[:, start + k, :] = jnp.broadcast_to(piece, (count, LANES))


def rows_body(
    place_ref,
    student_hbm,
    teacher_hbm,
    index_hbm,
    weight_hbm,
    rows_ref,
    x_ref,
    w_ref,
    student_ref,
    teacher_ref,
    index_ref,
    weight_ref,
    sems,
):
    copies = [
        pltpu.make_async_copy(index_hbm, index_ref, sems.at[0]),
        pltpu.make_async_copy(teacher_hbm, teacher_ref, sems.at[1]),
        pltpu.make_async_copy(student_hbm, student_ref, sems.at[2]),
        pltpu.make_async_copy(weight_hbm, weight_ref, sems.at[3]),
    ]
    for copy in copies:
        copy.start()
    for copy in copies:
        copy.wait()
    picks = index_ref[...]
    length = student_ref.shape[0]
    count = picks.shape[1]
    one_hot = (lax.broadcasted_iota(jnp.int32, (length, count), 0) == picks).astype(BF16)
    x = mm(one_hot, student_ref[...], TN)
    y = mm(one_hot, teacher_ref[...], TN)
    x_ref[...] = x
    unit_x = x * lax.rsqrt(jnp.sum(x * x, axis=1, keepdims=True) + EPS)
    unit_y = y * lax.rsqrt(jnp.sum(y * y, axis=1, keepdims=True) + EPS)
    both = jnp.concatenate([unit_y.astype(BF16), unit_x.astype(BF16)], axis=0)
    rows_ref[...] = jnp.broadcast_to(both[None], rows_ref.shape)
    lanes = w_ref.shape[1]
    spot = lax.broadcasted_iota(jnp.int32, (count, lanes), 1) - place_ref[0] * count
    spread = (spot == lax.broadcasted_iota(jnp.int32, (count, lanes), 0)).astype(BF16)
    w_ref[...] = jnp.broadcast_to(mm(weight_ref[...], spread), w_ref.shape)


def proto_body(w_hbm, unit_hbm, first_ref, inverse_ref, w_ref, unit_ref, in_sems, out_sems):
    count = unit_ref.shape[0]
    copies = [
        pltpu.make_async_copy(w_hbm.at[:, cols], w_ref.at[:, cols], in_sems.at[j])
        for j, cols in chunks(w_ref, count)
    ]
    stores = []
    for j, cols in chunks(w_ref, count):
        arrive(copies, j, 4)
        w = w_ref[:, cols].astype(F32)
        inverse = lax.rsqrt(jnp.sum(w * w, axis=0, keepdims=True) + EPS)
        inverse_ref[pl.ds(j, 1), :] = inverse
        unit = (w * inverse).astype(BF16)
        unit_ref[j] = unit
        if j < first_ref.shape[0]:
            first_ref[j] = unit
        store = pltpu.make_async_copy(unit_ref.at[j], unit_hbm.at[j], out_sems.at[j])
        store.start()
        stores.append(store)
    for store in stores:
        store.wait()


def table_body(rows_ref, first_ref, unit_hbm, table_ref, unit_ref, sums_ref, sems):
    skip, count = first_ref.shape[0], unit_ref.shape[0]
    copies = [
        pltpu.make_async_copy(unit_hbm.at[j], unit_ref.at[j], sems.at[j]) for j in range(count)
    ]
    for copy in copies[skip:] + copies[:skip]:
        copy.start()
    half = rows_ref.shape[1] // 2
    teacher = rows_ref[:, :half, :].reshape(-1, rows_ref.shape[2])
    for j, cols in chunks(table_ref, count):
        if j < skip:
            unit = first_ref[j]
        else:
            copies[j].wait()
            unit = unit_ref[j]
        table = jnp.exp(mm(teacher, unit) * (1.0 / TEACHER_TEMP)).astype(BF16)
        table_ref[:, cols] = table
        sums_ref[pl.ds(j, 1), :] = jnp.sum(table.astype(F32), axis=0, keepdims=True)
    for copy in copies[:skip]:
        copy.wait()


def row_pass_body(parts, *refs):
    sums_refs, table_ref, extra_refs, out_ref = refs[:parts], refs[parts], refs[parts + 1 : -1], refs[-1]
    scale = 1.0 / column_sum(sums_refs)
    n = table_ref.shape[0]
    total = jnp.zeros((16, n), F32)
    for j, cols in chunks(table_ref):
        total += mm(three_terms(scale[j : j + 1, :]), table_ref[:, cols], NT)
    write_rows(out_ref, 0, jnp.sum(total, axis=0, keepdims=True))
    write_rows(out_ref, n // LANES, column_sum(extra_refs)[0:1, :])


def col_pass_body(message_ref, table_ref, out_ref):
    terms = three_terms(1.0 / read_rows(message_ref, 0, table_ref.shape[0]))
    for j, cols in chunks(table_ref):
        out_ref[pl.ds(j, 1), :] = jnp.sum(mm(terms, table_ref[:, cols]), axis=0, keepdims=True)


def student_body(first, rows_ref, unit_ref, table_ref, sums_ref, feature_ref, *turned_refs):
    count = PIECES[first]
    start = sum(PIECES[:first])
    half = rows_ref.shape[1] // 2
    student = rows_ref[:, half:, :].reshape(-1, rows_ref.shape[2])
    total = jnp.zeros((16, student.shape[0]), F32)
    for j, cols in chunks(table_ref, count):
        unit = unit_ref[start + j]
        table = jnp.exp(mm(student, unit) * (1.0 / STUDENT_TEMP)).astype(BF16)
        table_ref[:, cols] = table
        total += mm(jnp.ones((16, table.shape[1]), BF16), table, NT)
        part = mm(unit, table, NT)
        if j == 0:
            feature_ref[...] = part
        else:
            feature_ref[...] += part
    sums_ref[...] = total[0:8]
    for turned_ref in turned_refs:
        d = student.shape[1]
        eye = (
            lax.broadcasted_iota(jnp.int32, (d, d), 0)
            == lax.broadcasted_iota(jnp.int32, (d, d), 1)
        ).astype(BF16)
        turned_ref[...] = mm(eye, student, NT).astype(BF16)


def last_row_pass_body(parts, *refs):
    sums_refs, table_ref, unit_ref = refs[:parts], refs[parts], refs[parts + 1]
    *extra_refs, out_ref, feature_ref = refs[parts + 2 :]
    scale = 1.0 / column_sum(sums_refs)
    n, d = table_ref.shape[0], unit_ref.shape[1]
    total = jnp.zeros((16, n), F32)
    for j, cols in chunks(table_ref):
        factor = scale[j : j + 1, :]
        scaled = (unit_ref[j].astype(F32) * factor).astype(BF16)
        left = jnp.concatenate([scaled, three_terms(factor)], axis=0)
        part = mm(left, table_ref[:, cols], NT)
        total += part[d:]
        if j == 0:
            feature_ref[...] = part[:d]
        else:
            feature_ref[...] += part[:d]
    write_rows(out_ref, 0, jnp.sum(total, axis=0, keepdims=True))
    write_rows(out_ref, n // LANES, column_sum(extra_refs)[0:1, :])


def row_factors(first_ref, last_ref, n):
    tile = n // LANES
    return read_rows(first_ref, tile, n), read_rows(last_ref, tile, n), read_rows(last_ref, 0, n)


def targets(place_ref, chips, share):
    x, core = place_ref[1], place_ref[2]
    spots = []
    for k in range(chips):
        for side in (core, 1 - core):
            spots.append(pl.ds(pl.multiple_of((2 * (x ^ k) + side) * share, share), share))
    return spots


def left_body(chips, place_ref, first_ref, last_ref, turned_ref, probs_ref, codes_ref):
    share = turned_ref.shape[0] // (2 * chips)
    weights, exp_total, total = row_factors(first_ref, last_ref, turned_ref.shape[1])
    over_probs = weights / exp_total * (1.0 / STUDENT_TEMP)
    over_codes = weights / total * (1.0 / STUDENT_TEMP)
    for m, spot in enumerate(targets(place_ref, chips, share)):
        rows = pl.ds(m * share, share)
        turned = turned_ref[spot, :].astype(F32)
        probs_ref[rows, :] = (turned * over_probs).astype(BF16)
        codes_ref[rows, :] = (turned * over_codes).astype(BF16)


def head_body(first, parts, *refs):
    place_ref, left_probs_ref, left_codes_ref = refs[:3]
    sums_refs = refs[3 : 3 + parts]
    inverse_ref, codes_ref, *piece_refs, w_ref = refs[3 + parts : -3]
    own_ref, keep_ref, near_ref = refs[-3:]
    chips, share = near_ref.shape[:2]
    width = inverse_ref.shape[1]
    spots = targets(place_ref, chips, share)
    left_probs, left_codes = left_probs_ref[...], left_codes_ref[...]
    scale = 1.0 / column_sum(sums_refs)
    where = [(p, at) for p, size in enumerate(PIECES) for at in range(size)]
    for j, cols in chunks(own_ref, own_ref.shape[1] // width):
        row = first + j
        here = pl.ds(row * width, width)
        piece, at = where[row]
        inverse = inverse_ref[pl.ds(row, 1), :]
        head = mm(left_probs, piece_refs[piece][:, pl.ds(at * width, width)]) - scale[
            row : row + 1, :
        ] * mm(left_codes, codes_ref[:, here])
        w = jnp.concatenate([w_ref[spot, here] for spot in spots], axis=0)
        unit = w.astype(F32) * inverse
        inner = jnp.sum(unit * head, axis=0, keepdims=True)
        grad = inverse * (head - unit * inner)
        own_ref[:, cols] = grad[0:share]
        for k in range(chips):
            low = 2 * k * share
            if k:
                keep_ref[k - 1, :, cols] = grad[low : low + share].astype(BF16)
            near_ref[k, :, cols] = grad[low + share : low + 2 * share].astype(BF16)


def pair_body(*refs):
    count = len(PARTS)
    start = 0
    for part in range(count):
        keep_ref, near_ref = refs[2 * part : 2 * part + 2]
        span = keep_ref.shape[2]
        for k, pair_ref in enumerate(refs[2 * count :]):
            total = keep_ref[k].astype(F32) + near_ref[k + 1].astype(F32)
            pair_ref[:, start : start + span] = total.astype(BF16)
        start += span


def own_sum_body(tails_ref, *refs):
    count = len(PARTS)
    start = 0
    for part in range(count):
        own_ref, near_ref = refs[2 * part : 2 * part + 2]
        span = own_ref.shape[1]
        refs[-2][:, start : start + span] = own_ref[...] + near_ref[0].astype(F32)
        start += span
    refs[-1][...] = tails_ref[...]


def final_body(own_ref, tails_ref, *refs):
    *far_refs, out_ref, loss_ref = refs
    total = own_ref[...]
    for far_ref in far_refs:
        total = total + far_ref[...].astype(F32)
    out_ref[...] = total
    terms = jnp.sum(tails_ref[...], axis=0)[0:1, :]
    lane = lax.broadcasted_iota(jnp.int32, terms.shape, 1)
    part = jnp.sum(jnp.where(lane < 3, terms, 0.0), axis=1, keepdims=True)
    count = jnp.sum(jnp.where((lane >= 3) & (lane < 6), terms, 0.0), axis=1, keepdims=True)
    loss_ref[...] = part / count


def owner_body(sent_ref, x_ref, grad_ref, tail_ref):
    sent = jnp.sum(sent_ref[...].astype(F32), axis=0)
    own = x_ref.shape[0]
    x = x_ref[...]
    feature = sent[:own]
    inverse = lax.rsqrt(jnp.sum(x * x, axis=1, keepdims=True) + EPS)
    unit = x * inverse
    grad_ref[...] = inverse * (feature - unit * jnp.sum(unit * feature, axis=1, keepdims=True))
    tail_ref[...] = jnp.broadcast_to(sent[own : own + 8, :LANES][None], tail_ref.shape)


def split(value):
    row = jnp.broadcast_to(value, (8, LANES))
    high = row.astype(BF16).astype(F32)
    mid = (row - high).astype(BF16).astype(F32)
    return [term[0:1, 0:1] for term in (high, mid, row - high - mid)]


def feature_body(first_ref, last_ref, codes_ref, turned_ref, *refs):
    *probs_refs, out_ref = refs
    n = codes_ref.shape[1]
    count = out_ref.shape[0]
    own = n // count
    weights, exp_total, total = row_factors(first_ref, last_ref, n)
    codes = codes_ref[...]
    over = weights / total * (1.0 / STUDENT_TEMP)
    probs = column_sum(probs_refs) * (weights / exp_total * (1.0 / STUDENT_TEMP))
    feature = (probs - codes * over).T.astype(BF16)
    out_ref[:, :own, :] = feature.reshape(count, own, feature.shape[1])
    share = 1.0 / count
    cross = jnp.sum(turned_ref[...].astype(F32) * codes, axis=0, keepdims=True)
    part = jnp.sum(weights * jnp.log(exp_total) * share - over * cross)
    tail = (out_ref.shape[1] - own, out_ref.shape[2])
    lane = lax.broadcasted_iota(jnp.int32, tail, 1)
    row = jnp.zeros(tail, F32)
    for k, term in enumerate(split(part) + split(jnp.sum(weights) * share)):
        row = jnp.where(lane == k, term, row)
    out_ref[:, own:, :] = jnp.broadcast_to(row.astype(BF16)[None], (count,) + tail)


def on_device(student_feats, teacher_feats, proto_weight, mask_index, row_weight):
    n_patch, n_proto = lax.axis_size("patch"), lax.axis_size("proto")
    d, protos = proto_weight.shape
    length = student_feats.shape[0]
    own = mask_index.shape[0]
    rows = own * n_proto
    chips = n_patch // 2
    share = d // n_patch
    width = protos // 8
    patch, proto = lax.axis_index("patch"), lax.axis_index("proto")
    place = jnp.stack([proto, patch // 2, patch % 2]).astype(jnp.int32)
    product = 2 * rows * d * protos

    def exchange(array, axis):
        return lax.all_to_all(array, axis, 0, 0)

    def hop(array, bits):
        return lax.ppermute(array, "patch", [(i, i ^ bits) for i in range(n_patch)])

    own_rows, x_rows, own_weights = call(
        rows_body,
        "own_rows",
        (
            shape((n_proto, 2 * own, d), BF16),
            shape((own, d), F32),
            shape((8, rows), F32),
        ),
        (place, student_feats, teacher_feats, mask_index[None, :], row_weight[None, :]),
        1 << 28,
        specs=[SMEM, HBM, HBM, HBM, HBM],
        scratch=[
            pltpu.VMEM((length, d), BF16),
            pltpu.VMEM((length, d), BF16),
            pltpu.VMEM((1, own), jnp.int32),
            pltpu.VMEM((1, own), BF16),
            pltpu.SemaphoreType.DMA((4,)),
        ],
    )
    all_rows = exchange(own_rows, "proto")
    unit, unit_first, inverse = call(
        proto_body,
        "proto_unit",
        (
            pltpu.HBM((8, d, width), BF16),
            shape((FIRST, d, width), BF16),
            shape((8, width), F32),
        ),
        (proto_weight,),
        product,
        specs=[HBM],
        scratch=[
            pltpu.VMEM((d, protos), BF16),
            pltpu.VMEM((8, d, width), BF16),
            pltpu.SemaphoreType.DMA((8,)),
            pltpu.SemaphoreType.DMA((8,)),
        ],
    )
    codes, unit, sums = call(
        table_body,
        "teacher_table",
        (
            shape((rows, protos), BF16),
            shape((8, d, width), BF16),
            shape((8, width), F32),
        ),
        (all_rows, unit_first, unit),
        2 * product,
        specs=[VMEM, VMEM, HBM],
        scratch=[pltpu.SemaphoreType.DMA((8,))],
    )

    messages = []
    pieces = []
    for sweep in range(SK_ITERS):
        sums = sums + hop(sums, 1)
        parts = [sums] + [hop(sums, 2 * k) for k in range(1, chips)]
        span = PIECES[sweep] * width
        last = sweep == SK_ITERS - 1
        pieces.append(
            call(
                functools.partial(student_body, sweep),
                "student_table",
                (shape((rows, span), BF16), shape((8, rows), F32), shape((d, rows), F32))
                + ((shape((d, rows), BF16),) if last else ()),
                (all_rows, unit),
                product,
                after=(sums,),
            )
        )
        if last:
            part, codes_feature = call(
                functools.partial(last_row_pass_body, chips),
                "last_row_pass",
                (shape((n_proto, 8, LANES), F32), shape((d, rows), F32)),
                (*parts, codes, unit, *[piece[1] for piece in pieces]),
                product,
            )
        else:
            part = call(
                functools.partial(row_pass_body, chips),
                "row_pass",
                shape((n_proto, 8, LANES), F32),
                (*parts, codes, own_weights),
                product,
                after=(pieces[-1][1],),
            )
        messages.append(exchange(part, "proto"))
        if not last:
            sums = call(
                col_pass_body,
                "col_pass",
                shape((8, width), F32),
                (messages[-1], codes),
                product // 2,
            )

    turned = pieces[-1][3]
    factors = (messages[0], messages[-1])
    lefts = call(
        functools.partial(left_body, chips),
        "row_factors",
        (shape((d, rows), BF16), shape((d, rows), BF16)),
        (place, *factors, turned),
        product // 8,
        specs=[SMEM] + [VMEM] * (len(factors) + 1),
    )
    heads = []
    for index, count in enumerate(PARTS):
        span = count * width
        heads.append(
            call(
                functools.partial(head_body, sum(PARTS[:index]), chips),
                "head",
                (
                    shape((share, span), F32),
                    shape((chips - 1, share, span), BF16),
                    shape((chips, share, span), BF16),
                ),
                (
                    place,
                    *lefts,
                    *parts,
                    inverse,
                    codes,
                    *[piece[0] for piece in pieces],
                    proto_weight,
                ),
                2 * product,
                specs=[SMEM] + [VMEM] * (chips + 5 + len(pieces)),
                after=(heads[-1][1],) if heads else (),
            )
        )
    feature_part = call(
        feature_body,
        "feature",
        shape((n_proto, own + 16, d), BF16),
        (*factors, codes_feature, turned, *[piece[2] for piece in pieces]),
        product // 4,
        after=(heads[-1][1],),
    )
    ends, nears = [], []
    for own_block, keep, near in heads:
        near = hop(near, 1)
        ends += [keep, near]
        nears += [own_block, near]
    pairs = call(
        pair_body,
        "pair_sums",
        tuple(shape((share, protos), BF16) for _ in range(chips - 1)),
        tuple(ends),
        product // 8,
        after=(feature_part,),
    )
    far = [hop(pairs[k - 1], 2 * k) for k in sorted(range(1, chips), key=lambda k: k % 2)]
    grad_student, tails = call(
        owner_body,
        "owner",
        (shape((own, d), F32), shape((n_patch, 8, LANES), F32)),
        (exchange(feature_part, "proto"), x_rows),
        product // 8,
    )
    own_sum, tails = call(
        own_sum_body,
        "own_sum",
        (shape((share, protos), F32), shape((n_patch, 8, LANES), F32)),
        (tails, *nears),
        product // 8,
    )
    grad_proto, loss = call(
        final_body,
        "assemble",
        (shape((share, protos), F32), shape((1, 1), F32)),
        (own_sum, exchange(tails, "patch"), *far),
        product // 4,
    )
    return (grad_student, grad_proto, loss.reshape(()))


def solution(mesh):
    both = ("patch", "proto")
    in_specs = (P(both, None), P(both, None), P(None, "proto"), P(both), P(both))
    out_specs = (P(both, None), P("patch", "proto"), P())
    return jax.shard_map(
        on_device, mesh=mesh, in_specs=in_specs, out_specs=out_specs, check_vma=False
    )
```
